256 devices in a mesh: row: 64 (over y, z, core), col: 4 (over x).
Axes of the slice: x: 4, y: 4, z: 8, core: 2. Of those that a mesh axis runs over, the one named last changes fastest.
Arguments:
- factor: float32 [8192, 8192], P('row', 'col'), may hold values from -0.125 to 0.125
- rhs: float32 [8192, 512], P('row', 'col'), may hold values from -6 to 6
- parent: int32 [7], replicated, may hold values from 4 to 6, as said below
- bounds: int32 [8], replicated, may hold values from 0 to 64, as said below
- slot: int32 [64], replicated, may hold values from 0 to 63, each once
- structure: int32 [7, 64], replicated, may hold values 0 or 1
Outputs:
- solution: float32 [8192, 512], P('row', 'col')
The draws below stay inside these ranges and needn't reach their ends.
Inputs may be any that keep to these rules, and one draw needn't show every extreme that they name: parent[s] is 4 or 5 for s = 0 to 3, and 6 for s = 4, 5, 6 (the root is its own entry). bounds[0] = 0, bounds[7] = 64, strictly increasing; supernode s holds logical blocks bounds[s] to bounds[s+1] - 1. `slot`: a permutation.
All inputs are finite; a program needn't handle non-finite values.
Results may differ from the reference program's by a relative error of at most 0.0001.
Values sent between devices are 32-bit elements; how exact they have to be, the bound alone decides.
A program may use at most 64 MiB of HBM per device.

```python
import jax
import jax.numpy as jnp
from jax import lax

B = 128
NRHS = 512
NODES = 7
NBLK = 64


def draw_parent(key, part):
    leaves = jax.random.randint(key, (4,), 4, 6).astype(jnp.int32)
    return jnp.concatenate([leaves, jnp.full((3,), 6, jnp.int32)])


def draw_bounds(key, part):
    least = NBLK // 8
    spare = NBLK - 7 * least
    picks = jnp.sort(jax.random.permutation(key, spare + 6)[:6].astype(jnp.int32))
    steps_in = jnp.arange(1, 7, dtype=jnp.int32)
    cuts = steps_in * least + picks - (steps_in - 1)
    return jnp.concatenate([jnp.zeros((1,), jnp.int32), cuts.astype(jnp.int32), jnp.full((1,), NBLK, jnp.int32)])


def plant(entries, own_key, low, top_value):
    shape = entries.shape
    spot = [jax.random.randint(jax.random.fold_in(own_key, axis), (), 0, shape[axis]) for axis in range(len(shape))]
    entries = entries.at[tuple(spot)].set(low)
    longest = shape.index(max(shape))
    spot[longest] = (spot[longest] + 1) % shape[longest]
    return entries.at[tuple(spot)].set(top_value)


def level_of(key, shape, shards, smallest, top_value):
    def one(dim, parts):
        draws = jax.random.uniform(jax.random.fold_in(jax.random.fold_in(key, 6), dim), (parts,), jnp.float32, smallest / len(shards), top_value / len(shards))
        return jnp.repeat(jnp.exp(draws), shape[dim] // parts).reshape((-1,) + (1,) * (len(shape) - dim - 1))

    factor_of = one(*shards[0])
    for cut in shards[1:]:
        factor_of = factor_of * one(*cut)
    return factor_of


def centred(stream_key, dims, deviation, bound, shards=(), held_as=jnp.bfloat16):
    result = deviation * jax.random.normal(stream_key, dims, jnp.float32)
    if shards:
        result = result * level_of(stream_key, dims, shards, -0.22, 0.18)
    return jnp.clip(result, -bound, bound).astype(held_as)


def setup_inputs(seed: int = 0) -> dict:
    key_list = jax.random.split(jax.random.key(seed), 7)
    factor = centred(key_list[0], (NBLK * B, NBLK * B), (B * NBLK // 4) ** -0.5, 0.125, ((0, 64), (1, 4)), jnp.float32)
    rhs = centred(key_list[1], (NBLK * B, NRHS), 1.0, 6.0, ((0, 64), (1, 4)), jnp.float32)
    parent = draw_parent(jax.random.fold_in(key_list[6], 71), 0)
    bounds = draw_bounds(jax.random.fold_in(key_list[6], 71), 0)
    slot = jax.random.permutation(key_list[4], NBLK).astype(jnp.int32)
    structure = plant((jax.random.randint(key_list[5], (NODES, NBLK), 0, 4) < 3).astype(jnp.int32), jax.random.fold_in(key_list[5], 1), 0, 1)
    return {"factor": factor, "rhs": rhs, "parent": parent, "bounds": bounds, "slot": slot, "structure": structure}


def block_masks(parent, bounds, slot, structure):
    count = slot.shape[0]
    ar = jnp.arange(count, dtype=jnp.int32)
    logical = jnp.sum(jnp.where(slot[:, None] == ar[None, :], ar[:, None], 0), axis=0).astype(jnp.int32)
    node = jnp.sum((logical[:, None] >= bounds[None, 1:7]).astype(jnp.int32), axis=1).astype(jnp.int32)
    level = (node >= 4).astype(jnp.int32) + (node >= 6).astype(jnp.int32)
    nodes = jnp.arange(7, dtype=jnp.int32)
    grand = parent[parent]
    ancestor = ((nodes[None, :] == parent[:, None]) | (nodes[None, :] == grand[:, None])) & (nodes[None, :] != nodes[:, None])
    same = node[:, None] == node[None, :]
    listed = structure[node[None, :], logical[:, None]] == 1
    link = ancestor[node[None, :], node[:, None]] & listed
    return level, same, link


def expand(matrix, mask, bsz):
    count = mask.shape[0]
    shaped = matrix.reshape(count, bsz, count, bsz) * mask[:, None, :, None].astype(jnp.float32)
    return shaped.reshape(matrix.shape)


def reference(factor, rhs, parent, bounds, slot, structure):
    count = slot.shape[0]
    bsz = factor.shape[0] // count
    level, same, link = block_masks(parent, bounds, slot, structure)
    diag_part = expand(factor, same, bsz)
    link_part = expand(factor, link, bsz)
    acc = jnp.zeros(rhs.shape, jnp.float32)
    solution = jnp.zeros(rhs.shape, jnp.float32)
    for section in range(3):
        rows = jnp.repeat(level == section, bsz)[:, None]
        solved = jnp.where(rows, jnp.dot(diag_part, rhs - acc, precision=lax.Precision.HIGHEST, preferred_element_type=jnp.float32), 0.0)
        solution = solution + solved
        if section < 2:
            acc = acc + jnp.dot(link_part, solved, precision=lax.Precision.HIGHEST, preferred_element_type=jnp.float32)
    return solution
```

```python
import functools

import jax
import jax.numpy as jnp
from jax import lax
from jax.experimental import pallas as pl
from jax.experimental.pallas import tpu as pltpu
from jax.sharding import PartitionSpec as P

B = 128
RB = 1
MESH = pl.DeviceIdType.MESH
NY, NZ, NC = 4, 8, 2


def block_masks(parent, bounds, slot, structure):
    count = slot.shape[0]
    ar = jnp.arange(count, dtype=jnp.int32)
    logical = jnp.sum(jnp.where(slot[:, None] == ar[None, :], ar[:, None], 0), axis=0)
    node = jnp.sum((logical[:, None] >= bounds[None, 1:7]).astype(jnp.int32), axis=1)
    level = (node >= 4).astype(jnp.int32) + (node >= 6).astype(jnp.int32)
    nodes = jnp.arange(7, dtype=jnp.int32)
    grand = parent[parent]
    ancestor = ((nodes[None, :] == parent[:, None]) | (nodes[None, :] == grand[:, None])) & (
        nodes[None, :] != nodes[:, None]
    )
    node_hot = (node[:, None] == nodes[None, :]).astype(jnp.float32)
    perm_hot = (logical[:, None] == ar[None, :]).astype(jnp.float32)
    listed_store = jnp.dot(
        structure.astype(jnp.float32), perm_hot.T, precision=lax.Precision.HIGHEST
    )
    anc_pairs = jnp.dot(
        node_hot,
        jnp.dot(ancestor.astype(jnp.float32), node_hot.T, precision=lax.Precision.HIGHEST),
        precision=lax.Precision.HIGHEST,
    )
    list_pairs = jnp.dot(node_hot, listed_store, precision=lax.Precision.HIGHEST)
    link = (anc_pairs * list_pairs).T > 0.5
    same = node[:, None] == node[None, :]
    return (level, same, link)


def masked(block_rows, mask):
    rblocks, width = mask.shape
    bsz = block_rows.shape[0] // rblocks
    shaped = block_rows.reshape(rblocks, bsz, width, bsz) * mask[:, None, :, None].astype(
        jnp.float32
    )
    return shaped.reshape(block_rows.shape)


def gather_kernel(x_ref, out_ref, G, local_sem, send_sem, recv_z, recv_y, recv_c):
    r = lax.axis_index("row")
    c = lax.axis_index("col")
    y = r // (NZ * NC)
    z = (r // NC) % NZ
    k = r % NC

    def dev(yy, zz, kk):
        return (((yy + NY) % NY) * NZ + (zz + NZ) % NZ) * NC + kk

    def slot(yy, zz, kk):
        return kk * (NY * NZ) + ((yy + NY) % NY) * NZ + (zz + NZ) % NZ

    zr, zl = dev(y, z + 1, k), dev(y, z - 1, k)
    yr, yl = dev(y + 1, z, k), dev(y - 1, z, k)
    partner = dev(y, z, 1 - k)

    barrier = pltpu.get_barrier_semaphore()
    for d in (zr, zl, yr, yl, partner):
        pl.semaphore_signal(barrier, inc=1, device_id=(d, c), device_id_type=MESH)
    pl.semaphore_wait(barrier, 5)

    own = slot(y, z, k)
    local = pltpu.make_async_copy(x_ref, G.at[own], local_sem.at[0])
    local.start()

    sends = []

    def remote(src, dst, si, rsem, d):
        cp = pltpu.make_async_remote_copy(
            src_ref=src, dst_ref=dst, send_sem=send_sem.at[si], recv_sem=rsem,
            device_id=(d, c), device_id_type=MESH,
        )
        return cp

    def wait_z(zsrc):
        s_ = slot(y, zsrc, k)
        remote(x_ref, G.at[s_], 0, recv_z.at[(zsrc + NZ) % NZ], zr).wait_recv()

    si = 0
    for s in range(4):
        if s >= 1:
            wait_z(z - s)
        src = x_ref if s == 0 else G.at[slot(y, z - s, k)]
        cp = remote(src, G.at[slot(y, z - s, k)], si, recv_z.at[(z - s + NZ) % NZ], zr)
        cp.start()
        sends.append(cp)
        si += 1
        if s < 3:
            if s >= 1:
                wait_z(z + s)
            src = x_ref if s == 0 else G.at[slot(y, z + s, k)]
            cp = remote(src, G.at[slot(y, z + s, k)], si, recv_z.at[(z + s) % NZ], zl)
            cp.start()
            sends.append(cp)
            si += 1
    wait_z(z - 4)
    wait_z(z + 3)
    local.wait()

    def chunk(yy, lo=0, n=NZ):
        return G.at[pl.ds(k * (NY * NZ) + ((yy + NY) % NY) * NZ + lo, n)]

    half = NZ // 2
    cp = remote(chunk(y), chunk(y), si, recv_y.at[0], yr)
    cp.start(); sends.append(cp); si += 1
    cp = remote(chunk(y), chunk(y), si, recv_y.at[1], yl)
    cp.start(); sends.append(cp); si += 1
    remote(chunk(y - 1), chunk(y - 1), 0, recv_y.at[0], yr).wait_recv()
    cp = remote(chunk(y - 1, 0, half), chunk(y - 1, 0, half), si, recv_y.at[2], yr)
    cp.start(); sends.append(cp); si += 1
    remote(chunk(y + 1), chunk(y + 1), 0, recv_y.at[1], yl).wait_recv()
    cp = remote(chunk(y + 1, half, half), chunk(y + 1, half, half), si, recv_y.at[3], yl)
    cp.start(); sends.append(cp); si += 1
    remote(chunk(y + 2, 0, half), chunk(y + 2, 0, half), 0, recv_y.at[2], yr).wait_recv()
    remote(chunk(y + 2, half, half), chunk(y + 2, half, half), 0, recv_y.at[3], yl).wait_recv()

    mine = G.at[pl.ds(k * (NY * NZ), NY * NZ)]
    theirs = G.at[pl.ds((1 - k) * (NY * NZ), NY * NZ)]
    cp = remote(mine, mine, si, recv_c.at[0], partner)
    cp.start(); sends.append(cp); si += 1
    remote(theirs, theirs, 0, recv_c.at[0], partner).wait_recv()

    for cp in sends:
        cp.wait_send()
    out_ref[...] = G[...]


def gather_rows(x, cid):
    nb, w = x.shape
    n = NY * NZ * NC
    return pl.pallas_call(
        gather_kernel,
        out_shape=jax.ShapeDtypeStruct((n, nb, w), x.dtype),
        in_specs=[pl.BlockSpec(memory_space=pltpu.VMEM)],
        out_specs=pl.BlockSpec(memory_space=pltpu.VMEM),
        scratch_shapes=[
            pltpu.VMEM((n, nb, w), x.dtype),
            pltpu.SemaphoreType.DMA((1,)),
            pltpu.SemaphoreType.DMA((16,)),
            pltpu.SemaphoreType.DMA((NZ,)),
            pltpu.SemaphoreType.DMA((4,)),
            pltpu.SemaphoreType.DMA((1,)),
        ],
        compiler_params=pltpu.CompilerParams(collective_id=cid, has_side_effects=True),
        cost_estimate=pl.CostEstimate(flops=0, transcendentals=0, bytes_accessed=2 * n * nb * w * 4),
    )(x).reshape(n * nb, w)


def to_slot_order(cols):
    rows = cols.shape[0]
    return cols.reshape(rows, NY * NZ, NC, B).transpose(0, 2, 1, 3).reshape(rows, -1)


def body(factor, rhs, parent, bounds, slot, structure):
    level, same, link = block_masks(parent, bounds, slot, structure)
    first = lax.axis_index("row") * RB
    level_mine = lax.dynamic_slice_in_dim(level, first, RB, 0)
    same_mine = lax.dynamic_slice_in_dim(same, first, RB, 0)
    link_mine = lax.dynamic_slice_in_dim(link, first, RB, 0)
    full_rows = lax.all_gather(factor, "col", axis=1, tiled=True)
    diag_part = to_slot_order(masked(full_rows, same_mine))
    link_part = to_slot_order(masked(full_rows, link_mine))

    calls = [0]

    def product(matrix, vector):
        cid = calls[0]
        calls[0] += 1
        return jnp.dot(
            matrix,
            gather_rows(vector, cid),
            precision=lax.Precision.HIGHEST,
            preferred_element_type=jnp.float32,
        )

    pieces = [rhs]
    accums = [jnp.zeros(p.shape, jnp.float32) for p in pieces]
    results = [jnp.zeros(p.shape, jnp.float32) for p in pieces]
    for section in range(3):
        rows = jnp.repeat(level_mine == section, B)[:, None]
        solved = jnp.where(rows, product(diag_part, pieces[0] - accums[0]), 0.0)
        results[0] = results[0] + solved
        if section < 2:
            accums[0] = accums[0] + product(link_part, solved)
    return results[0]


def solution(mesh):
    in_specs = (P("row", "col"), P("row", "col"), P(), P(), P(), P())
    out_specs = P("row", "col")
    return jax.shard_map(body, mesh=mesh, in_specs=in_specs, out_specs=out_specs, check_vma=False)
```

```python
import functools

import jax
import jax.numpy as jnp
from jax import lax
from jax.experimental import pallas as pl
from jax.experimental.pallas import tpu as pltpu
from jax.sharding import PartitionSpec as P

B = 128
RB = 1
MESH = pl.DeviceIdType.MESH
NY, NZ, NC = 4, 8, 2


def block_masks(parent, bounds, slot, structure):
    count = slot.shape[0]
    ar = jnp.arange(count, dtype=jnp.int32)
    logical = jnp.sum(jnp.where(slot[:, None] == ar[None, :], ar[:, None], 0), axis=0)
    node = jnp.sum((logical[:, None] >= bounds[None, 1:7]).astype(jnp.int32), axis=1)
    level = (node >= 4).astype(jnp.int32) + (node >= 6).astype(jnp.int32)
    nodes = jnp.arange(7, dtype=jnp.int32)
    grand = parent[parent]
    ancestor = ((nodes[None, :] == parent[:, None]) | (nodes[None, :] == grand[:, None])) & (
        nodes[None, :] != nodes[:, None]
    )
    node_hot = (node[:, None] == nodes[None, :]).astype(jnp.float32)
    perm_hot = (logical[:, None] == ar[None, :]).astype(jnp.float32)
    listed_store = jnp.dot(
        structure.astype(jnp.float32), perm_hot.T, precision=lax.Precision.HIGHEST
    )
    anc_pairs = jnp.dot(
        node_hot,
        jnp.dot(ancestor.astype(jnp.float32), node_hot.T, precision=lax.Precision.HIGHEST),
        precision=lax.Precision.HIGHEST,
    )
    list_pairs = jnp.dot(node_hot, listed_store, precision=lax.Precision.HIGHEST)
    link = (anc_pairs * list_pairs).T > 0.5
    same = node[:, None] == node[None, :]
    return (level, same, link)


def masked(block_rows, mask):
    rblocks, width = mask.shape
    bsz = block_rows.shape[0] // rblocks
    shaped = block_rows.reshape(rblocks, bsz, width, bsz) * mask[:, None, :, None].astype(
        jnp.float32
    )
    return shaped.reshape(block_rows.shape)


def gather_kernel(*refs, fused):
    if fused:
        x_ref, f_ref, out_ref, G, acc, local_sem, send_sem, recv_z, recv_y, recv_c = refs
    else:
        x_ref, out_ref, G, local_sem, send_sem, recv_z, recv_y, recv_c = refs
    nb = x_ref.shape[0]
    r = lax.axis_index("row")
    c = lax.axis_index("col")
    y = r // (NZ * NC)
    z = (r // NC) % NZ
    k = r % NC

    def dev(yy, zz, kk):
        return (((yy + NY) % NY) * NZ + (zz + NZ) % NZ) * NC + kk

    def slot(yy, zz, kk):
        return kk * (NY * NZ) + ((yy + NY) % NY) * NZ + (zz + NZ) % NZ

    def rows(first, n=1):
        return G.at[pl.ds(pl.multiple_of(first * nb, nb), n * nb)]

    zr, zl = dev(y, z + 1, k), dev(y, z - 1, k)
    yr, yl = dev(y + 1, z, k), dev(y - 1, z, k)
    partner = dev(y, z, 1 - k)

    barrier = pltpu.get_barrier_semaphore()
    for d in (zr, zl, yr, yl, partner):
        pl.semaphore_signal(barrier, inc=1, device_id=(d, c), device_id_type=MESH)
    pl.semaphore_wait(barrier, 5)

    own = slot(y, z, k)
    local = pltpu.make_async_copy(x_ref, rows(own), local_sem.at[0])
    local.start()
    if fused:
        acc[...] = jnp.zeros_like(acc)

    sends = []

    def remote(src, dst, si, rsem, d):
        return pltpu.make_async_remote_copy(
            src_ref=src, dst_ref=dst, send_sem=send_sem.at[si], recv_sem=rsem,
            device_id=(d, c), device_id_type=MESH,
        )

    def send(src, dst, rsem, d):
        cp = remote(src, dst, len(sends), rsem, d)
        cp.start()
        sends.append(cp)

    def wait_z(zsrc):
        remote(x_ref, rows(slot(y, zsrc, k)), 0, recv_z.at[(zsrc + NZ) % NZ], zr).wait_recv()

    def chunk_start(kk, yy):
        return kk * (NY * NZ) + ((yy + NY) % NY) * NZ

    def chunk(kk, yy, lo=0, n=NZ):
        return rows(chunk_start(kk, yy) + lo, n)

    def multiply(kk, yy):
        if fused:
            s0 = chunk_start(kk, yy)
            cols = pl.ds(pl.multiple_of(s0 * nb, nb), NZ * nb)
            acc[...] += jnp.dot(
                f_ref[:, cols], G[cols, :],
                precision=lax.Precision.HIGHEST, preferred_element_type=jnp.float32,
            )

    for s in range(4):
        if s >= 1:
            wait_z(z - s)
        src = x_ref if s == 0 else rows(slot(y, z - s, k))
        send(src, rows(slot(y, z - s, k)), recv_z.at[(z - s + NZ) % NZ], zr)
        if s < 3:
            if s >= 1:
                wait_z(z + s)
            src = x_ref if s == 0 else rows(slot(y, z + s, k))
            send(src, rows(slot(y, z + s, k)), recv_z.at[(z + s) % NZ], zl)
    wait_z(z - 4)
    wait_z(z + 3)
    local.wait()

    half = NZ // 2
    send(chunk(k, y), chunk(k, y), recv_y.at[0], yr)
    send(chunk(k, y), chunk(k, y), recv_y.at[1], yl)
    send(chunk(k, y), chunk(k, y), recv_c.at[0], partner)
    multiply(k, y)
    remote(chunk(k, y - 1), chunk(k, y - 1), 0, recv_y.at[0], yr).wait_recv()
    send(chunk(k, y - 1, 0, half), chunk(k, y - 1, 0, half), recv_y.at[2], yr)
    send(chunk(k, y - 1), chunk(k, y - 1), recv_c.at[3], partner)
    remote(chunk(k, y + 1), chunk(k, y + 1), 0, recv_y.at[1], yl).wait_recv()
    send(chunk(k, y + 1, half, half), chunk(k, y + 1, half, half), recv_y.at[3], yl)
    send(chunk(k, y + 1), chunk(k, y + 1), recv_c.at[1], partner)
    multiply(k, y - 1)
    multiply(k, y + 1)
    remote(chunk(k, y + 2, 0, half), chunk(k, y + 2, 0, half), 0, recv_y.at[2], yr).wait_recv()
    remote(chunk(k, y + 2, half, half), chunk(k, y + 2, half, half), 0, recv_y.at[3], yl).wait_recv()
    send(chunk(k, y + 2), chunk(k, y + 2), recv_c.at[2], partner)
    multiply(k, y + 2)

    for d in (0, 3, 1, 2):
        remote(chunk(1 - k, y + d), chunk(1 - k, y + d), 0, recv_c.at[d], partner).wait_recv()
        multiply(1 - k, y + d)

    for cp in sends:
        cp.wait_send()
    if fused:
        out_ref[...] = acc[...]
    else:
        out_ref[...] = G[...]


def _sems():
    return [
        pltpu.SemaphoreType.DMA((1,)),
        pltpu.SemaphoreType.DMA((16,)),
        pltpu.SemaphoreType.DMA((NZ,)),
        pltpu.SemaphoreType.DMA((4,)),
        pltpu.SemaphoreType.DMA((4,)),
    ]


def gather_rows(x, cid):
    nb, w = x.shape
    n = NY * NZ * NC
    return pl.pallas_call(
        functools.partial(gather_kernel, fused=False),
        out_shape=jax.ShapeDtypeStruct((n * nb, w), x.dtype),
        in_specs=[pl.BlockSpec(memory_space=pltpu.VMEM)],
        out_specs=pl.BlockSpec(memory_space=pltpu.VMEM),
        scratch_shapes=[pltpu.VMEM((n * nb, w), x.dtype)] + _sems(),
        compiler_params=pltpu.CompilerParams(collective_id=cid, has_side_effects=True),
        cost_estimate=pl.CostEstimate(flops=0, transcendentals=0, bytes_accessed=2 * n * nb * w * 4),
    )(x)


def gather_product(matrix, x, cid):
    nb, w = x.shape
    n = NY * NZ * NC
    return pl.pallas_call(
        functools.partial(gather_kernel, fused=True),
        out_shape=jax.ShapeDtypeStruct((matrix.shape[0], w), jnp.float32),
        in_specs=[pl.BlockSpec(memory_space=pltpu.VMEM)] * 2,
        out_specs=pl.BlockSpec(memory_space=pltpu.VMEM),
        scratch_shapes=[pltpu.VMEM((n * nb, w), x.dtype), pltpu.VMEM((matrix.shape[0], w), jnp.float32)]
        + _sems(),
        compiler_params=pltpu.CompilerParams(collective_id=cid, has_side_effects=True),
        cost_estimate=pl.CostEstimate(
            flops=2 * matrix.shape[0] * matrix.shape[1] * w, transcendentals=0,
            bytes_accessed=(matrix.size + 2 * n * nb * w) * 4,
        ),
    )(x, matrix)


def to_slot_order(cols):
    rows = cols.shape[0]
    return cols.reshape(rows, NY * NZ, NC, B).transpose(0, 2, 1, 3).reshape(rows, -1)


def body(factor, rhs, parent, bounds, slot, structure):
    level, same, link = block_masks(parent, bounds, slot, structure)
    first = lax.axis_index("row") * RB
    level_mine = lax.dynamic_slice_in_dim(level, first, RB, 0)
    same_mine = lax.dynamic_slice_in_dim(same, first, RB, 0)
    link_mine = lax.dynamic_slice_in_dim(link, first, RB, 0)
    full_rows = lax.all_gather(factor, "col", axis=1, tiled=True)
    diag_part = to_slot_order(masked(full_rows, same_mine))
    link_part = to_slot_order(masked(full_rows, link_mine))

    calls = [0]

    def product(matrix, vector):
        cid = calls[0]
        calls[0] += 1
        if cid == 0:
            return jnp.dot(
                matrix,
                gather_rows(vector, cid),
                precision=lax.Precision.HIGHEST,
                preferred_element_type=jnp.float32,
            )
        return gather_product(matrix, vector, cid)

    pieces = [rhs]
    accums = [jnp.zeros(p.shape, jnp.float32) for p in pieces]
    results = [jnp.zeros(p.shape, jnp.float32) for p in pieces]
    for section in range(3):
        rows = jnp.repeat(level_mine == section, B)[:, None]
        solved = jnp.where(rows, product(diag_part, pieces[0] - accums[0]), 0.0)
        results[0] = results[0] + solved
        if section < 2:
            accums[0] = accums[0] + product(link_part, solved)
    return results[0]


def solution(mesh):
    in_specs = (P("row", "col"), P("row", "col"), P(), P(), P(), P())
    out_specs = P("row", "col")
    return jax.shard_map(body, mesh=mesh, in_specs=in_specs, out_specs=out_specs, check_vma=False)
```

```python
import functools

import jax
import jax.numpy as jnp
from jax import lax
from jax.experimental import pallas as pl
from jax.experimental.pallas import tpu as pltpu
from jax.sharding import PartitionSpec as P

B = 128
RB = 1
MESH = pl.DeviceIdType.MESH
NY, NZ, NC = 4, 8, 2


def block_masks(parent, bounds, slot, structure):
    count = slot.shape[0]
    ar = jnp.arange(count, dtype=jnp.int32)
    logical = jnp.sum(jnp.where(slot[:, None] == ar[None, :], ar[:, None], 0), axis=0)
    node = jnp.sum((logical[:, None] >= bounds[None, 1:7]).astype(jnp.int32), axis=1)
    level = (node >= 4).astype(jnp.int32) + (node >= 6).astype(jnp.int32)
    nodes = jnp.arange(7, dtype=jnp.int32)
    grand = parent[parent]
    ancestor = ((nodes[None, :] == parent[:, None]) | (nodes[None, :] == grand[:, None])) & (
        nodes[None, :] != nodes[:, None]
    )
    node_hot = (node[:, None] == nodes[None, :]).astype(jnp.float32)
    perm_hot = (logical[:, None] == ar[None, :]).astype(jnp.float32)
    listed_store = jnp.dot(
        structure.astype(jnp.float32), perm_hot.T, precision=lax.Precision.HIGHEST
    )
    anc_pairs = jnp.dot(
        node_hot,
        jnp.dot(ancestor.astype(jnp.float32), node_hot.T, precision=lax.Precision.HIGHEST),
        precision=lax.Precision.HIGHEST,
    )
    list_pairs = jnp.dot(node_hot, listed_store, precision=lax.Precision.HIGHEST)
    link = (anc_pairs * list_pairs).T > 0.5
    same = node[:, None] == node[None, :]
    return (level, same, link)


def masked(block_rows, mask):
    rblocks, width = mask.shape
    bsz = block_rows.shape[0] // rblocks
    shaped = block_rows.reshape(rblocks, bsz, width, bsz) * mask[:, None, :, None].astype(
        jnp.float32
    )
    return shaped.reshape(block_rows.shape)


def gather_kernel(*refs, fused):
    if fused:
        x_ref, f_ref, out_ref, G, acc, local_sem, send_sem, recv1, recv2, recv_c = refs
    else:
        x_ref, out_ref, G, local_sem, send_sem, recv1, recv2, recv_c = refs
    nb = x_ref.shape[0]
    r = lax.axis_index("row")
    c = lax.axis_index("col")
    y = r // (NZ * NC)
    z = (r // NC) % NZ
    k = r % NC
    coord = {"y": y, "z": z}
    size = {"y": NY, "z": NZ}
    half_class = NY * NZ

    def dev_at(ax, delta, kk):
        yy = y + delta if ax == "y" else y
        zz = z + delta if ax == "z" else z
        return (((yy + NY) % NY) * NZ + (zz + NZ) % NZ) * NC + kk

    def rows(first, cnt):
        return G.at[pl.ds(pl.multiple_of(first * nb, nb), cnt * nb)]

    barrier = pltpu.get_barrier_semaphore()
    for ax in ("z", "y"):
        for delta in (1, -1):
            pl.semaphore_signal(barrier, inc=1, device_id=(dev_at(ax, delta, k), c), device_id_type=MESH)
    pl.semaphore_signal(barrier, inc=1, device_id=(dev_at("y", 0, 1 - k), c), device_id_type=MESH)
    pl.semaphore_wait(barrier, 5)

    if fused:
        acc[...] = jnp.zeros_like(acc)

    def multiply(first, cnt):
        if fused:
            cols = pl.ds(pl.multiple_of(first * nb, nb), cnt * nb)
            acc[...] += jnp.dot(
                f_ref[:, cols], G[cols, :],
                precision=lax.Precision.HIGHEST, preferred_element_type=jnp.float32,
            )

    def run(kk):
        ax_a, ax_b = ("z", "y") if kk == 0 else ("y", "z")
        na, nbr = size[ax_a], size[ax_b]
        a, b = coord[ax_a], coord[ax_b]
        partner = dev_at("y", 0, 1 - kk)
        sends = []

        def slot(ai, bi):
            return kk * half_class + ((bi + nbr) % nbr) * na + (ai + na) % na

        def remote(src, dst, rsem, d, si=0):
            return pltpu.make_async_remote_copy(
                src_ref=src, dst_ref=dst, send_sem=send_sem.at[si], recv_sem=rsem,
                device_id=(d, c), device_id_type=MESH,
            )

        def send(src, dst, rsem, d):
            cp = remote(src, dst, rsem, d, len(sends))
            cp.start()
            sends.append(cp)

        def wait(ref, rsem):
            remote(ref, ref, rsem, partner).wait_recv()

        local = pltpu.make_async_copy(x_ref, rows(slot(a, b), 1), local_sem.at[0])
        local.start()

        def p1(ai):
            return rows(slot(ai, b), 1)

        right, left = dev_at(ax_a, 1, kk), dev_at(ax_a, -1, kk)
        nr, nl = na // 2, na // 2 - 1
        for s in range(nr):
            if s >= 1:
                wait(p1(a - s), recv1.at[0, s - 1])
            send(x_ref if s == 0 else p1(a - s), p1(a - s), recv1.at[0, s], right)
            if s < nl:
                if s >= 1:
                    wait(p1(a + s), recv1.at[1, s - 1])
                send(x_ref if s == 0 else p1(a + s), p1(a + s), recv1.at[1, s], left)
        wait(p1(a - nr), recv1.at[0, nr - 1])
        if nl >= 1:
            wait(p1(a + nl), recv1.at[1, nl - 1])
        local.wait()

        def p2(bi, lo=0, cnt=na):
            return rows(slot(0, bi) + lo, cnt)

        def complete(off):
            send(p2(b + off), p2(b + off), recv_c.at[kk, off % nbr], partner)
            multiply(slot(0, b + off), na)

        right, left = dev_at(ax_b, 1, kk), dev_at(ax_b, -1, kk)
        nh, half = nbr // 2, na // 2
        for s in range(nh):
            last = s == nh - 1
            if s >= 1:
                wait(p2(b - s), recv2.at[0, s - 1])
            if last:
                send(p2(b - s, 0, half), p2(b - s, 0, half), recv2.at[0, s], right)
            else:
                send(p2(b - s), p2(b - s), recv2.at[0, s], right)
            if s >= 1:
                wait(p2(b + s), recv2.at[1, s - 1])
            if last:
                send(p2(b + s, half, half), p2(b + s, half, half), recv2.at[1, s], left)
            else:
                send(p2(b + s), p2(b + s), recv2.at[1, s], left)
            if s == 0:
                complete(0)
            else:
                complete(-s)
                complete(s)
        wait(p2(b - nh, 0, half), recv2.at[0, nh - 1])
        wait(p2(b + nh, half, half), recv2.at[1, nh - 1])
        complete(nh)

        order = [0]
        for d in range(1, na // 2 + 1):
            order.append(d)
            if d != na - d:
                order.append(na - d)
        for d in order:
            first = (1 - kk) * half_class + ((a + d) % na) * nbr
            wait(rows(first, nbr), recv_c.at[1 - kk, d])
            multiply(first, nbr)

        for cp in sends:
            cp.wait_send()

    @pl.when(k == 0)
    def _():
        run(0)

    @pl.when(k == 1)
    def _():
        run(1)

    if fused:
        out_ref[...] = acc[...]
    else:
        out_ref[...] = G[...]


def _sems():
    return [
        pltpu.SemaphoreType.DMA((1,)),
        pltpu.SemaphoreType.DMA((24,)),
        pltpu.SemaphoreType.DMA((2, 4)),
        pltpu.SemaphoreType.DMA((2, 4)),
        pltpu.SemaphoreType.DMA((2, 8)),
    ]


def gather_rows(x, cid):
    nb, w = x.shape
    n = NY * NZ * NC
    return pl.pallas_call(
        functools.partial(gather_kernel, fused=False),
        out_shape=jax.ShapeDtypeStruct((n * nb, w), x.dtype),
        in_specs=[pl.BlockSpec(memory_space=pltpu.VMEM)],
        out_specs=pl.BlockSpec(memory_space=pltpu.VMEM),
        scratch_shapes=[pltpu.VMEM((n * nb, w), x.dtype)] + _sems(),
        compiler_params=pltpu.CompilerParams(collective_id=cid, has_side_effects=True),
        cost_estimate=pl.CostEstimate(flops=0, transcendentals=0, bytes_accessed=2 * n * nb * w * 4),
    )(x)


def gather_product(matrix, x, cid):
    nb, w = x.shape
    n = NY * NZ * NC
    return pl.pallas_call(
        functools.partial(gather_kernel, fused=True),
        out_shape=jax.ShapeDtypeStruct((matrix.shape[0], w), jnp.float32),
        in_specs=[pl.BlockSpec(memory_space=pltpu.VMEM)] * 2,
        out_specs=pl.BlockSpec(memory_space=pltpu.VMEM),
        scratch_shapes=[pltpu.VMEM((n * nb, w), x.dtype), pltpu.VMEM((matrix.shape[0], w), jnp.float32)]
        + _sems(),
        compiler_params=pltpu.CompilerParams(collective_id=cid, has_side_effects=True),
        cost_estimate=pl.CostEstimate(
            flops=2 * matrix.shape[0] * matrix.shape[1] * w, transcendentals=0,
            bytes_accessed=(matrix.size + 2 * n * nb * w) * 4,
        ),
    )(x, matrix)


def to_slot_order(cols):
    rows = cols.shape[0]
    shaped = cols.reshape(rows, NY, NZ, NC, B)
    first = shaped[:, :, :, 0, :].reshape(rows, -1)
    second = shaped[:, :, :, 1, :].transpose(0, 2, 1, 3).reshape(rows, -1)
    return jnp.concatenate([first, second], axis=1)


def body(factor, rhs, parent, bounds, slot, structure):
    level, same, link = block_masks(parent, bounds, slot, structure)
    first = lax.axis_index("row") * RB
    level_mine = lax.dynamic_slice_in_dim(level, first, RB, 0)
    same_mine = lax.dynamic_slice_in_dim(same, first, RB, 0)
    link_mine = lax.dynamic_slice_in_dim(link, first, RB, 0)
    full_rows = lax.all_gather(factor, "col", axis=1, tiled=True)
    diag_part = to_slot_order(masked(full_rows, same_mine))
    link_part = to_slot_order(masked(full_rows, link_mine))

    calls = [0]

    def product(matrix, vector):
        cid = calls[0]
        calls[0] += 1
        if cid == 0:
            return jnp.dot(
                matrix,
                gather_rows(vector, cid),
                precision=lax.Precision.HIGHEST,
                preferred_element_type=jnp.float32,
            )
        return gather_product(matrix, vector, cid)

    pieces = [rhs]
    accums = [jnp.zeros(p.shape, jnp.float32) for p in pieces]
    results = [jnp.zeros(p.shape, jnp.float32) for p in pieces]
    for section in range(3):
        rows = jnp.repeat(level_mine == section, B)[:, None]
        solved = jnp.where(rows, product(diag_part, pieces[0] - accums[0]), 0.0)
        results[0] = results[0] + solved
        if section < 2:
            accums[0] = accums[0] + product(link_part, solved)
    return results[0]


def solution(mesh):
    in_specs = (P("row", "col"), P("row", "col"), P(), P(), P(), P())
    out_specs = P("row", "col")
    return jax.shard_map(body, mesh=mesh, in_specs=in_specs, out_specs=out_specs, check_vma=False)
```

```python
import functools

import jax
import jax.numpy as jnp
from jax import lax
from jax.experimental import pallas as pl
from jax.experimental.pallas import tpu as pltpu
from jax.sharding import PartitionSpec as P

B = 128
RB = 1
MESH = pl.DeviceIdType.MESH
NY, NZ, NC = 4, 8, 2


def block_masks(parent, bounds, slot, structure):
    count = slot.shape[0]
    ar = jnp.arange(count, dtype=jnp.int32)
    logical = jnp.sum(jnp.where(slot[:, None] == ar[None, :], ar[:, None], 0), axis=0)
    node = jnp.sum((logical[:, None] >= bounds[None, 1:7]).astype(jnp.int32), axis=1)
    level = (node >= 4).astype(jnp.int32) + (node >= 6).astype(jnp.int32)
    nodes = jnp.arange(7, dtype=jnp.int32)
    grand = parent[parent]
    ancestor = ((nodes[None, :] == parent[:, None]) | (nodes[None, :] == grand[:, None])) & (
        nodes[None, :] != nodes[:, None]
    )
    node_hot = (node[:, None] == nodes[None, :]).astype(jnp.float32)
    perm_hot = (logical[:, None] == ar[None, :]).astype(jnp.float32)
    listed_store = jnp.dot(
        structure.astype(jnp.float32), perm_hot.T, precision=lax.Precision.HIGHEST
    )
    anc_pairs = jnp.dot(
        node_hot,
        jnp.dot(ancestor.astype(jnp.float32), node_hot.T, precision=lax.Precision.HIGHEST),
        precision=lax.Precision.HIGHEST,
    )
    list_pairs = jnp.dot(node_hot, listed_store, precision=lax.Precision.HIGHEST)
    link = (anc_pairs * list_pairs).T > 0.5
    same = node[:, None] == node[None, :]
    return (level, same, link)


def masked(block_rows, mask):
    rblocks, width = mask.shape
    bsz = block_rows.shape[0] // rblocks
    shaped = block_rows.reshape(rblocks, bsz, width, bsz) * mask[:, None, :, None].astype(
        jnp.float32
    )
    return shaped.reshape(block_rows.shape)


def gather_kernel(*refs, fused):
    if fused:
        x_ref, f_ref, out_ref, G, acc, local_sem, send_sem, recv_z, recv_y, recv_c = refs
    else:
        x_ref, out_ref, G, local_sem, send_sem, recv_z, recv_y, recv_c = refs
    nb, w = x_ref.shape
    r = lax.axis_index("row")
    c = lax.axis_index("col")
    y = r // (NZ * NC)
    z = (r // NC) % NZ
    k = r % NC

    def dev(yy, zz, kk):
        return (((yy + NY) % NY) * NZ + (zz + NZ) % NZ) * NC + kk

    def blk(yy, zz, kk):
        return G.at[((yy + NY) % NY) * NZ + (zz + NZ) % NZ, kk]

    def chunk(kk, yy, lo=0, n=NZ):
        return G.at[pl.ds(((yy + NY) % NY) * NZ + lo, n), kk]

    zr, zl = dev(y, z + 1, k), dev(y, z - 1, k)
    yr, yl = dev(y + 1, z, k), dev(y - 1, z, k)
    partner = dev(y, z, 1 - k)

    barrier = pltpu.get_barrier_semaphore()
    for d in (zr, zl, yr, yl, partner):
        pl.semaphore_signal(barrier, inc=1, device_id=(d, c), device_id_type=MESH)
    pl.semaphore_wait(barrier, 5)

    local = pltpu.make_async_copy(x_ref, blk(y, z, k), local_sem.at[0])
    local.start()
    if fused:
        acc[...] = jnp.zeros_like(acc)

    sends = []

    def remote(src, dst, rsem, d, si=0):
        return pltpu.make_async_remote_copy(
            src_ref=src, dst_ref=dst, send_sem=send_sem.at[si], recv_sem=rsem,
            device_id=(d, c), device_id_type=MESH,
        )

    def send(src, dst, rsem, d):
        cp = remote(src, dst, rsem, d, len(sends))
        cp.start()
        sends.append(cp)

    def wait(ref, rsem):
        remote(ref, ref, rsem, partner).wait_recv()

    def multiply(yy):
        if fused:
            plane = (yy + NY) % NY
            cols = pl.ds(pl.multiple_of(plane * (NZ * NC * nb), nb), NZ * NC * nb)
            vec = G[pl.ds(plane * NZ, NZ)].reshape(NZ * NC * nb, w)
            acc[...] += jnp.dot(
                f_ref[:, cols], vec,
                precision=lax.Precision.HIGHEST, preferred_element_type=jnp.float32,
            )

    for s in range(4):
        if s >= 1:
            wait(blk(y, z - s, k), recv_z.at[(z - s + NZ) % NZ])
        send(x_ref if s == 0 else blk(y, z - s, k), blk(y, z - s, k), recv_z.at[(z - s + NZ) % NZ], zr)
        if s < 3:
            if s >= 1:
                wait(blk(y, z + s, k), recv_z.at[(z + s) % NZ])
            send(x_ref if s == 0 else blk(y, z + s, k), blk(y, z + s, k), recv_z.at[(z + s) % NZ], zl)
    wait(blk(y, z - 4, k), recv_z.at[(z - 4 + NZ) % NZ])
    wait(blk(y, z + 3, k), recv_z.at[(z + 3) % NZ])
    local.wait()

    half = NZ // 2
    send(chunk(k, y), chunk(k, y), recv_y.at[0], yr)
    send(chunk(k, y), chunk(k, y), recv_y.at[1], yl)
    send(chunk(k, y), chunk(k, y), recv_c.at[0], partner)
    wait(chunk(k, y - 1), recv_y.at[0])
    send(chunk(k, y - 1, 0, half), chunk(k, y - 1, 0, half), recv_y.at[2], yr)
    send(chunk(k, y - 1), chunk(k, y - 1), recv_c.at[3], partner)
    wait(chunk(k, y + 1), recv_y.at[1])
    send(chunk(k, y + 1, half, half), chunk(k, y + 1, half, half), recv_y.at[3], yl)
    send(chunk(k, y + 1), chunk(k, y + 1), recv_c.at[1], partner)
    wait(chunk(1 - k, y), recv_c.at[0])
    multiply(y)
    wait(chunk(k, y + 2, 0, half), recv_y.at[2])
    wait(chunk(k, y + 2, half, half), recv_y.at[3])
    send(chunk(k, y + 2), chunk(k, y + 2), recv_c.at[2], partner)

    for d in (3, 1, 2):
        wait(chunk(1 - k, y + d), recv_c.at[d])
        multiply(y + d)

    for cp in sends:
        cp.wait_send()
    if fused:
        out_ref[...] = acc[...]
    else:
        out_ref[...] = G[...]


def _sems():
    return [
        pltpu.SemaphoreType.DMA((1,)),
        pltpu.SemaphoreType.DMA((16,)),
        pltpu.SemaphoreType.DMA((NZ,)),
        pltpu.SemaphoreType.DMA((4,)),
        pltpu.SemaphoreType.DMA((4,)),
    ]


def gather_rows(x, cid):
    nb, w = x.shape
    shape = (NY * NZ, NC, nb, w)
    return pl.pallas_call(
        functools.partial(gather_kernel, fused=False),
        out_shape=jax.ShapeDtypeStruct(shape, x.dtype),
        in_specs=[pl.BlockSpec(memory_space=pltpu.VMEM)],
        out_specs=pl.BlockSpec(memory_space=pltpu.VMEM),
        scratch_shapes=[pltpu.VMEM(shape, x.dtype)] + _sems(),
        compiler_params=pltpu.CompilerParams(collective_id=cid, has_side_effects=True),
        cost_estimate=pl.CostEstimate(flops=0, transcendentals=0, bytes_accessed=2 * x.size * 64 * 4),
    )(x).reshape(-1, w)


def gather_product(matrix, x, cid):
    nb, w = x.shape
    shape = (NY * NZ, NC, nb, w)
    return pl.pallas_call(
        functools.partial(gather_kernel, fused=True),
        out_shape=jax.ShapeDtypeStruct((matrix.shape[0], w), jnp.float32),
        in_specs=[pl.BlockSpec(memory_space=pltpu.VMEM)] * 2,
        out_specs=pl.BlockSpec(memory_space=pltpu.VMEM),
        scratch_shapes=[pltpu.VMEM(shape, x.dtype), pltpu.VMEM((matrix.shape[0], w), jnp.float32)]
        + _sems(),
        compiler_params=pltpu.CompilerParams(collective_id=cid, has_side_effects=True),
        cost_estimate=pl.CostEstimate(
            flops=2 * matrix.shape[0] * matrix.shape[1] * w, transcendentals=0,
            bytes_accessed=(matrix.size + 2 * x.size * 64) * 4,
        ),
    )(x, matrix)


def body(factor, rhs, parent, bounds, slot, structure):
    level, same, link = block_masks(parent, bounds, slot, structure)
    first = lax.axis_index("row") * RB
    level_mine = lax.dynamic_slice_in_dim(level, first, RB, 0)
    same_mine = lax.dynamic_slice_in_dim(same, first, RB, 0)
    link_mine = lax.dynamic_slice_in_dim(link, first, RB, 0)
    full_rows = lax.all_gather(factor, "col", axis=1, tiled=True)
    diag_part = masked(full_rows, same_mine)
    link_part = masked(full_rows, link_mine)

    calls = [0]

    def product(matrix, vector):
        cid = calls[0]
        calls[0] += 1
        if cid == 0:
            return jnp.dot(
                matrix,
                gather_rows(vector, cid),
                precision=lax.Precision.HIGHEST,
                preferred_element_type=jnp.float32,
            )
        return gather_product(matrix, vector, cid)

    pieces = [rhs]
    accums = [jnp.zeros(p.shape, jnp.float32) for p in pieces]
    results = [jnp.zeros(p.shape, jnp.float32) for p in pieces]
    for section in range(3):
        rows = jnp.repeat(level_mine == section, B)[:, None]
        solved = jnp.where(rows, product(diag_part, pieces[0] - accums[0]), 0.0)
        results[0] = results[0] + solved
        if section < 2:
            accums[0] = accums[0] + product(link_part, solved)
    return results[0]


def solution(mesh):
    in_specs = (P("row", "col"), P("row", "col"), P(), P(), P(), P())
    out_specs = P("row", "col")
    return jax.shard_map(body, mesh=mesh, in_specs=in_specs, out_specs=out_specs, check_vma=False)
```

```python
import functools

import jax
import jax.numpy as jnp
from jax import lax
from jax.experimental import pallas as pl
from jax.experimental.pallas import tpu as pltpu
from jax.sharding import PartitionSpec as P

B = 128
RB = 1
MESH = pl.DeviceIdType.MESH
NY, NZ, NC = 4, 8, 2


def block_masks(parent, bounds, slot, structure):
    count = slot.shape[0]
    ar = jnp.arange(count, dtype=jnp.int32)
    logical = jnp.sum(jnp.where(slot[:, None] == ar[None, :], ar[:, None], 0), axis=0)
    node = jnp.sum((logical[:, None] >= bounds[None, 1:7]).astype(jnp.int32), axis=1)
    level = (node >= 4).astype(jnp.int32) + (node >= 6).astype(jnp.int32)
    nodes = jnp.arange(7, dtype=jnp.int32)
    grand = parent[parent]
    ancestor = ((nodes[None, :] == parent[:, None]) | (nodes[None, :] == grand[:, None])) & (
        nodes[None, :] != nodes[:, None]
    )
    node_hot = (node[:, None] == nodes[None, :]).astype(jnp.float32)
    perm_hot = (logical[:, None] == ar[None, :]).astype(jnp.float32)
    listed_store = jnp.dot(
        structure.astype(jnp.float32), perm_hot.T, precision=lax.Precision.HIGHEST
    )
    anc_pairs = jnp.dot(
        node_hot,
        jnp.dot(ancestor.astype(jnp.float32), node_hot.T, precision=lax.Precision.HIGHEST),
        precision=lax.Precision.HIGHEST,
    )
    list_pairs = jnp.dot(node_hot, listed_store, precision=lax.Precision.HIGHEST)
    link = (anc_pairs * list_pairs).T > 0.5
    same = node[:, None] == node[None, :]
    return (level, same, link)


def masked(block_rows, mask):
    rblocks, width = mask.shape
    bsz = block_rows.shape[0] // rblocks
    shaped = block_rows.reshape(rblocks, bsz, width, bsz) * mask[:, None, :, None].astype(
        jnp.float32
    )
    return shaped.reshape(block_rows.shape)


def gather_kernel(*refs, fused):
    if fused:
        x_ref, f_ref, out_ref, G, acc, local_sem, send_sem, recv_z, recv_y, recv_c = refs
    else:
        x_ref, out_ref, G, local_sem, send_sem, recv_z, recv_y, recv_c = refs
    nb, w = x_ref.shape
    r = lax.axis_index("row")
    c = lax.axis_index("col")
    y = r // (NZ * NC)
    z = (r // NC) % NZ
    k = r % NC

    def dev(yy, zz, kk):
        return (((yy + NY) % NY) * NZ + (zz + NZ) % NZ) * NC + kk

    def blk(yy, zz, kk):
        return G.at[((yy + NY) % NY) * NZ + (zz + NZ) % NZ, kk]

    def chunk(kk, yy, lo=0, n=NZ):
        return G.at[pl.ds(((yy + NY) % NY) * NZ + lo, n), kk]

    zr, zl = dev(y, z + 1, k), dev(y, z - 1, k)
    yr, yl = dev(y + 1, z, k), dev(y - 1, z, k)
    partner = dev(y, z, 1 - k)

    barrier = pltpu.get_barrier_semaphore()
    for d in (zr, zl, yr, yl, partner):
        pl.semaphore_signal(barrier, inc=1, device_id=(d, c), device_id_type=MESH)
    pl.semaphore_wait(barrier, 5)

    local = pltpu.make_async_copy(x_ref, blk(y, z, k), local_sem.at[0])
    local.start()
    if fused:
        acc[...] = jnp.zeros_like(acc)

    sends = []

    def remote(src, dst, rsem, d, si=0):
        return pltpu.make_async_remote_copy(
            src_ref=src, dst_ref=dst, send_sem=send_sem.at[si], recv_sem=rsem,
            device_id=(d, c), device_id_type=MESH,
        )

    def send(src, dst, rsem, d):
        cp = remote(src, dst, rsem, d, len(sends))
        cp.start()
        sends.append(cp)

    def wait(ref, rsem):
        remote(ref, ref, rsem, partner).wait_recv()

    def multiply(yy):
        if fused:
            plane = (yy + NY) % NY
            cols = pl.ds(pl.multiple_of(plane * (NZ * NC * nb), nb), NZ * NC * nb)
            vec = G[pl.ds(plane * NZ, NZ)].reshape(NZ * NC * nb, w)
            acc[...] += jnp.dot(
                f_ref[:, cols], vec,
                precision=lax.Precision.HIGHEST, preferred_element_type=jnp.float32,
            )

    offs = [0, -1, 1, -2, 2, -3, 3, -4]
    to_right = {0, -1, -2, -3}

    def spread(off):
        i = offs.index(off)
        ref = x_ref if off == 0 else blk(y, z + off, k)
        send(ref, blk(y, z + off, k), recv_y.at[0, i], yr)
        send(ref, blk(y, z + off, k), recv_y.at[1, i], yl)
        send(ref, blk(y, z + off, k), recv_c.at[0, i], partner)

    for s in range(4):
        if s >= 1:
            wait(blk(y, z - s, k), recv_z.at[(z - s + NZ) % NZ])
        send(x_ref if s == 0 else blk(y, z - s, k), blk(y, z - s, k), recv_z.at[(z - s + NZ) % NZ], zr)
        if s < 3:
            if s >= 1:
                wait(blk(y, z + s, k), recv_z.at[(z + s) % NZ])
            send(x_ref if s == 0 else blk(y, z + s, k), blk(y, z + s, k), recv_z.at[(z + s) % NZ], zl)
        if s == 0:
            spread(0)
        else:
            spread(-s)
            if s < 3:
                spread(s)
    wait(blk(y, z - 4, k), recv_z.at[(z - 4 + NZ) % NZ])
    spread(-4)
    wait(blk(y, z + 3, k), recv_z.at[(z + 3) % NZ])
    spread(3)
    local.wait()

    for i, off in enumerate(offs):
        wait(blk(y - 1, z + off, k), recv_y.at[0, i])
        if off in to_right:
            send(blk(y - 1, z + off, k), blk(y - 1, z + off, k), recv_y.at[2, i], yr)
        send(blk(y - 1, z + off, k), blk(y - 1, z + off, k), recv_c.at[3, i], partner)
        wait(blk(y + 1, z + off, k), recv_y.at[1, i])
        if off not in to_right:
            send(blk(y + 1, z + off, k), blk(y + 1, z + off, k), recv_y.at[3, i], yl)
        send(blk(y + 1, z + off, k), blk(y + 1, z + off, k), recv_c.at[1, i], partner)

    def partner_plane(d):
        for i, off in enumerate(offs):
            wait(blk(y + d, z + off, 1 - k), recv_c.at[d % NY, i])
        multiply(y + d)

    partner_plane(0)
    for i, off in enumerate(offs):
        wait(blk(y + 2, z + off, k), recv_y.at[2 if off in to_right else 3, i])
        send(blk(y + 2, z + off, k), blk(y + 2, z + off, k), recv_c.at[2, i], partner)
    for d in (-1, 1, 2):
        partner_plane(d)

    for cp in sends:
        cp.wait_send()
    if fused:
        out_ref[...] = acc[...]
    else:
        out_ref[...] = G[...]


def _sems():
    return [
        pltpu.SemaphoreType.DMA((1,)),
        pltpu.SemaphoreType.DMA((64,)),
        pltpu.SemaphoreType.DMA((NZ,)),
        pltpu.SemaphoreType.DMA((4, NZ)),
        pltpu.SemaphoreType.DMA((NY, NZ)),
    ]


def gather_rows(x, cid):
    nb, w = x.shape
    shape = (NY * NZ, NC, nb, w)
    return pl.pallas_call(
        functools.partial(gather_kernel, fused=False),
        out_shape=jax.ShapeDtypeStruct(shape, x.dtype),
        in_specs=[pl.BlockSpec(memory_space=pltpu.VMEM)],
        out_specs=pl.BlockSpec(memory_space=pltpu.VMEM),
        scratch_shapes=[pltpu.VMEM(shape, x.dtype)] + _sems(),
        compiler_params=pltpu.CompilerParams(collective_id=cid, has_side_effects=True),
        cost_estimate=pl.CostEstimate(flops=0, transcendentals=0, bytes_accessed=2 * x.size * 64 * 4),
    )(x).reshape(-1, w)


def gather_product(matrix, x, cid):
    nb, w = x.shape
    shape = (NY * NZ, NC, nb, w)
    return pl.pallas_call(
        functools.partial(gather_kernel, fused=True),
        out_shape=jax.ShapeDtypeStruct((matrix.shape[0], w), jnp.float32),
        in_specs=[pl.BlockSpec(memory_space=pltpu.VMEM)] * 2,
        out_specs=pl.BlockSpec(memory_space=pltpu.VMEM),
        scratch_shapes=[pltpu.VMEM(shape, x.dtype), pltpu.VMEM((matrix.shape[0], w), jnp.float32)]
        + _sems(),
        compiler_params=pltpu.CompilerParams(collective_id=cid, has_side_effects=True),
        cost_estimate=pl.CostEstimate(
            flops=2 * matrix.shape[0] * matrix.shape[1] * w, transcendentals=0,
            bytes_accessed=(matrix.size + 2 * x.size * 64) * 4,
        ),
    )(x, matrix)


def body(factor, rhs, parent, bounds, slot, structure):
    level, same, link = block_masks(parent, bounds, slot, structure)
    first = lax.axis_index("row") * RB
    level_mine = lax.dynamic_slice_in_dim(level, first, RB, 0)
    same_mine = lax.dynamic_slice_in_dim(same, first, RB, 0)
    link_mine = lax.dynamic_slice_in_dim(link, first, RB, 0)
    full_rows = lax.all_gather(factor, "col", axis=1, tiled=True)
    diag_part = masked(full_rows, same_mine)
    link_part = masked(full_rows, link_mine)

    calls = [0]

    def product(matrix, vector):
        cid = calls[0]
        calls[0] += 1
        if cid == 0:
            return jnp.dot(
                matrix,
                gather_rows(vector, cid),
                precision=lax.Precision.HIGHEST,
                preferred_element_type=jnp.float32,
            )
        return gather_product(matrix, vector, cid)

    pieces = [rhs]
    accums = [jnp.zeros(p.shape, jnp.float32) for p in pieces]
    results = [jnp.zeros(p.shape, jnp.float32) for p in pieces]
    for section in range(3):
        rows = jnp.repeat(level_mine == section, B)[:, None]
        solved = jnp.where(rows, product(diag_part, pieces[0] - accums[0]), 0.0)
        results[0] = results[0] + solved
        if section < 2:
            accums[0] = accums[0] + product(link_part, solved)
    return results[0]


def solution(mesh):
    in_specs = (P("row", "col"), P("row", "col"), P(), P(), P(), P())
    out_specs = P("row", "col")
    return jax.shard_map(body, mesh=mesh, in_specs=in_specs, out_specs=out_specs, check_vma=False)
```

```python
import functools

import jax
import jax.numpy as jnp
from jax import lax
from jax.experimental import pallas as pl
from jax.experimental.pallas import tpu as pltpu
from jax.sharding import PartitionSpec as P

B = 128
RB = 1
MESH = pl.DeviceIdType.MESH
NY, NZ, NC = 4, 8, 2


def block_masks(parent, bounds, slot, structure):
    count = slot.shape[0]
    ar = jnp.arange(count, dtype=jnp.int32)
    logical = jnp.sum(jnp.where(slot[:, None] == ar[None, :], ar[:, None], 0), axis=0)
    node = jnp.sum((logical[:, None] >= bounds[None, 1:7]).astype(jnp.int32), axis=1)
    level = (node >= 4).astype(jnp.int32) + (node >= 6).astype(jnp.int32)
    nodes = jnp.arange(7, dtype=jnp.int32)
    grand = parent[parent]
    ancestor = ((nodes[None, :] == parent[:, None]) | (nodes[None, :] == grand[:, None])) & (
        nodes[None, :] != nodes[:, None]
    )
    node_hot = (node[:, None] == nodes[None, :]).astype(jnp.float32)
    perm_hot = (logical[:, None] == ar[None, :]).astype(jnp.float32)
    listed_store = jnp.dot(
        structure.astype(jnp.float32), perm_hot.T, precision=lax.Precision.HIGHEST
    )
    anc_pairs = jnp.dot(
        node_hot,
        jnp.dot(ancestor.astype(jnp.float32), node_hot.T, precision=lax.Precision.HIGHEST),
        precision=lax.Precision.HIGHEST,
    )
    list_pairs = jnp.dot(node_hot, listed_store, precision=lax.Precision.HIGHEST)
    link = (anc_pairs * list_pairs).T > 0.5
    same = node[:, None] == node[None, :]
    return (level, same, link)


def masked(block_rows, mask):
    rblocks, width = mask.shape
    bsz = block_rows.shape[0] // rblocks
    shaped = block_rows.reshape(rblocks, bsz, width, bsz) * mask[:, None, :, None].astype(
        jnp.float32
    )
    return shaped.reshape(block_rows.shape)


def gather_kernel(*refs, fused):
    if fused:
        x_ref, f_ref, out_ref, G, acc, local_sem, send_sem, recv_z, recv_y, recv_c = refs
    else:
        x_ref, out_ref, G, local_sem, send_sem, recv_z, recv_y, recv_c = refs
    nb, w = x_ref.shape
    r = lax.axis_index("row")
    c = lax.axis_index("col")
    y = r // (NZ * NC)
    z = (r // NC) % NZ
    k = r % NC

    def dev(yy, zz, kk):
        return (((yy + NY) % NY) * NZ + (zz + NZ) % NZ) * NC + kk

    def blk(yy, zz, kk):
        return G.at[((yy + NY) % NY) * NZ + (zz + NZ) % NZ, kk]

    def chunk(kk, yy, lo=0, n=NZ):
        return G.at[pl.ds(((yy + NY) % NY) * NZ + lo, n), kk]

    zr, zl = dev(y, z + 1, k), dev(y, z - 1, k)
    yr, yl = dev(y + 1, z, k), dev(y - 1, z, k)
    partner = dev(y, z, 1 - k)

    barrier = pltpu.get_barrier_semaphore()
    peers = (zr, zl, dev(y, z + 2, k), dev(y, z - 2, k), yr, yl, partner)
    for d in peers:
        pl.semaphore_signal(barrier, inc=1, device_id=(d, c), device_id_type=MESH)
    pl.semaphore_wait(barrier, len(peers))

    local = pltpu.make_async_copy(x_ref, blk(y, z, k), local_sem.at[0])
    local.start()
    if fused:
        acc[...] = jnp.zeros_like(acc)

    sends = []

    def remote(src, dst, rsem, d, si=0):
        return pltpu.make_async_remote_copy(
            src_ref=src, dst_ref=dst, send_sem=send_sem.at[si], recv_sem=rsem,
            device_id=(d, c), device_id_type=MESH,
        )

    def send(src, dst, rsem, d):
        cp = remote(src, dst, rsem, d, len(sends))
        cp.start()
        sends.append(cp)

    def wait(ref, rsem):
        remote(ref, ref, rsem, partner).wait_recv()

    def multiply(yy):
        if fused:
            plane = (yy + NY) % NY
            cols = pl.ds(pl.multiple_of(plane * (NZ * NC * nb), nb), NZ * NC * nb)
            vec = G[pl.ds(plane * NZ, NZ)].reshape(NZ * NC * nb, w)
            acc[...] += jnp.dot(
                f_ref[:, cols], vec,
                precision=lax.Precision.HIGHEST, preferred_element_type=jnp.float32,
            )

    offs = [0, -1, 1, -2, 2, -3, 3, -4]
    to_right = {0, -1, -2, -3}

    def spread(off):
        i = offs.index(off)
        ref = x_ref if off == 0 else blk(y, z + off, k)
        send(ref, blk(y, z + off, k), recv_y.at[0, i], yr)
        send(ref, blk(y, z + off, k), recv_y.at[1, i], yl)
        send(ref, blk(y, z + off, k), recv_c.at[0, i], partner)

    def recv_of(zsrc):
        return recv_z.at[(zsrc + NZ) % NZ]

    for d in (1, 2, -1, -2):
        send(x_ref, blk(y, z, k), recv_of(z), dev(y, z + d, k))
    spread(0)
    wait(blk(y, z - 2, k), recv_of(z - 2))
    send(blk(y, z - 2, k), blk(y, z - 2, k), recv_of(z - 2), dev(y, z + 1, k))
    send(blk(y, z - 2, k), blk(y, z - 2, k), recv_of(z - 2), dev(y, z + 2, k))
    wait(blk(y, z + 2, k), recv_of(z + 2))
    send(blk(y, z + 2, k), blk(y, z + 2, k), recv_of(z + 2), dev(y, z - 1, k))
    for off in (-1, 1):
        wait(blk(y, z + off, k), recv_of(z + off))
        spread(off)
    spread(-2)
    spread(2)
    for off in (-3, 3, -4):
        wait(blk(y, z + off, k), recv_of(z + off))
        spread(off)
    local.wait()

    for i, off in enumerate(offs):
        wait(blk(y - 1, z + off, k), recv_y.at[0, i])
        if off in to_right:
            send(blk(y - 1, z + off, k), blk(y - 1, z + off, k), recv_y.at[2, i], yr)
        send(blk(y - 1, z + off, k), blk(y - 1, z + off, k), recv_c.at[3, i], partner)
        wait(blk(y + 1, z + off, k), recv_y.at[1, i])
        if off not in to_right:
            send(blk(y + 1, z + off, k), blk(y + 1, z + off, k), recv_y.at[3, i], yl)
        send(blk(y + 1, z + off, k), blk(y + 1, z + off, k), recv_c.at[1, i], partner)

    def partner_plane(d):
        for i, off in enumerate(offs):
            wait(blk(y + d, z + off, 1 - k), recv_c.at[d % NY, i])
        multiply(y + d)

    partner_plane(0)
    for i, off in enumerate(offs):
        wait(blk(y + 2, z + off, k), recv_y.at[2 if off in to_right else 3, i])
        send(blk(y + 2, z + off, k), blk(y + 2, z + off, k), recv_c.at[2, i], partner)
    for d in (-1, 1, 2):
        partner_plane(d)

    for cp in sends:
        cp.wait_send()
    if fused:
        out_ref[...] = acc[...]
    else:
        out_ref[...] = G[...]


def _sems():
    return [
        pltpu.SemaphoreType.DMA((1,)),
        pltpu.SemaphoreType.DMA((64,)),
        pltpu.SemaphoreType.DMA((NZ,)),
        pltpu.SemaphoreType.DMA((4, NZ)),
        pltpu.SemaphoreType.DMA((NY, NZ)),
    ]


def gather_rows(x, cid):
    nb, w = x.shape
    shape = (NY * NZ, NC, nb, w)
    return pl.pallas_call(
        functools.partial(gather_kernel, fused=False),
        out_shape=jax.ShapeDtypeStruct(shape, x.dtype),
        in_specs=[pl.BlockSpec(memory_space=pltpu.VMEM)],
        out_specs=pl.BlockSpec(memory_space=pltpu.VMEM),
        scratch_shapes=[pltpu.VMEM(shape, x.dtype)] + _sems(),
        compiler_params=pltpu.CompilerParams(collective_id=cid, has_side_effects=True),
        cost_estimate=pl.CostEstimate(flops=0, transcendentals=0, bytes_accessed=2 * x.size * 64 * 4),
    )(x).reshape(-1, w)


def gather_product(matrix, x, cid):
    nb, w = x.shape
    shape = (NY * NZ, NC, nb, w)
    return pl.pallas_call(
        functools.partial(gather_kernel, fused=True),
        out_shape=jax.ShapeDtypeStruct((matrix.shape[0], w), jnp.float32),
        in_specs=[pl.BlockSpec(memory_space=pltpu.VMEM)] * 2,
        out_specs=pl.BlockSpec(memory_space=pltpu.VMEM),
        scratch_shapes=[pltpu.VMEM(shape, x.dtype), pltpu.VMEM((matrix.shape[0], w), jnp.float32)]
        + _sems(),
        compiler_params=pltpu.CompilerParams(collective_id=cid, has_side_effects=True),
        cost_estimate=pl.CostEstimate(
            flops=2 * matrix.shape[0] * matrix.shape[1] * w, transcendentals=0,
            bytes_accessed=(matrix.size + 2 * x.size * 64) * 4,
        ),
    )(x, matrix)


def body(factor, rhs, parent, bounds, slot, structure):
    level, same, link = block_masks(parent, bounds, slot, structure)
    first = lax.axis_index("row") * RB
    level_mine = lax.dynamic_slice_in_dim(level, first, RB, 0)
    same_mine = lax.dynamic_slice_in_dim(same, first, RB, 0)
    link_mine = lax.dynamic_slice_in_dim(link, first, RB, 0)
    full_rows = lax.all_gather(factor, "col", axis=1, tiled=True)
    diag_part = masked(full_rows, same_mine)
    link_part = masked(full_rows, link_mine)

    calls = [0]

    def product(matrix, vector):
        cid = calls[0]
        calls[0] += 1
        if cid == 0:
            return jnp.dot(
                matrix,
                gather_rows(vector, cid),
                precision=lax.Precision.HIGHEST,
                preferred_element_type=jnp.float32,
            )
        return gather_product(matrix, vector, cid)

    pieces = [rhs]
    accums = [jnp.zeros(p.shape, jnp.float32) for p in pieces]
    results = [jnp.zeros(p.shape, jnp.float32) for p in pieces]
    for section in range(3):
        rows = jnp.repeat(level_mine == section, B)[:, None]
        solved = jnp.where(rows, product(diag_part, pieces[0] - accums[0]), 0.0)
        results[0] = results[0] + solved
        if section < 2:
            accums[0] = accums[0] + product(link_part, solved)
    return results[0]


def solution(mesh):
    in_specs = (P("row", "col"), P("row", "col"), P(), P(), P(), P())
    out_specs = P("row", "col")
    return jax.shard_map(body, mesh=mesh, in_specs=in_specs, out_specs=out_specs, check_vma=False)
```

```python
import functools

import jax
import jax.numpy as jnp
from jax import lax
from jax.experimental import pallas as pl
from jax.experimental.pallas import tpu as pltpu
from jax.sharding import PartitionSpec as P

B = 128
RB = 1
MESH = pl.DeviceIdType.MESH
NY, NZ, NC = 4, 8, 2


def block_masks(parent, bounds, slot, structure):
    count = slot.shape[0]
    ar = jnp.arange(count, dtype=jnp.int32)
    logical = jnp.sum(jnp.where(slot[:, None] == ar[None, :], ar[:, None], 0), axis=0)
    node = jnp.sum((logical[:, None] >= bounds[None, 1:7]).astype(jnp.int32), axis=1)
    level = (node >= 4).astype(jnp.int32) + (node >= 6).astype(jnp.int32)
    nodes = jnp.arange(7, dtype=jnp.int32)
    grand = parent[parent]
    ancestor = ((nodes[None, :] == parent[:, None]) | (nodes[None, :] == grand[:, None])) & (
        nodes[None, :] != nodes[:, None]
    )
    node_hot = (node[:, None] == nodes[None, :]).astype(jnp.float32)
    perm_hot = (logical[:, None] == ar[None, :]).astype(jnp.float32)
    listed_store = jnp.dot(
        structure.astype(jnp.float32), perm_hot.T, precision=lax.Precision.HIGHEST
    )
    anc_pairs = jnp.dot(
        node_hot,
        jnp.dot(ancestor.astype(jnp.float32), node_hot.T, precision=lax.Precision.HIGHEST),
        precision=lax.Precision.HIGHEST,
    )
    list_pairs = jnp.dot(node_hot, listed_store, precision=lax.Precision.HIGHEST)
    link = (anc_pairs * list_pairs).T > 0.5
    same = node[:, None] == node[None, :]
    return (level, same, link)


def masked(block_rows, mask):
    rblocks, width = mask.shape
    bsz = block_rows.shape[0] // rblocks
    shaped = block_rows.reshape(rblocks, bsz, width, bsz) * mask[:, None, :, None].astype(
        jnp.float32
    )
    return shaped.reshape(block_rows.shape)


def gather_kernel(*refs, mode):
    fused = True
    if mode == "first":
        x_ref, floc_ref, m_ref, out_ref, fout_ref, G, f_ref, acc, local_sem, send_sem, recv_z, recv_y, recv_c, \
            recv_x = refs
    else:
        x_ref, f_ref, m_ref, out_ref, G, acc, local_sem, send_sem, recv_z, recv_y, recv_c = refs
    nb, w = x_ref.shape
    r = lax.axis_index("row")
    c = lax.axis_index("col")
    y = r // (NZ * NC)
    z = (r // NC) % NZ
    k = r % NC

    def dev(yy, zz, kk):
        return (((yy + NY) % NY) * NZ + (zz + NZ) % NZ) * NC + kk

    def blk(yy, zz, kk):
        return G.at[((yy + NY) % NY) * NZ + (zz + NZ) % NZ, kk]

    def chunk(kk, yy, lo=0, n=NZ):
        return G.at[pl.ds(((yy + NY) % NY) * NZ + lo, n), kk]

    zr, zl = dev(y, z + 1, k), dev(y, z - 1, k)
    yr, yl = dev(y + 1, z, k), dev(y - 1, z, k)
    partner = dev(y, z, 1 - k)

    barrier = pltpu.get_barrier_semaphore()
    peers = [(d, c) for d in (zr, zl, dev(y, z + 2, k), dev(y, z - 2, k), yr, yl, partner)]
    nx = 4
    xr, xl = (r, (c + 1) % nx), (r, (c + nx - 1) % nx)
    if mode == "first":
        peers += [xr, xl]
    for d in peers:
        pl.semaphore_signal(barrier, inc=1, device_id=d, device_id_type=MESH)
    pl.semaphore_wait(barrier, len(peers))

    local = pltpu.make_async_copy(x_ref, blk(y, z, k), local_sem.at[0])
    local.start()
    acc[...] = jnp.zeros_like(acc)

    if mode == "first":
        wcol = floc_ref.shape[1]
        hcol = wcol // 2

        def fcols(cc, lo=0, n=wcol):
            return f_ref.at[:, pl.ds(pl.multiple_of(((cc + nx) % nx) * wcol + lo, 128), n)]

        def xcopy(src, dst, si, rsem, d):
            return pltpu.make_async_remote_copy(
                src_ref=src, dst_ref=dst, send_sem=send_sem.at[si], recv_sem=rsem,
                device_id=d, device_id_type=MESH,
            )

        flocal = pltpu.make_async_copy(floc_ref, fcols(c), local_sem.at[1])
        flocal.start()
        xsends = [xcopy(floc_ref, fcols(c), 64, recv_x.at[0], xr), xcopy(floc_ref, fcols(c), 65, recv_x.at[1], xl)]
        for cp in xsends:
            cp.start()

    sends = []

    def remote(src, dst, rsem, d, si=0):
        return pltpu.make_async_remote_copy(
            src_ref=src, dst_ref=dst, send_sem=send_sem.at[si], recv_sem=rsem,
            device_id=(d, c), device_id_type=MESH,
        )

    def send(src, dst, rsem, d):
        cp = remote(src, dst, rsem, d, len(sends))
        cp.start()
        sends.append(cp)

    def wait(ref, rsem):
        remote(ref, ref, rsem, partner).wait_recv()

    def multiply(yy):
        if fused:
            plane = (yy + NY) % NY
            cols = pl.ds(pl.multiple_of(plane * (NZ * NC * nb), nb), NZ * NC * nb)
            vec = G[pl.ds(plane * NZ, NZ)].reshape(NZ * NC * nb, w)
            acc[...] += jnp.dot(
                f_ref[:, cols] * m_ref[:, cols], vec,
                precision=lax.Precision.HIGHEST, preferred_element_type=jnp.float32,
            )

    offs = [0, -1, 1, -2, 2, -3, 3, -4]
    to_right = {0, -1, -2, -3}

    def spread(off):
        i = offs.index(off)
        ref = x_ref if off == 0 else blk(y, z + off, k)
        send(ref, blk(y, z + off, k), recv_y.at[0, i], yr)
        send(ref, blk(y, z + off, k), recv_y.at[1, i], yl)
        send(ref, blk(y, z + off, k), recv_c.at[0, i], partner)

    def recv_of(zsrc):
        return recv_z.at[(zsrc + NZ) % NZ]

    for d in (1, 2, -1, -2):
        send(x_ref, blk(y, z, k), recv_of(z), dev(y, z + d, k))
    spread(0)
    wait(blk(y, z - 2, k), recv_of(z - 2))
    send(blk(y, z - 2, k), blk(y, z - 2, k), recv_of(z - 2), dev(y, z + 1, k))
    send(blk(y, z - 2, k), blk(y, z - 2, k), recv_of(z - 2), dev(y, z + 2, k))
    wait(blk(y, z + 2, k), recv_of(z + 2))
    send(blk(y, z + 2, k), blk(y, z + 2, k), recv_of(z + 2), dev(y, z - 1, k))
    for off in (-1, 1):
        wait(blk(y, z + off, k), recv_of(z + off))
        spread(off)
    spread(-2)
    spread(2)
    for off in (-3, 3, -4):
        wait(blk(y, z + off, k), recv_of(z + off))
        spread(off)
    local.wait()

    for i, off in enumerate(offs):
        wait(blk(y - 1, z + off, k), recv_y.at[0, i])
        if off in to_right:
            send(blk(y - 1, z + off, k), blk(y - 1, z + off, k), recv_y.at[2, i], yr)
        send(blk(y - 1, z + off, k), blk(y - 1, z + off, k), recv_c.at[3, i], partner)
        wait(blk(y + 1, z + off, k), recv_y.at[1, i])
        if off not in to_right:
            send(blk(y + 1, z + off, k), blk(y + 1, z + off, k), recv_y.at[3, i], yl)
        send(blk(y + 1, z + off, k), blk(y + 1, z + off, k), recv_c.at[1, i], partner)

    def partner_plane(d):
        for i, off in enumerate(offs):
            wait(blk(y + d, z + off, 1 - k), recv_c.at[d % NY, i])
        multiply(y + d)

    def partner_wait(d):
        for i, off in enumerate(offs):
            wait(blk(y + d, z + off, 1 - k), recv_c.at[d % NY, i])

    if mode == "first":
        xcopy(floc_ref, fcols(c - 1), 0, recv_x.at[0], xr).wait_recv()
        xsends.append(xcopy(fcols(c - 1, 0, hcol), fcols(c - 1, 0, hcol), 66, recv_x.at[2], xr))
        xsends[-1].start()
        xcopy(floc_ref, fcols(c + 1), 0, recv_x.at[1], xr).wait_recv()
        xsends.append(xcopy(fcols(c + 1, hcol, hcol), fcols(c + 1, hcol, hcol), 67, recv_x.at[3], xl))
        xsends[-1].start()
    else:
        partner_wait(0)
        multiply(y)
    for i, off in enumerate(offs):
        wait(blk(y + 2, z + off, k), recv_y.at[2 if off in to_right else 3, i])
        send(blk(y + 2, z + off, k), blk(y + 2, z + off, k), recv_c.at[2, i], partner)
    if mode == "first":
        for d in (0, -1, 1, 2):
            partner_wait(d)
        flocal.wait()
        multiply(c)
        multiply(c - 1)
        multiply(c + 1)
        xcopy(fcols(c + 2, 0, hcol), fcols(c + 2, 0, hcol), 0, recv_x.at[2], xr).wait_recv()
        xcopy(fcols(c + 2, hcol, hcol), fcols(c + 2, hcol, hcol), 0, recv_x.at[3], xr).wait_recv()
        multiply(c + 2)
        for cp in xsends:
            cp.wait_send()
        fout = pltpu.make_async_copy(f_ref, fout_ref, local_sem.at[1])
        fout.start()
        fout.wait()
    else:
        for d in (-1, 1, 2):
            partner_wait(d)
            multiply(y + d)

    for cp in sends:
        cp.wait_send()
    out_ref[...] = acc[...]


def _sems():
    return [
        pltpu.SemaphoreType.DMA((2,)),
        pltpu.SemaphoreType.DMA((68,)),
        pltpu.SemaphoreType.DMA((NZ,)),
        pltpu.SemaphoreType.DMA((4, NZ)),
        pltpu.SemaphoreType.DMA((NY, NZ)),
    ]


def _specs(n):
    return [pl.BlockSpec(memory_space=pltpu.VMEM)] * n


def first_product(floc, mask_row, x, cid):
    nb, w = x.shape
    rows = floc.shape[0]
    ncol = floc.shape[1] * 4
    return pl.pallas_call(
        functools.partial(gather_kernel, mode="first"),
        out_shape=(jax.ShapeDtypeStruct((rows, w), jnp.float32), jax.ShapeDtypeStruct((rows, ncol), floc.dtype)),
        in_specs=_specs(3),
        out_specs=(pl.BlockSpec(memory_space=pltpu.VMEM), pl.BlockSpec(memory_space=pl.ANY)),
        scratch_shapes=[pltpu.VMEM((NY * NZ, NC, nb, w), x.dtype), pltpu.VMEM((rows, ncol), floc.dtype),
                        pltpu.VMEM((rows, w), jnp.float32)]
        + _sems() + [pltpu.SemaphoreType.DMA((4,))],
        compiler_params=pltpu.CompilerParams(collective_id=cid, has_side_effects=True),
        cost_estimate=pl.CostEstimate(
            flops=2 * rows * ncol * w, transcendentals=0, bytes_accessed=(2 * rows * ncol + 2 * x.size * 64) * 4,
        ),
    )(x, floc, mask_row)


def gather_product(matrix, mask_row, x, cid):
    nb, w = x.shape
    shape = (NY * NZ, NC, nb, w)
    return pl.pallas_call(
        functools.partial(gather_kernel, mode="fused"),
        out_shape=jax.ShapeDtypeStruct((matrix.shape[0], w), jnp.float32),
        in_specs=_specs(3),
        out_specs=pl.BlockSpec(memory_space=pltpu.VMEM),
        scratch_shapes=[pltpu.VMEM(shape, x.dtype), pltpu.VMEM((matrix.shape[0], w), jnp.float32)]
        + _sems(),
        compiler_params=pltpu.CompilerParams(collective_id=cid, has_side_effects=True),
        cost_estimate=pl.CostEstimate(
            flops=2 * matrix.shape[0] * matrix.shape[1] * w, transcendentals=0,
            bytes_accessed=(matrix.size + 2 * x.size * 64) * 4,
        ),
    )(x, matrix, mask_row)


def body(factor, rhs, parent, bounds, slot, structure):
    level, same, link = block_masks(parent, bounds, slot, structure)
    first = lax.axis_index("row") * RB
    level_mine = lax.dynamic_slice_in_dim(level, first, RB, 0)
    same_row = jnp.repeat(lax.dynamic_slice_in_dim(same, first, RB, 0).astype(jnp.float32), B, axis=1)
    link_row = jnp.repeat(lax.dynamic_slice_in_dim(link, first, RB, 0).astype(jnp.float32), B, axis=1)

    rows0 = jnp.repeat(level_mine == 0, B)[:, None]
    first_prod, full_rows = first_product(factor, same_row, rhs, 0)
    solved = jnp.where(rows0, first_prod, 0.0)
    result = solved
    accum = gather_product(full_rows, link_row, solved, 1)
    for section in (1, 2):
        rows = jnp.repeat(level_mine == section, B)[:, None]
        solved = jnp.where(rows, gather_product(full_rows, same_row, rhs - accum, 2 * section), 0.0)
        result = result + solved
        if section < 2:
            accum = accum + gather_product(full_rows, link_row, solved, 2 * section + 1)
    return result


def solution(mesh):
    in_specs = (P("row", "col"), P("row", "col"), P(), P(), P(), P())
    out_specs = P("row", "col")
    return jax.shard_map(body, mesh=mesh, in_specs=in_specs, out_specs=out_specs, check_vma=False)
```

```python
import functools

import jax
import jax.numpy as jnp
from jax import lax
from jax.experimental import pallas as pl
from jax.experimental.pallas import tpu as pltpu
from jax.sharding import PartitionSpec as P

B = 128
RB = 1
MESH = pl.DeviceIdType.MESH
NY, NZ, NC = 4, 8, 2


def row_masks(parent, bounds, slot, structure, r):
    count = slot.shape[0]
    ar = jnp.arange(count, dtype=jnp.int32)
    nodes = jnp.arange(parent.shape[0], dtype=jnp.int32)
    logical = jnp.sum(jnp.where(slot[:, None] == ar[None, :], ar[:, None], 0), axis=0)
    node = jnp.sum((logical[:, None] >= bounds[None, 1:7]).astype(jnp.int32), axis=1)
    mine = ar == r
    node_r = jnp.sum(jnp.where(mine, node, 0))
    logical_r = jnp.sum(jnp.where(mine, logical, 0))
    level_r = (node_r >= 4).astype(jnp.int32) + (node_r >= 6).astype(jnp.int32)
    hot = node[:, None] == nodes[None, :]
    par = jnp.sum(jnp.where(hot, parent[None, :], 0), axis=1)
    grand = jnp.sum(jnp.where(par[:, None] == nodes[None, :], parent[None, :], 0), axis=1)
    ancestor = ((par == node_r) | (grand == node_r)) & (node != node_r)
    column = jnp.sum(jnp.where(ar[None, :] == logical_r, structure, 0), axis=1)
    listed = jnp.sum(jnp.where(hot, column[None, :], 0), axis=1) == 1
    return level_r, node == node_r, ancestor & listed


def gather_kernel(*refs, mode):
    fused = True
    if mode == "first":
        x_ref, floc_ref, m_ref, out_ref, fout_ref, G, f_ref, acc, local_sem, send_sem, recv_z, recv_y, recv_c, \
            recv_x = refs
    else:
        x_ref, f_ref, m_ref, out_ref, G, acc, local_sem, send_sem, recv_z, recv_y, recv_c = refs
    nb, w = x_ref.shape
    r = lax.axis_index("row")
    c = lax.axis_index("col")
    y = r // (NZ * NC)
    z = (r // NC) % NZ
    k = r % NC

    def dev(yy, zz, kk):
        return (((yy + NY) % NY) * NZ + (zz + NZ) % NZ) * NC + kk

    def blk(yy, zz, kk):
        return G.at[((yy + NY) % NY) * NZ + (zz + NZ) % NZ, kk]

    def chunk(kk, yy, lo=0, n=NZ):
        return G.at[pl.ds(((yy + NY) % NY) * NZ + lo, n), kk]

    zr, zl = dev(y, z + 1, k), dev(y, z - 1, k)
    yr, yl = dev(y + 1, z, k), dev(y - 1, z, k)
    partner = dev(y, z, 1 - k)

    barrier = pltpu.get_barrier_semaphore()
    peers = [(d, c) for d in (zr, zl, dev(y, z + 2, k), dev(y, z - 2, k), yr, yl, partner)]
    nx = 4
    xr, xl = (r, (c + 1) % nx), (r, (c + nx - 1) % nx)
    if mode == "first":
        peers += [xr, xl]
    for d in peers:
        pl.semaphore_signal(barrier, inc=1, device_id=d, device_id_type=MESH)
    pl.semaphore_wait(barrier, len(peers))

    local = pltpu.make_async_copy(x_ref, blk(y, z, k), local_sem.at[0])
    local.start()
    acc[...] = jnp.zeros_like(acc)

    if mode == "first":
        wcol = floc_ref.shape[1]
        hcol = wcol // 2

        def fcols(cc, lo=0, n=wcol):
            return f_ref.at[:, pl.ds(pl.multiple_of(((cc + nx) % nx) * wcol + lo, 128), n)]

        def xcopy(src, dst, si, rsem, d):
            return pltpu.make_async_remote_copy(
                src_ref=src, dst_ref=dst, send_sem=send_sem.at[si], recv_sem=rsem,
                device_id=d, device_id_type=MESH,
            )

        flocal = pltpu.make_async_copy(floc_ref, fcols(c), local_sem.at[1])
        flocal.start()
        xsends = [xcopy(floc_ref, fcols(c), 64, recv_x.at[0], xr), xcopy(floc_ref, fcols(c), 65, recv_x.at[1], xl)]
        for cp in xsends:
            cp.start()

    sends = []

    def remote(src, dst, rsem, d, si=0):
        return pltpu.make_async_remote_copy(
            src_ref=src, dst_ref=dst, send_sem=send_sem.at[si], recv_sem=rsem,
            device_id=(d, c), device_id_type=MESH,
        )

    def send(src, dst, rsem, d):
        cp = remote(src, dst, rsem, d, len(sends))
        cp.start()
        sends.append(cp)

    def wait(ref, rsem):
        remote(ref, ref, rsem, partner).wait_recv()

    def multiply(yy):
        if fused:
            plane = (yy + NY) % NY
            cols = pl.ds(pl.multiple_of(plane * (NZ * NC * nb), nb), NZ * NC * nb)
            vec = G[pl.ds(plane * NZ, NZ)].reshape(NZ * NC * nb, w)
            acc[...] += jnp.dot(
                f_ref[:, cols] * m_ref[:, cols], vec,
                precision=lax.Precision.HIGHEST, preferred_element_type=jnp.float32,
            )

    offs = [0, -1, 1, -2, 2, -3, 3, -4]
    to_right = {0, -1, -2, -3}

    def spread(off):
        i = offs.index(off)
        ref = x_ref if off == 0 else blk(y, z + off, k)
        send(ref, blk(y, z + off, k), recv_y.at[0, i], yr)
        send(ref, blk(y, z + off, k), recv_y.at[1, i], yl)
        send(ref, blk(y, z + off, k), recv_c.at[0, i], partner)

    def recv_of(zsrc):
        return recv_z.at[(zsrc + NZ) % NZ]

    for d in (1, 2, -1, -2):
        send(x_ref, blk(y, z, k), recv_of(z), dev(y, z + d, k))
    spread(0)
    wait(blk(y, z - 2, k), recv_of(z - 2))
    send(blk(y, z - 2, k), blk(y, z - 2, k), recv_of(z - 2), dev(y, z + 1, k))
    send(blk(y, z - 2, k), blk(y, z - 2, k), recv_of(z - 2), dev(y, z + 2, k))
    wait(blk(y, z + 2, k), recv_of(z + 2))
    send(blk(y, z + 2, k), blk(y, z + 2, k), recv_of(z + 2), dev(y, z - 1, k))
    for off in (-1, 1):
        wait(blk(y, z + off, k), recv_of(z + off))
        spread(off)
    spread(-2)
    spread(2)
    for off in (-3, 3, -4):
        wait(blk(y, z + off, k), recv_of(z + off))
        spread(off)
    local.wait()

    for i, off in enumerate(offs):
        wait(blk(y - 1, z + off, k), recv_y.at[0, i])
        if off in to_right:
            send(blk(y - 1, z + off, k), blk(y - 1, z + off, k), recv_y.at[2, i], yr)
        send(blk(y - 1, z + off, k), blk(y - 1, z + off, k), recv_c.at[3, i], partner)
        wait(blk(y + 1, z + off, k), recv_y.at[1, i])
        if off not in to_right:
            send(blk(y + 1, z + off, k), blk(y + 1, z + off, k), recv_y.at[3, i], yl)
        send(blk(y + 1, z + off, k), blk(y + 1, z + off, k), recv_c.at[1, i], partner)

    def partner_plane(d):
        for i, off in enumerate(offs):
            wait(blk(y + d, z + off, 1 - k), recv_c.at[d % NY, i])
        multiply(y + d)

    def partner_wait(d):
        for i, off in enumerate(offs):
            wait(blk(y + d, z + off, 1 - k), recv_c.at[d % NY, i])

    if mode == "first":
        xcopy(floc_ref, fcols(c - 1), 0, recv_x.at[0], xr).wait_recv()
        xsends.append(xcopy(fcols(c - 1, 0, hcol), fcols(c - 1, 0, hcol), 66, recv_x.at[2], xr))
        xsends[-1].start()
        xcopy(floc_ref, fcols(c + 1), 0, recv_x.at[1], xr).wait_recv()
        xsends.append(xcopy(fcols(c + 1, hcol, hcol), fcols(c + 1, hcol, hcol), 67, recv_x.at[3], xl))
        xsends[-1].start()
    else:
        partner_wait(0)
        multiply(y)
    for i, off in enumerate(offs):
        wait(blk(y + 2, z + off, k), recv_y.at[2 if off in to_right else 3, i])
        send(blk(y + 2, z + off, k), blk(y + 2, z + off, k), recv_c.at[2, i], partner)
    if mode == "first":
        for d in (0, -1, 1, 2):
            partner_wait(d)
        flocal.wait()
        multiply(c)
        multiply(c - 1)
        multiply(c + 1)
        xcopy(fcols(c + 2, 0, hcol), fcols(c + 2, 0, hcol), 0, recv_x.at[2], xr).wait_recv()
        xcopy(fcols(c + 2, hcol, hcol), fcols(c + 2, hcol, hcol), 0, recv_x.at[3], xr).wait_recv()
        multiply(c + 2)
        for cp in xsends:
            cp.wait_send()
        fout = pltpu.make_async_copy(f_ref, fout_ref, local_sem.at[1])
        fout.start()
        fout.wait()
    else:
        for d in (-1, 1, 2):
            partner_wait(d)
            multiply(y + d)

    for cp in sends:
        cp.wait_send()
    out_ref[...] = acc[...]


def _sems():
    return [
        pltpu.SemaphoreType.DMA((2,)),
        pltpu.SemaphoreType.DMA((68,)),
        pltpu.SemaphoreType.DMA((NZ,)),
        pltpu.SemaphoreType.DMA((4, NZ)),
        pltpu.SemaphoreType.DMA((NY, NZ)),
    ]


def _specs(n):
    return [pl.BlockSpec(memory_space=pltpu.VMEM)] * n


def first_product(floc, mask_row, x, cid):
    nb, w = x.shape
    rows = floc.shape[0]
    ncol = floc.shape[1] * 4
    return pl.pallas_call(
        functools.partial(gather_kernel, mode="first"),
        out_shape=(jax.ShapeDtypeStruct((rows, w), jnp.float32), jax.ShapeDtypeStruct((rows, ncol), floc.dtype)),
        in_specs=_specs(3),
        out_specs=(pl.BlockSpec(memory_space=pltpu.VMEM), pl.BlockSpec(memory_space=pl.ANY)),
        scratch_shapes=[pltpu.VMEM((NY * NZ, NC, nb, w), x.dtype), pltpu.VMEM((rows, ncol), floc.dtype),
                        pltpu.VMEM((rows, w), jnp.float32)]
        + _sems() + [pltpu.SemaphoreType.DMA((4,))],
        compiler_params=pltpu.CompilerParams(collective_id=cid, has_side_effects=True),
        cost_estimate=pl.CostEstimate(
            flops=2 * rows * ncol * w, transcendentals=0, bytes_accessed=(2 * rows * ncol + 2 * x.size * 64) * 4,
        ),
    )(x, floc, mask_row)


def gather_product(matrix, mask_row, x, cid):
    nb, w = x.shape
    shape = (NY * NZ, NC, nb, w)
    return pl.pallas_call(
        functools.partial(gather_kernel, mode="fused"),
        out_shape=jax.ShapeDtypeStruct((matrix.shape[0], w), jnp.float32),
        in_specs=_specs(3),
        out_specs=pl.BlockSpec(memory_space=pltpu.VMEM),
        scratch_shapes=[pltpu.VMEM(shape, x.dtype), pltpu.VMEM((matrix.shape[0], w), jnp.float32)]
        + _sems(),
        compiler_params=pltpu.CompilerParams(collective_id=cid, has_side_effects=True),
        cost_estimate=pl.CostEstimate(
            flops=2 * matrix.shape[0] * matrix.shape[1] * w, transcendentals=0,
            bytes_accessed=(matrix.size + 2 * x.size * 64) * 4,
        ),
    )(x, matrix, mask_row)


def body(factor, rhs, parent, bounds, slot, structure):
    level_mine, same, link = row_masks(parent, bounds, slot, structure, lax.axis_index("row"))
    same_row = jnp.repeat(same.astype(jnp.float32), B)[None, :]
    link_row = jnp.repeat(link.astype(jnp.float32), B)[None, :]

    rows0 = level_mine == 0
    first_prod, full_rows = first_product(factor, same_row, rhs, 0)
    solved = jnp.where(rows0, first_prod, 0.0)
    result = solved
    accum = gather_product(full_rows, link_row, solved, 1)
    for section in (1, 2):
        rows = level_mine == section
        solved = jnp.where(rows, gather_product(full_rows, same_row, rhs - accum, 2 * section), 0.0)
        result = result + solved
        if section < 2:
            accum = accum + gather_product(full_rows, link_row, solved, 2 * section + 1)
    return result


def solution(mesh):
    in_specs = (P("row", "col"), P("row", "col"), P(), P(), P(), P())
    out_specs = P("row", "col")
    return jax.shard_map(body, mesh=mesh, in_specs=in_specs, out_specs=out_specs, check_vma=False)
```

```python
import functools

import jax
import jax.numpy as jnp
from jax import lax
from jax.experimental import pallas as pl
from jax.experimental.pallas import tpu as pltpu
from jax.sharding import PartitionSpec as P

B = 128
RB = 1
MESH = pl.DeviceIdType.MESH
NY, NZ, NC = 4, 8, 2


def row_masks(parent, bounds, slot, structure, r):
    count = slot.shape[0]
    ar = jnp.arange(count, dtype=jnp.int32)
    nodes = jnp.arange(parent.shape[0], dtype=jnp.int32)
    logical = jnp.sum(jnp.where(slot[:, None] == ar[None, :], ar[:, None], 0), axis=0)
    node = jnp.sum((logical[:, None] >= bounds[None, 1:7]).astype(jnp.int32), axis=1)
    mine = ar == r
    node_r = jnp.sum(jnp.where(mine, node, 0))
    logical_r = jnp.sum(jnp.where(mine, logical, 0))
    level_r = (node_r >= 4).astype(jnp.int32) + (node_r >= 6).astype(jnp.int32)
    hot = node[:, None] == nodes[None, :]
    par = jnp.sum(jnp.where(hot, parent[None, :], 0), axis=1)
    grand = jnp.sum(jnp.where(par[:, None] == nodes[None, :], parent[None, :], 0), axis=1)
    ancestor = ((par == node_r) | (grand == node_r)) & (node != node_r)
    column = jnp.sum(jnp.where(ar[None, :] == logical_r, structure, 0), axis=1)
    listed = jnp.sum(jnp.where(hot, column[None, :], 0), axis=1) == 1
    return level_r, node == node_r, ancestor & listed


def gather_kernel(*refs, mode):
    fused = True
    if mode == "first":
        x_ref, floc_ref, m_ref, out_ref, fout_ref, G, f_ref, acc, local_sem, send_sem, recv_z, recv_y, recv_c, \
            recv_w, recv_x = refs
    else:
        x_ref, f_ref, m_ref, out_ref, G, acc, local_sem, send_sem, recv_z, recv_y, recv_c, recv_w = refs
    nb, w = x_ref.shape
    r = lax.axis_index("row")
    c = lax.axis_index("col")
    y = r // (NZ * NC)
    z = (r // NC) % NZ
    k = r % NC

    def dev(yy, zz, kk):
        return (((yy + NY) % NY) * NZ + (zz + NZ) % NZ) * NC + kk

    def blk(yy, zz, kk):
        return G.at[((yy + NY) % NY) * NZ + (zz + NZ) % NZ, kk]

    def chunk(kk, yy, lo=0, n=NZ):
        return G.at[pl.ds(((yy + NY) % NY) * NZ + lo, n), kk]

    zr, zl = dev(y, z + 1, k), dev(y, z - 1, k)
    yr, yl = dev(y + 1, z, k), dev(y - 1, z, k)
    partner = dev(y, z, 1 - k)

    barrier = pltpu.get_barrier_semaphore()
    peers = [(d, c) for d in (zr, zl, yr, yl, partner)]
    nx = 4
    xr, xl = (r, (c + 1) % nx), (r, (c + nx - 1) % nx)
    if mode == "first":
        peers += [xr, xl]
    for d in peers:
        pl.semaphore_signal(barrier, inc=1, device_id=d, device_id_type=MESH)
    pl.semaphore_wait(barrier, len(peers))

    local = pltpu.make_async_copy(x_ref, blk(y, z, k), local_sem.at[0])
    local.start()
    acc[...] = jnp.zeros_like(acc)

    if mode == "first":
        wcol = floc_ref.shape[1]
        hcol = wcol // 2

        def fcols(cc, lo=0, n=wcol):
            return f_ref.at[:, pl.ds(pl.multiple_of(((cc + nx) % nx) * wcol + lo, 128), n)]

        def xcopy(src, dst, si, rsem, d):
            return pltpu.make_async_remote_copy(
                src_ref=src, dst_ref=dst, send_sem=send_sem.at[si], recv_sem=rsem,
                device_id=d, device_id_type=MESH,
            )

        flocal = pltpu.make_async_copy(floc_ref, fcols(c), local_sem.at[1])
        flocal.start()
        xsends = [xcopy(floc_ref, fcols(c), 64, recv_x.at[0], xr), xcopy(floc_ref, fcols(c), 65, recv_x.at[1], xl)]
        for cp in xsends:
            cp.start()

    sends = []

    def remote(src, dst, rsem, d, si=0):
        return pltpu.make_async_remote_copy(
            src_ref=src, dst_ref=dst, send_sem=send_sem.at[si], recv_sem=rsem,
            device_id=(d, c), device_id_type=MESH,
        )

    def send(src, dst, rsem, d):
        cp = remote(src, dst, rsem, d, len(sends))
        cp.start()
        sends.append(cp)

    def wait(ref, rsem):
        remote(ref, ref, rsem, partner).wait_recv()

    def multiply(yy):
        if fused:
            plane = (yy + NY) % NY
            cols = pl.ds(pl.multiple_of(plane * (NZ * NC * nb), nb), NZ * NC * nb)
            vec = G[pl.ds(plane * NZ, NZ)].reshape(NZ * NC * nb, w)
            acc[...] += jnp.dot(
                f_ref[:, cols] * m_ref[:, cols], vec,
                precision=lax.Precision.HIGHEST, preferred_element_type=jnp.float32,
            )

    offs = [0, -1, 1, -2, 2, -3, 3, -4]
    to_right = {0, -1, -2, -3}

    def idx(off):
        return offs.index(-4 if off == 4 else off)

    def middle():
        if mode == "first":
            del xsends[2:]
            xcopy(floc_ref, fcols(c - 1), 0, recv_x.at[0], xr).wait_recv()
            xsends.append(xcopy(fcols(c - 1, 0, hcol), fcols(c - 1, 0, hcol), 66, recv_x.at[2], xr))
            xsends[-1].start()
            xcopy(floc_ref, fcols(c + 1), 0, recv_x.at[1], xr).wait_recv()
            xsends.append(xcopy(fcols(c + 1, hcol, hcol), fcols(c + 1, hcol, hcol), 67, recv_x.at[3], xl))
            xsends[-1].start()

    def finish(kk):
        local.wait()
        for d in (0, -1, 1, 2):
            for i, off in enumerate(offs):
                wait(blk(y + d, z + off, 1 - kk), recv_c.at[d % NY, i])
        if mode == "first":
            flocal.wait()
            multiply(c)
            multiply(c - 1)
            multiply(c + 1)
            xcopy(fcols(c + 2, 0, hcol), fcols(c + 2, 0, hcol), 0, recv_x.at[2], xr).wait_recv()
            xcopy(fcols(c + 2, hcol, hcol), fcols(c + 2, hcol, hcol), 0, recv_x.at[3], xr).wait_recv()
            multiply(c + 2)
            for cp in xsends:
                cp.wait_send()
        else:
            for d in (0, -1, 1, 2):
                multiply(y + d)
        for cp in sends:
            cp.wait_send()

    def recv_of(zsrc):
        return recv_z.at[(zsrc + NZ) % NZ]

    def core0():
        kk = 0
        sends.clear()

        def spread(off):
            i = idx(off)
            ref = x_ref if off == 0 else blk(y, z + off, kk)
            send(ref, blk(y, z + off, kk), recv_y.at[0, i], yr)
            send(ref, blk(y, z + off, kk), recv_y.at[1, i], yl)
            send(ref, blk(y, z + off, kk), recv_c.at[0, i], partner)

        for s in range(4):
            if s >= 1:
                wait(blk(y, z - s, kk), recv_of(z - s))
            send(x_ref if s == 0 else blk(y, z - s, kk), blk(y, z - s, kk), recv_of(z - s), zr)
            if s < 3:
                if s >= 1:
                    wait(blk(y, z + s, kk), recv_of(z + s))
                send(x_ref if s == 0 else blk(y, z + s, kk), blk(y, z + s, kk), recv_of(z + s), zl)
            if s == 0:
                spread(0)
            else:
                spread(-s)
                if s < 3:
                    spread(s)
        wait(blk(y, z - 4, kk), recv_of(z - 4))
        spread(-4)
        wait(blk(y, z + 3, kk), recv_of(z + 3))
        spread(3)

        for i, off in enumerate(offs):
            wait(blk(y - 1, z + off, kk), recv_y.at[0, i])
            if off in to_right:
                send(blk(y - 1, z + off, kk), blk(y - 1, z + off, kk), recv_y.at[2, i], yr)
            send(blk(y - 1, z + off, kk), blk(y - 1, z + off, kk), recv_c.at[3, i], partner)
            wait(blk(y + 1, z + off, kk), recv_y.at[1, i])
            if off not in to_right:
                send(blk(y + 1, z + off, kk), blk(y + 1, z + off, kk), recv_y.at[3, i], yl)
            send(blk(y + 1, z + off, kk), blk(y + 1, z + off, kk), recv_c.at[1, i], partner)
        middle()
        for i, off in enumerate(offs):
            wait(blk(y + 2, z + off, kk), recv_y.at[2 if off in to_right else 3, i])
            send(blk(y + 2, z + off, kk), blk(y + 2, z + off, kk), recv_c.at[2, i], partner)
        finish(kk)

    def core1():
        kk = 1
        sends.clear()
        own = blk(y, z, kk)
        send(x_ref, own, recv_y.at[0, 0], yr)
        send(x_ref, own, recv_y.at[1, 0], yl)
        send(x_ref, own, recv_c.at[0, 0], partner)
        planes = (0, -1, 1, 2)
        steps = {d: ((4, 3) if d % 2 == 0 else (3, 4)) for d in planes}

        def ring_send(d, s, sign):
            off = -s if sign > 0 else s
            ref = (x_ref if d == 0 else blk(y + d, z, kk)) if s == 0 else blk(y + d, z + off, kk)
            send(ref, blk(y + d, z + off, kk), recv_w.at[d % NY, (z + off + NZ) % NZ], zr if sign > 0 else zl)

        def ring_recv(d, s, sign):
            off = -s if sign > 0 else s
            wait(blk(y + d, z + off, kk), recv_w.at[d % NY, (z + off + NZ) % NZ])
            send(blk(y + d, z + off, kk), blk(y + d, z + off, kk), recv_c.at[d % NY, idx(off)], partner)

        for d in planes:
            if d == -1:
                wait(blk(y - 1, z, kk), recv_y.at[0, 0])
                send(blk(y - 1, z, kk), blk(y - 1, z, kk), recv_y.at[2, 0], yr)
                send(blk(y - 1, z, kk), blk(y - 1, z, kk), recv_c.at[3, 0], partner)
            elif d == 1:
                wait(blk(y + 1, z, kk), recv_y.at[1, 0])
                send(blk(y + 1, z, kk), blk(y + 1, z, kk), recv_c.at[1, 0], partner)
            elif d == 2:
                wait(blk(y + 2, z, kk), recv_y.at[2, 0])
                send(blk(y + 2, z, kk), blk(y + 2, z, kk), recv_c.at[2, 0], partner)
            ring_send(d, 0, 1)
            ring_send(d, 0, -1)
        for s in range(1, 5):
            for d in planes:
                nr, nl = steps[d]
                if s <= nr:
                    ring_recv(d, s, 1)
                    if s < nr:
                        ring_send(d, s, 1)
                if s <= nl:
                    ring_recv(d, s, -1)
                    if s < nl:
                        ring_send(d, s, -1)
            if s == 2:
                middle()
        finish(kk)

    @pl.when(k == 0)
    def _():
        core0()

    @pl.when(k == 1)
    def _():
        core1()

    if mode == "first":
        fout = pltpu.make_async_copy(f_ref, fout_ref, local_sem.at[1])
        fout.start()
        fout.wait()

    out_ref[...] = acc[...]


def _sems():
    return [
        pltpu.SemaphoreType.DMA((2,)),
        pltpu.SemaphoreType.DMA((68,)),
        pltpu.SemaphoreType.DMA((NZ,)),
        pltpu.SemaphoreType.DMA((4, NZ)),
        pltpu.SemaphoreType.DMA((NY, NZ)),
        pltpu.SemaphoreType.DMA((NY, NZ)),
    ]


def _specs(n):
    return [pl.BlockSpec(memory_space=pltpu.VMEM)] * n


def first_product(floc, mask_row, x, cid):
    nb, w = x.shape
    rows = floc.shape[0]
    ncol = floc.shape[1] * 4
    return pl.pallas_call(
        functools.partial(gather_kernel, mode="first"),
        out_shape=(jax.ShapeDtypeStruct((rows, w), jnp.float32), jax.ShapeDtypeStruct((rows, ncol), floc.dtype)),
        in_specs=_specs(3),
        out_specs=(pl.BlockSpec(memory_space=pltpu.VMEM), pl.BlockSpec(memory_space=pl.ANY)),
        scratch_shapes=[pltpu.VMEM((NY * NZ, NC, nb, w), x.dtype), pltpu.VMEM((rows, ncol), floc.dtype),
                        pltpu.VMEM((rows, w), jnp.float32)]
        + _sems() + [pltpu.SemaphoreType.DMA((4,))],
        compiler_params=pltpu.CompilerParams(collective_id=cid, has_side_effects=True),
        cost_estimate=pl.CostEstimate(
            flops=2 * rows * ncol * w, transcendentals=0, bytes_accessed=(2 * rows * ncol + 2 * x.size * 64) * 4,
        ),
    )(x, floc, mask_row)


def gather_product(matrix, mask_row, x, cid):
    nb, w = x.shape
    shape = (NY * NZ, NC, nb, w)
    return pl.pallas_call(
        functools.partial(gather_kernel, mode="fused"),
        out_shape=jax.ShapeDtypeStruct((matrix.shape[0], w), jnp.float32),
        in_specs=_specs(3),
        out_specs=pl.BlockSpec(memory_space=pltpu.VMEM),
        scratch_shapes=[pltpu.VMEM(shape, x.dtype), pltpu.VMEM((matrix.shape[0], w), jnp.float32)]
        + _sems(),
        compiler_params=pltpu.CompilerParams(collective_id=cid, has_side_effects=True),
        cost_estimate=pl.CostEstimate(
            flops=2 * matrix.shape[0] * matrix.shape[1] * w, transcendentals=0,
            bytes_accessed=(matrix.size + 2 * x.size * 64) * 4,
        ),
    )(x, matrix, mask_row)


def body(factor, rhs, parent, bounds, slot, structure):
    level_mine, same, link = row_masks(parent, bounds, slot, structure, lax.axis_index("row"))
    same_row = jnp.repeat(same.astype(jnp.float32), B)[None, :]
    link_row = jnp.repeat(link.astype(jnp.float32), B)[None, :]

    rows0 = level_mine == 0
    first_prod, full_rows = first_product(factor, same_row, rhs, 0)
    solved = jnp.where(rows0, first_prod, 0.0)
    result = solved
    accum = gather_product(full_rows, link_row, solved, 1)
    for section in (1, 2):
        rows = level_mine == section
        solved = jnp.where(rows, gather_product(full_rows, same_row, rhs - accum, 2 * section), 0.0)
        result = result + solved
        if section < 2:
            accum = accum + gather_product(full_rows, link_row, solved, 2 * section + 1)
    return result


def solution(mesh):
    in_specs = (P("row", "col"), P("row", "col"), P(), P(), P(), P())
    out_specs = P("row", "col")
    return jax.shard_map(body, mesh=mesh, in_specs=in_specs, out_specs=out_specs, check_vma=False)
```

```python
import functools

import jax
import jax.numpy as jnp
from jax import lax
from jax.experimental import pallas as pl
from jax.experimental.pallas import tpu as pltpu
from jax.sharding import PartitionSpec as P

B = 128
RB = 1
MESH = pl.DeviceIdType.MESH
NY, NZ, NC = 4, 8, 2


def row_masks(parent, bounds, slot, structure, r):
    count = slot.shape[0]
    ar = jnp.arange(count, dtype=jnp.int32)
    nodes = jnp.arange(parent.shape[0], dtype=jnp.int32)
    logical = jnp.sum(jnp.where(slot[:, None] == ar[None, :], ar[:, None], 0), axis=0)
    node = jnp.sum((logical[:, None] >= bounds[None, 1:7]).astype(jnp.int32), axis=1)
    mine = ar == r
    node_r = jnp.sum(jnp.where(mine, node, 0))
    logical_r = jnp.sum(jnp.where(mine, logical, 0))
    level_r = (node_r >= 4).astype(jnp.int32) + (node_r >= 6).astype(jnp.int32)
    hot = node[:, None] == nodes[None, :]
    par = jnp.sum(jnp.where(hot, parent[None, :], 0), axis=1)
    grand = jnp.sum(jnp.where(par[:, None] == nodes[None, :], parent[None, :], 0), axis=1)
    ancestor = ((par == node_r) | (grand == node_r)) & (node != node_r)
    column = jnp.sum(jnp.where(ar[None, :] == logical_r, structure, 0), axis=1)
    listed = jnp.sum(jnp.where(hot, column[None, :], 0), axis=1) == 1
    return level_r, node == node_r, ancestor & listed


def gather_kernel(*refs, mode):
    fused = True
    if mode == "first":
        x_ref, floc_ref, m_ref, out_ref, fout_ref, G, f_ref, acc, local_sem, send_sem, recv_z, recv_y, recv_c, \
            recv_x = refs
    else:
        x_ref, f_ref, m_ref, out_ref, G, acc, local_sem, send_sem, recv_z, recv_y, recv_c = refs
    nb, w = x_ref.shape
    r = lax.axis_index("row")
    c = lax.axis_index("col")
    y = r // (NZ * NC)
    z = (r // NC) % NZ
    k = r % NC

    def dev(yy, zz, kk):
        return (((yy + NY) % NY) * NZ + (zz + NZ) % NZ) * NC + kk

    def blk(yy, zz, kk):
        return G.at[((yy + NY) % NY) * NZ + (zz + NZ) % NZ, kk]

    def chunk(kk, yy, lo=0, n=NZ):
        return G.at[pl.ds(((yy + NY) % NY) * NZ + lo, n), kk]

    zr, zl = dev(y, z + 1, k), dev(y, z - 1, k)
    yr, yl = dev(y + 1, z, k), dev(y - 1, z, k)
    partner = dev(y, z, 1 - k)

    barrier = pltpu.get_barrier_semaphore()
    peers = [(d, c) for d in (zr, zl, dev(y, z + 2, k), dev(y, z - 2, k), yr, yl, partner)]
    nx = 4
    xr, xl = (r, (c + 1) % nx), (r, (c + nx - 1) % nx)
    if mode == "first":
        peers += [xr, xl]
    for d in peers:
        pl.semaphore_signal(barrier, inc=1, device_id=d, device_id_type=MESH)
    pl.semaphore_wait(barrier, len(peers))

    local = pltpu.make_async_copy(x_ref, blk(y, z, k), local_sem.at[0])
    local.start()
    acc[...] = jnp.zeros_like(acc)

    if mode == "first":
        wcol = floc_ref.shape[1]
        hcol = wcol // 2

        def fcols(cc, lo=0, n=wcol):
            return f_ref.at[:, pl.ds(pl.multiple_of(((cc + nx) % nx) * wcol + lo, 128), n)]

        def xcopy(src, dst, si, rsem, d):
            return pltpu.make_async_remote_copy(
                src_ref=src, dst_ref=dst, send_sem=send_sem.at[si], recv_sem=rsem,
                device_id=d, device_id_type=MESH,
            )

        flocal = pltpu.make_async_copy(floc_ref, fcols(c), local_sem.at[1])
        flocal.start()
        xsends = [xcopy(floc_ref, fcols(c), 64, recv_x.at[0], xr), xcopy(floc_ref, fcols(c), 65, recv_x.at[1], xl)]
        for cp in xsends:
            cp.start()

    sends = []

    def remote(src, dst, rsem, d, si=0):
        return pltpu.make_async_remote_copy(
            src_ref=src, dst_ref=dst, send_sem=send_sem.at[si], recv_sem=rsem,
            device_id=(d, c), device_id_type=MESH,
        )

    def send(src, dst, rsem, d):
        cp = remote(src, dst, rsem, d, len(sends))
        cp.start()
        sends.append(cp)

    def wait(ref, rsem):
        remote(ref, ref, rsem, partner).wait_recv()

    def multiply(yy):
        if fused:
            plane = (yy + NY) % NY
            cols = pl.ds(pl.multiple_of(plane * (NZ * NC * nb), nb), NZ * NC * nb)
            vec = G[pl.ds(plane * NZ, NZ)].reshape(NZ * NC * nb, w)
            acc[...] += jnp.dot(
                f_ref[:, cols] * m_ref[:, cols], vec,
                precision=lax.Precision.HIGHEST, preferred_element_type=jnp.float32,
            )

    offs = [0, -1, 1, -2, 2, -3, 3, -4]
    to_right = {0, -1, -2, -3}

    def spread(off):
        i = offs.index(off)
        ref = x_ref if off == 0 else blk(y, z + off, k)
        send(ref, blk(y, z + off, k), recv_y.at[0, i], yr)
        send(ref, blk(y, z + off, k), recv_y.at[1, i], yl)
        send(ref, blk(y, z + off, k), recv_c.at[0, i], partner)

    def recv_of(zsrc):
        return recv_z.at[(zsrc + NZ) % NZ]

    for d in (1, 2, -1, -2):
        send(x_ref, blk(y, z, k), recv_of(z), dev(y, z + d, k))
    spread(0)
    wait(blk(y, z - 2, k), recv_of(z - 2))
    send(blk(y, z - 2, k), blk(y, z - 2, k), recv_of(z - 2), dev(y, z + 1, k))
    send(blk(y, z - 2, k), blk(y, z - 2, k), recv_of(z - 2), dev(y, z + 2, k))
    wait(blk(y, z + 2, k), recv_of(z + 2))
    send(blk(y, z + 2, k), blk(y, z + 2, k), recv_of(z + 2), dev(y, z - 1, k))
    for off in (-1, 1):
        wait(blk(y, z + off, k), recv_of(z + off))
        spread(off)
    spread(-2)
    spread(2)
    for off in (-3, 3, -4):
        wait(blk(y, z + off, k), recv_of(z + off))
        spread(off)
    local.wait()

    for i, off in enumerate(offs):
        wait(blk(y - 1, z + off, k), recv_y.at[0, i])
        if off in to_right:
            send(blk(y - 1, z + off, k), blk(y - 1, z + off, k), recv_y.at[2, i], yr)
        send(blk(y - 1, z + off, k), blk(y - 1, z + off, k), recv_c.at[3, i], partner)
        wait(blk(y + 1, z + off, k), recv_y.at[1, i])
        if off not in to_right:
            send(blk(y + 1, z + off, k), blk(y + 1, z + off, k), recv_y.at[3, i], yl)
        send(blk(y + 1, z + off, k), blk(y + 1, z + off, k), recv_c.at[1, i], partner)

    def partner_plane(d):
        for i, off in enumerate(offs):
            wait(blk(y + d, z + off, 1 - k), recv_c.at[d % NY, i])
        multiply(y + d)

    def partner_wait(d):
        for i, off in enumerate(offs):
            wait(blk(y + d, z + off, 1 - k), recv_c.at[d % NY, i])

    if mode == "first":
        xcopy(floc_ref, fcols(c - 1), 0, recv_x.at[0], xr).wait_recv()
        xsends.append(xcopy(fcols(c - 1, 0, hcol), fcols(c - 1, 0, hcol), 66, recv_x.at[2], xr))
        xsends[-1].start()
        xcopy(floc_ref, fcols(c + 1), 0, recv_x.at[1], xr).wait_recv()
        xsends.append(xcopy(fcols(c + 1, hcol, hcol), fcols(c + 1, hcol, hcol), 67, recv_x.at[3], xl))
        xsends[-1].start()
    else:
        partner_wait(0)
        multiply(y)
    for i, off in enumerate(offs):
        wait(blk(y + 2, z + off, k), recv_y.at[2 if off in to_right else 3, i])
        send(blk(y + 2, z + off, k), blk(y + 2, z + off, k), recv_c.at[2, i], partner)
    if mode == "first":
        for d in (0, -1, 1, 2):
            partner_wait(d)
        flocal.wait()
        multiply(c)
        multiply(c - 1)
        multiply(c + 1)
        xcopy(fcols(c + 2, 0, hcol), fcols(c + 2, 0, hcol), 0, recv_x.at[2], xr).wait_recv()
        xcopy(fcols(c + 2, hcol, hcol), fcols(c + 2, hcol, hcol), 0, recv_x.at[3], xr).wait_recv()
        multiply(c + 2)
        for cp in xsends:
            cp.wait_send()
        fout = pltpu.make_async_copy(f_ref, fout_ref, local_sem.at[1])
        fout.start()
        fout.wait()
    else:
        for d in (-1, 1, 2):
            partner_wait(d)
            multiply(y + d)

    for cp in sends:
        cp.wait_send()
    out_ref[...] = acc[...]


def split_kernel(x_ref, fo_ref, fp_ref, mo_ref, mp_ref, oo_ref, op_ref, G, acc_o, acc_p, local_sem, send_sem,
                 recv_z, recv_y):
    nb, w = x_ref.shape
    r = lax.axis_index("row")
    c = lax.axis_index("col")
    y = r // (NZ * NC)
    z = (r // NC) % NZ
    k = r % NC

    def dev(yy, zz):
        return (((yy + NY) % NY) * NZ + (zz + NZ) % NZ) * NC + k

    def blk(yy, zz):
        return G.at[((yy + NY) % NY) * NZ + (zz + NZ) % NZ]

    zr, zl, yr, yl = dev(y, z + 1), dev(y, z - 1), dev(y + 1, z), dev(y - 1, z)
    barrier = pltpu.get_barrier_semaphore()
    for d in (zr, zl, yr, yl):
        pl.semaphore_signal(barrier, inc=1, device_id=(d, c), device_id_type=MESH)
    pl.semaphore_wait(barrier, 4)

    local = pltpu.make_async_copy(x_ref, blk(y, z), local_sem.at[0])
    local.start()
    sends = []

    def remote(src, dst, rsem, d, si=0):
        return pltpu.make_async_remote_copy(
            src_ref=src, dst_ref=dst, send_sem=send_sem.at[si], recv_sem=rsem,
            device_id=(d, c), device_id_type=MESH,
        )

    def send(src, dst, rsem, d):
        cp = remote(src, dst, rsem, d, len(sends))
        cp.start()
        sends.append(cp)

    def wait(ref, rsem):
        remote(ref, ref, rsem, zr).wait_recv()

    def recv_of(zsrc):
        return recv_z.at[(zsrc + NZ) % NZ]

    offs = [0, -1, 1, -2, 2, -3, 3, -4]
    to_right = {0, -1, -2, -3}

    def spread(off):
        i = offs.index(off)
        ref = x_ref if off == 0 else blk(y, z + off)
        send(ref, blk(y, z + off), recv_y.at[0, i], yr)
        send(ref, blk(y, z + off), recv_y.at[1, i], yl)

    for s in range(4):
        if s >= 1:
            wait(blk(y, z - s), recv_of(z - s))
        send(x_ref if s == 0 else blk(y, z - s), blk(y, z - s), recv_of(z - s), zr)
        if s < 3:
            if s >= 1:
                wait(blk(y, z + s), recv_of(z + s))
            send(x_ref if s == 0 else blk(y, z + s), blk(y, z + s), recv_of(z + s), zl)
        if s == 0:
            spread(0)
        else:
            spread(-s)
            if s < 3:
                spread(s)
    wait(blk(y, z - 4), recv_of(z - 4))
    spread(-4)
    wait(blk(y, z + 3), recv_of(z + 3))
    spread(3)
    for i, off in enumerate(offs):
        wait(blk(y - 1, z + off), recv_y.at[0, i])
        if off in to_right:
            send(blk(y - 1, z + off), blk(y - 1, z + off), recv_y.at[2, i], yr)
        wait(blk(y + 1, z + off), recv_y.at[1, i])
        if off not in to_right:
            send(blk(y + 1, z + off), blk(y + 1, z + off), recv_y.at[3, i], yl)
    local.wait()
    acc_o[...] = jnp.zeros_like(acc_o)
    acc_p[...] = jnp.zeros_like(acc_p)

    def multiply(yy):
        plane = (yy + NY) % NY
        cols = pl.ds(pl.multiple_of(plane * (NZ * nb), nb), NZ * nb)
        vec = G[pl.ds(plane * NZ, NZ)].reshape(NZ * nb, w)
        acc_o[...] += jnp.dot(fo_ref[:, cols] * mo_ref[:, cols], vec,
                              precision=lax.Precision.HIGHEST, preferred_element_type=jnp.float32)
        acc_p[...] += jnp.dot(fp_ref[:, cols] * mp_ref[:, cols], vec,
                              precision=lax.Precision.HIGHEST, preferred_element_type=jnp.float32)

    multiply(y)
    multiply(y - 1)
    multiply(y + 1)
    for i, off in enumerate(offs):
        wait(blk(y + 2, z + off), recv_y.at[2 if off in to_right else 3, i])
    multiply(y + 2)
    for cp in sends:
        cp.wait_send()
    oo_ref[...] = acc_o[...]
    op_ref[...] = acc_p[...]


def split_product(fo, fp, mo, mp, x, cid):
    nb, w = x.shape
    rows = fo.shape[0]
    out = jax.ShapeDtypeStruct((rows, w), jnp.float32)
    return pl.pallas_call(
        split_kernel,
        out_shape=(out, out),
        in_specs=_specs(5),
        out_specs=(pl.BlockSpec(memory_space=pltpu.VMEM), pl.BlockSpec(memory_space=pltpu.VMEM)),
        scratch_shapes=[pltpu.VMEM((NY * NZ, nb, w), x.dtype), pltpu.VMEM((rows, w), jnp.float32),
                        pltpu.VMEM((rows, w), jnp.float32), pltpu.SemaphoreType.DMA((1,)),
                        pltpu.SemaphoreType.DMA((40,)), pltpu.SemaphoreType.DMA((NZ,)),
                        pltpu.SemaphoreType.DMA((4, NZ))],
        compiler_params=pltpu.CompilerParams(collective_id=cid, has_side_effects=True),
        cost_estimate=pl.CostEstimate(
            flops=4 * rows * fo.shape[1] * w, transcendentals=0,
            bytes_accessed=(2 * fo.size + x.size * 64) * 4,
        ),
    )(x, fo, fp, mo, mp)


def _sems():
    return [
        pltpu.SemaphoreType.DMA((2,)),
        pltpu.SemaphoreType.DMA((68,)),
        pltpu.SemaphoreType.DMA((NZ,)),
        pltpu.SemaphoreType.DMA((4, NZ)),
        pltpu.SemaphoreType.DMA((NY, NZ)),
    ]


def _specs(n):
    return [pl.BlockSpec(memory_space=pltpu.VMEM)] * n


def first_product(floc, mask_row, x, cid):
    nb, w = x.shape
    rows = floc.shape[0]
    ncol = floc.shape[1] * 4
    return pl.pallas_call(
        functools.partial(gather_kernel, mode="first"),
        out_shape=(jax.ShapeDtypeStruct((rows, w), jnp.float32), jax.ShapeDtypeStruct((rows, ncol), floc.dtype)),
        in_specs=_specs(3),
        out_specs=(pl.BlockSpec(memory_space=pltpu.VMEM), pl.BlockSpec(memory_space=pl.ANY)),
        scratch_shapes=[pltpu.VMEM((NY * NZ, NC, nb, w), x.dtype), pltpu.VMEM((rows, ncol), floc.dtype),
                        pltpu.VMEM((rows, w), jnp.float32)]
        + _sems() + [pltpu.SemaphoreType.DMA((4,))],
        compiler_params=pltpu.CompilerParams(collective_id=cid, has_side_effects=True),
        cost_estimate=pl.CostEstimate(
            flops=2 * rows * ncol * w, transcendentals=0, bytes_accessed=(2 * rows * ncol + 2 * x.size * 64) * 4,
        ),
    )(x, floc, mask_row)


def gather_product(matrix, mask_row, x, cid):
    nb, w = x.shape
    shape = (NY * NZ, NC, nb, w)
    return pl.pallas_call(
        functools.partial(gather_kernel, mode="fused"),
        out_shape=jax.ShapeDtypeStruct((matrix.shape[0], w), jnp.float32),
        in_specs=_specs(3),
        out_specs=pl.BlockSpec(memory_space=pltpu.VMEM),
        scratch_shapes=[pltpu.VMEM(shape, x.dtype), pltpu.VMEM((matrix.shape[0], w), jnp.float32)]
        + _sems(),
        compiler_params=pltpu.CompilerParams(collective_id=cid, has_side_effects=True),
        cost_estimate=pl.CostEstimate(
            flops=2 * matrix.shape[0] * matrix.shape[1] * w, transcendentals=0,
            bytes_accessed=(matrix.size + 2 * x.size * 64) * 4,
        ),
    )(x, matrix, mask_row)


def body(factor, rhs, parent, bounds, slot, structure):
    r = lax.axis_index("row")
    level_mine, same, link = row_masks(parent, bounds, slot, structure, r)
    _, same_p, link_p = row_masks(parent, bounds, slot, structure, r + 1 - 2 * (r % NC))
    same_row = jnp.repeat(same.astype(jnp.float32), B)[None, :]
    link_row = jnp.repeat(link.astype(jnp.float32), B)[None, :]

    rows0 = level_mine == 0
    first_prod, full_rows = first_product(factor, same_row, rhs, 0)
    solved = jnp.where(rows0, first_prod, 0.0)
    result = solved

    k = r % NC
    pairs = [(i, i + 1 - 2 * (i % NC)) for i in range(NY * NZ * NC)]

    def classes(a):
        return a.reshape(a.shape[0], NY * NZ, NC, B)

    def pick(a, kk):
        return lax.dynamic_index_in_dim(classes(a), kk, axis=2, keepdims=False).reshape(a.shape[0], -1)

    f_own = pick(full_rows, k)
    f_part = lax.ppermute(pick(full_rows, 1 - k), "row", pairs)
    masks = {
        "same": (pick(same_row, k), pick(jnp.repeat(same_p.astype(jnp.float32), B)[None, :], k)),
        "link": (pick(link_row, k), pick(jnp.repeat(link_p.astype(jnp.float32), B)[None, :], k)),
    }

    def product(kind, x, cid):
        own, part = split_product(f_own, f_part, masks[kind][0], masks[kind][1], x, cid)
        return own + lax.ppermute(part, "row", pairs)

    accum = product("link", solved, 1)
    for section in (1, 2):
        rows = level_mine == section
        solved = jnp.where(rows, product("same", rhs - accum, 2 * section), 0.0)
        result = result + solved
        if section < 2:
            accum = accum + product("link", solved, 2 * section + 1)
    return result


def solution(mesh):
    in_specs = (P("row", "col"), P("row", "col"), P(), P(), P(), P())
    out_specs = P("row", "col")
    return jax.shard_map(body, mesh=mesh, in_specs=in_specs, out_specs=out_specs, check_vma=False)
```

```python
import functools

import jax
import jax.numpy as jnp
from jax import lax
from jax.experimental import pallas as pl
from jax.experimental.pallas import tpu as pltpu
from jax.sharding import PartitionSpec as P

B = 128
RB = 1
MESH = pl.DeviceIdType.MESH
NY, NZ, NC = 4, 8, 2


def row_masks(parent, bounds, slot, structure, r):
    count = slot.shape[0]
    ar = jnp.arange(count, dtype=jnp.int32)
    nodes = jnp.arange(parent.shape[0], dtype=jnp.int32)
    logical = jnp.sum(jnp.where(slot[:, None] == ar[None, :], ar[:, None], 0), axis=0)
    node = jnp.sum((logical[:, None] >= bounds[None, 1:7]).astype(jnp.int32), axis=1)
    mine = ar == r
    node_r = jnp.sum(jnp.where(mine, node, 0))
    logical_r = jnp.sum(jnp.where(mine, logical, 0))
    level_r = (node_r >= 4).astype(jnp.int32) + (node_r >= 6).astype(jnp.int32)
    hot = node[:, None] == nodes[None, :]
    par = jnp.sum(jnp.where(hot, parent[None, :], 0), axis=1)
    grand = jnp.sum(jnp.where(par[:, None] == nodes[None, :], parent[None, :], 0), axis=1)
    ancestor = ((par == node_r) | (grand == node_r)) & (node != node_r)
    column = jnp.sum(jnp.where(ar[None, :] == logical_r, structure, 0), axis=1)
    listed = jnp.sum(jnp.where(hot, column[None, :], 0), axis=1) == 1
    return level_r, node == node_r, ancestor & listed


def gather_kernel(*refs, mode, epilogue=None, n_extra=0, n_out=1):
    fused = True
    if mode == "first":
        x_ref, floc_ref, m_ref, out_ref, fout_ref, G, f_ref, acc, local_sem, send_sem, recv_z, recv_y, recv_c, \
            recv_x = refs
    else:
        x_ref, f_ref, m_ref = refs[:3]
        extra_refs = refs[3:3 + n_extra]
        out_refs = refs[3 + n_extra:3 + n_extra + n_out]
        G, acc, local_sem, send_sem, recv_z, recv_y, recv_c = refs[3 + n_extra + n_out:]
    nb, w = x_ref.shape
    r = lax.axis_index("row")
    c = lax.axis_index("col")
    y = r // (NZ * NC)
    z = (r // NC) % NZ
    k = r % NC

    def dev(yy, zz, kk):
        return (((yy + NY) % NY) * NZ + (zz + NZ) % NZ) * NC + kk

    def blk(yy, zz, kk):
        return G.at[((yy + NY) % NY) * NZ + (zz + NZ) % NZ, kk]

    def chunk(kk, yy, lo=0, n=NZ):
        return G.at[pl.ds(((yy + NY) % NY) * NZ + lo, n), kk]

    zr, zl = dev(y, z + 1, k), dev(y, z - 1, k)
    yr, yl = dev(y + 1, z, k), dev(y - 1, z, k)
    partner = dev(y, z, 1 - k)

    barrier = pltpu.get_barrier_semaphore()
    peers = [(d, c) for d in (zr, zl, dev(y, z + 2, k), dev(y, z - 2, k), yr, yl, partner)]
    nx = 4
    xr, xl = (r, (c + 1) % nx), (r, (c + nx - 1) % nx)
    if mode == "first":
        peers += [xr, xl]
    for d in peers:
        pl.semaphore_signal(barrier, inc=1, device_id=d, device_id_type=MESH)
    pl.semaphore_wait(barrier, len(peers))

    local = pltpu.make_async_copy(x_ref, blk(y, z, k), local_sem.at[0])
    local.start()
    acc[...] = jnp.zeros_like(acc)

    if mode == "first":
        wcol = floc_ref.shape[1]
        hcol = wcol // 2

        def fcols(cc, lo=0, n=wcol):
            return f_ref.at[:, pl.ds(pl.multiple_of(((cc + nx) % nx) * wcol + lo, 128), n)]

        def xcopy(src, dst, si, rsem, d):
            return pltpu.make_async_remote_copy(
                src_ref=src, dst_ref=dst, send_sem=send_sem.at[si], recv_sem=rsem,
                device_id=d, device_id_type=MESH,
            )

        flocal = pltpu.make_async_copy(floc_ref, fcols(c), local_sem.at[1])
        flocal.start()
        xsends = [xcopy(floc_ref, fcols(c), 64, recv_x.at[0], xr), xcopy(floc_ref, fcols(c), 65, recv_x.at[1], xl)]
        for cp in xsends:
            cp.start()

    sends = []

    def remote(src, dst, rsem, d, si=0):
        return pltpu.make_async_remote_copy(
            src_ref=src, dst_ref=dst, send_sem=send_sem.at[si], recv_sem=rsem,
            device_id=(d, c), device_id_type=MESH,
        )

    def send(src, dst, rsem, d):
        cp = remote(src, dst, rsem, d, len(sends))
        cp.start()
        sends.append(cp)

    def wait(ref, rsem):
        remote(ref, ref, rsem, partner).wait_recv()

    def multiply(yy):
        if fused:
            plane = (yy + NY) % NY
            cols = pl.ds(pl.multiple_of(plane * (NZ * NC * nb), nb), NZ * NC * nb)
            vec = G[pl.ds(plane * NZ, NZ)].reshape(NZ * NC * nb, w)
            acc[...] += jnp.dot(
                f_ref[:, cols] * m_ref[:, cols], vec,
                precision=lax.Precision.HIGHEST, preferred_element_type=jnp.float32,
            )

    offs = [0, -1, 1, -2, 2, -3, 3, -4]
    to_right = {0, -1, -2, -3}

    def spread(off):
        i = offs.index(off)
        ref = x_ref if off == 0 else blk(y, z + off, k)
        send(ref, blk(y, z + off, k), recv_y.at[0, i], yr)
        send(ref, blk(y, z + off, k), recv_y.at[1, i], yl)
        send(ref, blk(y, z + off, k), recv_c.at[0, i], partner)

    def recv_of(zsrc):
        return recv_z.at[(zsrc + NZ) % NZ]

    for d in (1, 2, -1, -2):
        send(x_ref, blk(y, z, k), recv_of(z), dev(y, z + d, k))
    spread(0)
    wait(blk(y, z - 2, k), recv_of(z - 2))
    send(blk(y, z - 2, k), blk(y, z - 2, k), recv_of(z - 2), dev(y, z + 1, k))
    send(blk(y, z - 2, k), blk(y, z - 2, k), recv_of(z - 2), dev(y, z + 2, k))
    wait(blk(y, z + 2, k), recv_of(z + 2))
    send(blk(y, z + 2, k), blk(y, z + 2, k), recv_of(z + 2), dev(y, z - 1, k))
    for off in (-1, 1):
        wait(blk(y, z + off, k), recv_of(z + off))
        spread(off)
    spread(-2)
    spread(2)
    for off in (-3, 3, -4):
        wait(blk(y, z + off, k), recv_of(z + off))
        spread(off)
    local.wait()

    for i, off in enumerate(offs):
        wait(blk(y - 1, z + off, k), recv_y.at[0, i])
        if off in to_right:
            send(blk(y - 1, z + off, k), blk(y - 1, z + off, k), recv_y.at[2, i], yr)
        send(blk(y - 1, z + off, k), blk(y - 1, z + off, k), recv_c.at[3, i], partner)
        wait(blk(y + 1, z + off, k), recv_y.at[1, i])
        if off not in to_right:
            send(blk(y + 1, z + off, k), blk(y + 1, z + off, k), recv_y.at[3, i], yl)
        send(blk(y + 1, z + off, k), blk(y + 1, z + off, k), recv_c.at[1, i], partner)

    def partner_plane(d):
        for i, off in enumerate(offs):
            wait(blk(y + d, z + off, 1 - k), recv_c.at[d % NY, i])
        multiply(y + d)

    def partner_wait(d):
        for i, off in enumerate(offs):
            wait(blk(y + d, z + off, 1 - k), recv_c.at[d % NY, i])

    if mode == "first":
        xcopy(floc_ref, fcols(c - 1), 0, recv_x.at[0], xr).wait_recv()
        xsends.append(xcopy(fcols(c - 1, 0, hcol), fcols(c - 1, 0, hcol), 66, recv_x.at[2], xr))
        xsends[-1].start()
        xcopy(floc_ref, fcols(c + 1), 0, recv_x.at[1], xr).wait_recv()
        xsends.append(xcopy(fcols(c + 1, hcol, hcol), fcols(c + 1, hcol, hcol), 67, recv_x.at[3], xl))
        xsends[-1].start()
    else:
        partner_wait(0)
        multiply(y)
    for i, off in enumerate(offs):
        wait(blk(y + 2, z + off, k), recv_y.at[2 if off in to_right else 3, i])
        send(blk(y + 2, z + off, k), blk(y + 2, z + off, k), recv_c.at[2, i], partner)
    if mode == "first":
        for d in (0, -1, 1, 2):
            partner_wait(d)
        flocal.wait()
        multiply(c)
        multiply(c - 1)
        multiply(c + 1)
        xcopy(fcols(c + 2, 0, hcol), fcols(c + 2, 0, hcol), 0, recv_x.at[2], xr).wait_recv()
        xcopy(fcols(c + 2, hcol, hcol), fcols(c + 2, hcol, hcol), 0, recv_x.at[3], xr).wait_recv()
        multiply(c + 2)
        for cp in xsends:
            cp.wait_send()
        fout = pltpu.make_async_copy(f_ref, fout_ref, local_sem.at[1])
        fout.start()
        fout.wait()
    else:
        for d in (-1, 1, 2):
            partner_wait(d)
            multiply(y + d)

    for cp in sends:
        cp.wait_send()
    if mode == "first":
        out_ref[...] = acc[...]
    else:
        for ref, value in zip(out_refs, epilogue(acc[...], *[e[...] for e in extra_refs])):
            ref[...] = value


def _sems():
    return [
        pltpu.SemaphoreType.DMA((2,)),
        pltpu.SemaphoreType.DMA((68,)),
        pltpu.SemaphoreType.DMA((NZ,)),
        pltpu.SemaphoreType.DMA((4, NZ)),
        pltpu.SemaphoreType.DMA((NY, NZ)),
    ]


def _specs(n):
    return [pl.BlockSpec(memory_space=pltpu.VMEM)] * n


def first_product(floc, mask_row, x, cid):
    nb, w = x.shape
    rows = floc.shape[0]
    ncol = floc.shape[1] * 4
    return pl.pallas_call(
        functools.partial(gather_kernel, mode="first"),
        out_shape=(jax.ShapeDtypeStruct((rows, w), jnp.float32), jax.ShapeDtypeStruct((rows, ncol), floc.dtype)),
        in_specs=_specs(3),
        out_specs=(pl.BlockSpec(memory_space=pltpu.VMEM), pl.BlockSpec(memory_space=pl.ANY)),
        scratch_shapes=[pltpu.VMEM((NY * NZ, NC, nb, w), x.dtype), pltpu.VMEM((rows, ncol), floc.dtype),
                        pltpu.VMEM((rows, w), jnp.float32)]
        + _sems() + [pltpu.SemaphoreType.DMA((4,))],
        compiler_params=pltpu.CompilerParams(collective_id=cid, has_side_effects=True),
        cost_estimate=pl.CostEstimate(
            flops=2 * rows * ncol * w, transcendentals=0, bytes_accessed=(2 * rows * ncol + 2 * x.size * 64) * 4,
        ),
    )(x, floc, mask_row)


def gather_product(matrix, mask_row, x, cid, extras, epilogue, n_out):
    nb, w = x.shape
    shape = (NY * NZ, NC, nb, w)
    out = jax.ShapeDtypeStruct((matrix.shape[0], w), jnp.float32)
    return pl.pallas_call(
        functools.partial(gather_kernel, mode="fused", epilogue=epilogue, n_extra=len(extras), n_out=n_out),
        out_shape=tuple([out] * n_out),
        in_specs=_specs(3 + len(extras)),
        out_specs=tuple(pl.BlockSpec(memory_space=pltpu.VMEM) for _ in range(n_out)),
        scratch_shapes=[pltpu.VMEM(shape, x.dtype), pltpu.VMEM((matrix.shape[0], w), jnp.float32)]
        + _sems(),
        compiler_params=pltpu.CompilerParams(collective_id=cid, has_side_effects=True),
        cost_estimate=pl.CostEstimate(
            flops=2 * matrix.shape[0] * matrix.shape[1] * w, transcendentals=0,
            bytes_accessed=(matrix.size + 2 * x.size * 64) * 4,
        ),
    )(x, matrix, mask_row, *extras)


def _link_epilogue(prod, accum, rhs):
    accum = accum + prod
    return accum, rhs - accum


def _diag_epilogue(prod, sel, result):
    solved = jnp.where(sel > 0.5, prod, 0.0)
    return solved, result + solved


def body(factor, rhs, parent, bounds, slot, structure):
    level_mine, same, link = row_masks(parent, bounds, slot, structure, lax.axis_index("row"))
    same_row = jnp.repeat(same.astype(jnp.float32), B)[None, :]
    link_row = jnp.repeat(link.astype(jnp.float32), B)[None, :]

    rows0 = level_mine == 0
    first_prod, full_rows = first_product(factor, same_row, rhs, 0)
    solved = jnp.where(rows0, first_prod, 0.0)
    result = solved
    accum = jnp.zeros(rhs.shape, jnp.float32)
    accum, vector = gather_product(full_rows, link_row, solved, 1, (accum, rhs), _link_epilogue, 2)
    for section in (1, 2):
        sel = jnp.full((1, rhs.shape[1]), (level_mine == section).astype(jnp.float32))
        solved, result = gather_product(full_rows, same_row, vector, 2 * section, (sel, result), _diag_epilogue, 2)
        if section < 2:
            accum, vector = gather_product(full_rows, link_row, solved, 2 * section + 1, (accum, rhs),
                                           _link_epilogue, 2)
    return result


def solution(mesh):
    in_specs = (P("row", "col"), P("row", "col"), P(), P(), P(), P())
    out_specs = P("row", "col")
    return jax.shard_map(body, mesh=mesh, in_specs=in_specs, out_specs=out_specs, check_vma=False)
```

```python
import functools

import jax
import jax.numpy as jnp
from jax import lax
from jax.experimental import pallas as pl
from jax.experimental.pallas import tpu as pltpu
from jax.sharding import PartitionSpec as P

B = 128
RB = 1
MESH = pl.DeviceIdType.MESH
NY, NZ, NC = 4, 8, 2


def row_masks(parent, bounds, slot, structure, r):
    count = slot.shape[0]
    ar = jnp.arange(count, dtype=jnp.int32)
    nodes = jnp.arange(parent.shape[0], dtype=jnp.int32)
    logical = jnp.sum(jnp.where(slot[:, None] == ar[None, :], ar[:, None], 0), axis=0)
    node = jnp.sum((logical[:, None] >= bounds[None, 1:7]).astype(jnp.int32), axis=1)
    mine = ar == r
    node_r = jnp.sum(jnp.where(mine, node, 0))
    logical_r = jnp.sum(jnp.where(mine, logical, 0))
    level_r = (node_r >= 4).astype(jnp.int32) + (node_r >= 6).astype(jnp.int32)
    hot = node[:, None] == nodes[None, :]
    par = jnp.sum(jnp.where(hot, parent[None, :], 0), axis=1)
    grand = jnp.sum(jnp.where(par[:, None] == nodes[None, :], parent[None, :], 0), axis=1)
    ancestor = ((par == node_r) | (grand == node_r)) & (node != node_r)
    column = jnp.sum(jnp.where(ar[None, :] == logical_r, structure, 0), axis=1)
    listed = jnp.sum(jnp.where(hot, column[None, :], 0), axis=1) == 1
    return level_r, node == node_r, ancestor & listed


def gather_kernel(*refs, mode, epilogue=None, n_extra=0, n_out=1):
    fused = True
    if mode == "first":
        x_ref, floc_ref, m_ref, sel_ref, out_ref, fout_ref, G, f_ref, acc, local_sem, send_sem, recv_z, recv_y, recv_c, \
            recv_x = refs
    else:
        x_ref, f_ref, m_ref = refs[:3]
        extra_refs = refs[3:3 + n_extra]
        out_refs = refs[3 + n_extra:3 + n_extra + n_out]
        G, acc, local_sem, send_sem, recv_z, recv_y, recv_c = refs[3 + n_extra + n_out:]
    nb, w = x_ref.shape
    r = lax.axis_index("row")
    c = lax.axis_index("col")
    y = r // (NZ * NC)
    z = (r // NC) % NZ
    k = r % NC

    def dev(yy, zz, kk):
        return (((yy + NY) % NY) * NZ + (zz + NZ) % NZ) * NC + kk

    def blk(yy, zz, kk):
        return G.at[((yy + NY) % NY) * NZ + (zz + NZ) % NZ, kk]

    def chunk(kk, yy, lo=0, n=NZ):
        return G.at[pl.ds(((yy + NY) % NY) * NZ + lo, n), kk]

    zr, zl = dev(y, z + 1, k), dev(y, z - 1, k)
    yr, yl = dev(y + 1, z, k), dev(y - 1, z, k)
    partner = dev(y, z, 1 - k)

    barrier = pltpu.get_barrier_semaphore()
    peers = [(d, c) for d in (zr, zl, dev(y, z + 2, k), dev(y, z - 2, k), yr, yl, partner)]
    nx = 4
    xr, xl = (r, (c + 1) % nx), (r, (c + nx - 1) % nx)
    if mode == "first":
        peers += [xr, xl]
    for d in peers:
        pl.semaphore_signal(barrier, inc=1, device_id=d, device_id_type=MESH)
    pl.semaphore_wait(barrier, len(peers))

    local = pltpu.make_async_copy(x_ref, blk(y, z, k), local_sem.at[0])
    local.start()
    acc[...] = jnp.zeros_like(acc)

    if mode == "first":
        wcol = floc_ref.shape[1]
        hcol = wcol // 2

        def fcols(cc, lo=0, n=wcol):
            return f_ref.at[:, pl.ds(pl.multiple_of(((cc + nx) % nx) * wcol + lo, 128), n)]

        def xcopy(src, dst, si, rsem, d):
            return pltpu.make_async_remote_copy(
                src_ref=src, dst_ref=dst, send_sem=send_sem.at[si], recv_sem=rsem,
                device_id=d, device_id_type=MESH,
            )

        flocal = pltpu.make_async_copy(floc_ref, fcols(c), local_sem.at[1])
        flocal.start()
        xsends = [xcopy(floc_ref, fcols(c), 64, recv_x.at[0], xr), xcopy(floc_ref, fcols(c), 65, recv_x.at[1], xl)]
        for cp in xsends:
            cp.start()

    sends = []

    def remote(src, dst, rsem, d, si=0):
        return pltpu.make_async_remote_copy(
            src_ref=src, dst_ref=dst, send_sem=send_sem.at[si], recv_sem=rsem,
            device_id=(d, c), device_id_type=MESH,
        )

    def send(src, dst, rsem, d):
        cp = remote(src, dst, rsem, d, len(sends))
        cp.start()
        sends.append(cp)

    def wait(ref, rsem):
        remote(ref, ref, rsem, partner).wait_recv()

    def multiply(yy):
        if fused:
            plane = (yy + NY) % NY
            cols = pl.ds(pl.multiple_of(plane * (NZ * NC * nb), nb), NZ * NC * nb)
            vec = G[pl.ds(plane * NZ, NZ)].reshape(NZ * NC * nb, w)
            acc[...] += jnp.dot(
                f_ref[:, cols] * m_ref[:, cols], vec,
                precision=lax.Precision.HIGHEST, preferred_element_type=jnp.float32,
            )

    offs = [0, -1, 1, -2, 2, -3, 3, -4]
    to_right = {0, -1, -2, -3}

    def spread(off):
        i = offs.index(off)
        ref = x_ref if off == 0 else blk(y, z + off, k)
        send(ref, blk(y, z + off, k), recv_y.at[0, i], yr)
        send(ref, blk(y, z + off, k), recv_y.at[1, i], yl)
        send(ref, blk(y, z + off, k), recv_c.at[0, i], partner)

    def recv_of(zsrc):
        return recv_z.at[(zsrc + NZ) % NZ]

    for d in (1, 2, -1, -2):
        send(x_ref, blk(y, z, k), recv_of(z), dev(y, z + d, k))
    spread(0)
    wait(blk(y, z - 2, k), recv_of(z - 2))
    send(blk(y, z - 2, k), blk(y, z - 2, k), recv_of(z - 2), dev(y, z + 1, k))
    send(blk(y, z - 2, k), blk(y, z - 2, k), recv_of(z - 2), dev(y, z + 2, k))
    wait(blk(y, z + 2, k), recv_of(z + 2))
    send(blk(y, z + 2, k), blk(y, z + 2, k), recv_of(z + 2), dev(y, z - 1, k))
    for off in (-1, 1):
        wait(blk(y, z + off, k), recv_of(z + off))
        spread(off)
    spread(-2)
    spread(2)
    for off in (-3, 3, -4):
        wait(blk(y, z + off, k), recv_of(z + off))
        spread(off)
    local.wait()

    for i, off in enumerate(offs):
        wait(blk(y - 1, z + off, k), recv_y.at[0, i])
        if off in to_right:
            send(blk(y - 1, z + off, k), blk(y - 1, z + off, k), recv_y.at[2, i], yr)
        send(blk(y - 1, z + off, k), blk(y - 1, z + off, k), recv_c.at[3, i], partner)
        wait(blk(y + 1, z + off, k), recv_y.at[1, i])
        if off not in to_right:
            send(blk(y + 1, z + off, k), blk(y + 1, z + off, k), recv_y.at[3, i], yl)
        send(blk(y + 1, z + off, k), blk(y + 1, z + off, k), recv_c.at[1, i], partner)

    def partner_plane(d):
        for i, off in enumerate(offs):
            wait(blk(y + d, z + off, 1 - k), recv_c.at[d % NY, i])
        multiply(y + d)

    def partner_wait(d):
        for i, off in enumerate(offs):
            wait(blk(y + d, z + off, 1 - k), recv_c.at[d % NY, i])

    if mode == "first":
        xcopy(floc_ref, fcols(c - 1), 0, recv_x.at[0], xr).wait_recv()
        xsends.append(xcopy(fcols(c - 1, 0, hcol), fcols(c - 1, 0, hcol), 66, recv_x.at[2], xr))
        xsends[-1].start()
        xcopy(floc_ref, fcols(c + 1), 0, recv_x.at[1], xr).wait_recv()
        xsends.append(xcopy(fcols(c + 1, hcol, hcol), fcols(c + 1, hcol, hcol), 67, recv_x.at[3], xl))
        xsends[-1].start()
    else:
        partner_wait(0)
        multiply(y)
    for i, off in enumerate(offs):
        wait(blk(y + 2, z + off, k), recv_y.at[2 if off in to_right else 3, i])
        send(blk(y + 2, z + off, k), blk(y + 2, z + off, k), recv_c.at[2, i], partner)
    if mode == "first":
        for d in (0, -1, 1, 2):
            partner_wait(d)
        flocal.wait()
        multiply(c)
        multiply(c - 1)
        multiply(c + 1)
        xcopy(fcols(c + 2, 0, hcol), fcols(c + 2, 0, hcol), 0, recv_x.at[2], xr).wait_recv()
        xcopy(fcols(c + 2, hcol, hcol), fcols(c + 2, hcol, hcol), 0, recv_x.at[3], xr).wait_recv()
        multiply(c + 2)
        for cp in xsends:
            cp.wait_send()
        fout = pltpu.make_async_copy(f_ref, fout_ref, local_sem.at[1])
        fout.start()
        fout.wait()
    else:
        for d in (-1, 1, 2):
            partner_wait(d)
            multiply(y + d)

    for cp in sends:
        cp.wait_send()
    if mode == "first":
        out_ref[...] = jnp.where(sel_ref[...] > 0.5, acc[...], 0.0)
    else:
        for ref, value in zip(out_refs, epilogue(acc[...], *[e[...] for e in extra_refs])):
            ref[...] = value


def _sems():
    return [
        pltpu.SemaphoreType.DMA((2,)),
        pltpu.SemaphoreType.DMA((68,)),
        pltpu.SemaphoreType.DMA((NZ,)),
        pltpu.SemaphoreType.DMA((4, NZ)),
        pltpu.SemaphoreType.DMA((NY, NZ)),
    ]


def _specs(n):
    return [pl.BlockSpec(memory_space=pltpu.VMEM)] * n


def first_product(floc, mask_row, sel, x, cid):
    nb, w = x.shape
    rows = floc.shape[0]
    ncol = floc.shape[1] * 4
    return pl.pallas_call(
        functools.partial(gather_kernel, mode="first"),
        out_shape=(jax.ShapeDtypeStruct((rows, w), jnp.float32), jax.ShapeDtypeStruct((rows, ncol), floc.dtype)),
        in_specs=_specs(4),
        out_specs=(pl.BlockSpec(memory_space=pltpu.VMEM), pl.BlockSpec(memory_space=pl.ANY)),
        scratch_shapes=[pltpu.VMEM((NY * NZ, NC, nb, w), x.dtype), pltpu.VMEM((rows, ncol), floc.dtype),
                        pltpu.VMEM((rows, w), jnp.float32)]
        + _sems() + [pltpu.SemaphoreType.DMA((4,))],
        compiler_params=pltpu.CompilerParams(collective_id=cid, has_side_effects=True),
        cost_estimate=pl.CostEstimate(
            flops=2 * rows * ncol * w, transcendentals=0, bytes_accessed=(2 * rows * ncol + 2 * x.size * 64) * 4,
        ),
    )(x, floc, mask_row, sel)


def gather_product(matrix, mask_row, x, cid, extras, epilogue, n_out):
    nb, w = x.shape
    shape = (NY * NZ, NC, nb, w)
    out = jax.ShapeDtypeStruct((matrix.shape[0], w), jnp.float32)
    return pl.pallas_call(
        functools.partial(gather_kernel, mode="fused", epilogue=epilogue, n_extra=len(extras), n_out=n_out),
        out_shape=tuple([out] * n_out),
        in_specs=_specs(3 + len(extras)),
        out_specs=tuple(pl.BlockSpec(memory_space=pltpu.VMEM) for _ in range(n_out)),
        scratch_shapes=[pltpu.VMEM(shape, x.dtype), pltpu.VMEM((matrix.shape[0], w), jnp.float32)]
        + _sems(),
        compiler_params=pltpu.CompilerParams(collective_id=cid, has_side_effects=True),
        cost_estimate=pl.CostEstimate(
            flops=2 * matrix.shape[0] * matrix.shape[1] * w, transcendentals=0,
            bytes_accessed=(matrix.size + 2 * x.size * 64) * 4,
        ),
    )(x, matrix, mask_row, *extras)


def _link_epilogue(prod, accum, rhs):
    accum = accum + prod
    return accum, rhs - accum


def _first_link_epilogue(prod, rhs):
    accum = jnp.zeros_like(prod) + prod
    return accum, rhs - accum


def _diag_epilogue(prod, sel, result):
    solved = jnp.where(sel > 0.5, prod, 0.0)
    return solved, result + solved


def body(factor, rhs, parent, bounds, slot, structure):
    level_mine, same, link = row_masks(parent, bounds, slot, structure, lax.axis_index("row"))
    same_row = jnp.repeat(same.astype(jnp.float32), B)[None, :]
    link_row = jnp.repeat(link.astype(jnp.float32), B)[None, :]

    def selector(section):
        return jnp.full((1, rhs.shape[1]), (level_mine == section).astype(jnp.float32))

    solved, full_rows = first_product(factor, same_row, selector(0), rhs, 0)
    result = solved
    accum, vector = gather_product(full_rows, link_row, solved, 1, (rhs,), _first_link_epilogue, 2)
    for section in (1, 2):
        solved, result = gather_product(full_rows, same_row, vector, 2 * section, (selector(section), result),
                                        _diag_epilogue, 2)
        if section < 2:
            accum, vector = gather_product(full_rows, link_row, solved, 2 * section + 1, (accum, rhs),
                                           _link_epilogue, 2)
    return result


def solution(mesh):
    in_specs = (P("row", "col"), P("row", "col"), P(), P(), P(), P())
    out_specs = P("row", "col")
    return jax.shard_map(body, mesh=mesh, in_specs=in_specs, out_specs=out_specs, check_vma=False)
```

```python
import functools

import jax
import jax.numpy as jnp
from jax import lax
from jax.experimental import pallas as pl
from jax.experimental.pallas import tpu as pltpu
from jax.sharding import PartitionSpec as P

B = 128
RB = 1
MESH = pl.DeviceIdType.MESH
NY, NZ, NC = 4, 8, 2


def row_masks(parent, bounds, slot, structure, r):
    count = slot.shape[0]
    ar = jnp.arange(count, dtype=jnp.int32)
    nodes = jnp.arange(parent.shape[0], dtype=jnp.int32)
    logical = jnp.sum(jnp.where(slot[:, None] == ar[None, :], ar[:, None], 0), axis=0)
    node = jnp.sum((logical[:, None] >= bounds[None, 1:7]).astype(jnp.int32), axis=1)
    mine = ar == r
    node_r = jnp.sum(jnp.where(mine, node, 0))
    logical_r = jnp.sum(jnp.where(mine, logical, 0))
    level_r = (node_r >= 4).astype(jnp.int32) + (node_r >= 6).astype(jnp.int32)
    hot = node[:, None] == nodes[None, :]
    par = jnp.sum(jnp.where(hot, parent[None, :], 0), axis=1)
    grand = jnp.sum(jnp.where(par[:, None] == nodes[None, :], parent[None, :], 0), axis=1)
    ancestor = ((par == node_r) | (grand == node_r)) & (node != node_r)
    column = jnp.sum(jnp.where(ar[None, :] == logical_r, structure, 0), axis=1)
    listed = jnp.sum(jnp.where(hot, column[None, :], 0), axis=1) == 1
    return level_r, node == node_r, ancestor & listed


def gather_kernel(*refs, mode, which, section=0, epilogue=None, n_extra=0, n_out=1):
    fused = True
    if mode == "first":
        x_ref, floc_ref, m_ref, sel_ref, out_ref, fout_ref, G, f_ref, acc, local_sem, send_sem, recv_z, recv_y, recv_c, \
            recv_x = refs
    else:
        x_ref, f_ref, m_ref = refs[:3]
        extra_refs = refs[3:3 + n_extra]
        out_refs = refs[3 + n_extra:3 + n_extra + n_out]
        G, acc, local_sem, send_sem, recv_z, recv_y, recv_c = refs[3 + n_extra + n_out:]
    nb, w = x_ref.shape
    r = lax.axis_index("row")
    c = lax.axis_index("col")
    y = r // (NZ * NC)
    z = (r // NC) % NZ
    k = r % NC

    def dev(yy, zz, kk):
        return (((yy + NY) % NY) * NZ + (zz + NZ) % NZ) * NC + kk

    def blk(yy, zz, kk):
        return G.at[((yy + NY) % NY) * NZ + (zz + NZ) % NZ, kk]

    def chunk(kk, yy, lo=0, n=NZ):
        return G.at[pl.ds(((yy + NY) % NY) * NZ + lo, n), kk]

    zr, zl = dev(y, z + 1, k), dev(y, z - 1, k)
    yr, yl = dev(y + 1, z, k), dev(y - 1, z, k)
    partner = dev(y, z, 1 - k)

    barrier = pltpu.get_barrier_semaphore()
    peers = [(d, c) for d in (zr, zl, dev(y, z + 2, k), dev(y, z - 2, k), yr, yl, partner)]
    nx = 4
    xr, xl = (r, (c + 1) % nx), (r, (c + nx - 1) % nx)
    if mode == "first":
        peers += [xr, xl]
    for d in peers:
        pl.semaphore_signal(barrier, inc=1, device_id=d, device_id_type=MESH)
    pl.semaphore_wait(barrier, len(peers))

    local = pltpu.make_async_copy(x_ref, blk(y, z, k), local_sem.at[0])
    local.start()
    acc[...] = jnp.zeros_like(acc)

    if mode == "first":
        wcol = floc_ref.shape[1]
        hcol = wcol // 2

        def fcols(cc, lo=0, n=wcol):
            return f_ref.at[:, pl.ds(pl.multiple_of(((cc + nx) % nx) * wcol + lo, 128), n)]

        def xcopy(src, dst, si, rsem, d):
            return pltpu.make_async_remote_copy(
                src_ref=src, dst_ref=dst, send_sem=send_sem.at[si], recv_sem=rsem,
                device_id=d, device_id_type=MESH,
            )

        flocal = pltpu.make_async_copy(floc_ref, fcols(c), local_sem.at[1])
        flocal.start()
        xsends = [xcopy(floc_ref, fcols(c), 64, recv_x.at[0], xr), xcopy(floc_ref, fcols(c), 65, recv_x.at[1], xl)]
        for cp in xsends:
            cp.start()

    sends = []

    def remote(src, dst, rsem, d, si=0):
        return pltpu.make_async_remote_copy(
            src_ref=src, dst_ref=dst, send_sem=send_sem.at[si], recv_sem=rsem,
            device_id=(d, c), device_id_type=MESH,
        )

    def send(src, dst, rsem, d):
        cp = remote(src, dst, rsem, d, len(sends))
        cp.start()
        sends.append(cp)

    def wait(ref, rsem):
        remote(ref, ref, rsem, partner).wait_recv()

    def multiply(yy):
        if fused:
            plane = (yy + NY) % NY
            cols = pl.ds(pl.multiple_of(plane * (NZ * NC * nb), nb), NZ * NC * nb)
            vec = G[pl.ds(plane * NZ, NZ)].reshape(NZ * NC * nb, w)
            acc[...] += jnp.dot(
                f_ref[:, cols] * m_ref[which:which + 1, cols], vec,
                precision=lax.Precision.HIGHEST, preferred_element_type=jnp.float32,
            )

    offs = [0, -1, 1, -2, 2, -3, 3, -4]
    to_right = {0, -1, -2, -3}

    def spread(off):
        i = offs.index(off)
        ref = x_ref if off == 0 else blk(y, z + off, k)
        send(ref, blk(y, z + off, k), recv_y.at[0, i], yr)
        send(ref, blk(y, z + off, k), recv_y.at[1, i], yl)
        send(ref, blk(y, z + off, k), recv_c.at[0, i], partner)

    def recv_of(zsrc):
        return recv_z.at[(zsrc + NZ) % NZ]

    for d in (1, 2, -1, -2):
        send(x_ref, blk(y, z, k), recv_of(z), dev(y, z + d, k))
    spread(0)
    wait(blk(y, z - 2, k), recv_of(z - 2))
    send(blk(y, z - 2, k), blk(y, z - 2, k), recv_of(z - 2), dev(y, z + 1, k))
    send(blk(y, z - 2, k), blk(y, z - 2, k), recv_of(z - 2), dev(y, z + 2, k))
    wait(blk(y, z + 2, k), recv_of(z + 2))
    send(blk(y, z + 2, k), blk(y, z + 2, k), recv_of(z + 2), dev(y, z - 1, k))
    for off in (-1, 1):
        wait(blk(y, z + off, k), recv_of(z + off))
        spread(off)
    spread(-2)
    spread(2)
    for off in (-3, 3, -4):
        wait(blk(y, z + off, k), recv_of(z + off))
        spread(off)
    local.wait()

    for i, off in enumerate(offs):
        wait(blk(y - 1, z + off, k), recv_y.at[0, i])
        if off in to_right:
            send(blk(y - 1, z + off, k), blk(y - 1, z + off, k), recv_y.at[2, i], yr)
        send(blk(y - 1, z + off, k), blk(y - 1, z + off, k), recv_c.at[3, i], partner)
        wait(blk(y + 1, z + off, k), recv_y.at[1, i])
        if off not in to_right:
            send(blk(y + 1, z + off, k), blk(y + 1, z + off, k), recv_y.at[3, i], yl)
        send(blk(y + 1, z + off, k), blk(y + 1, z + off, k), recv_c.at[1, i], partner)

    def partner_plane(d):
        for i, off in enumerate(offs):
            wait(blk(y + d, z + off, 1 - k), recv_c.at[d % NY, i])
        multiply(y + d)

    def partner_wait(d):
        for i, off in enumerate(offs):
            wait(blk(y + d, z + off, 1 - k), recv_c.at[d % NY, i])

    if mode == "first":
        xcopy(floc_ref, fcols(c - 1), 0, recv_x.at[0], xr).wait_recv()
        xsends.append(xcopy(fcols(c - 1, 0, hcol), fcols(c - 1, 0, hcol), 66, recv_x.at[2], xr))
        xsends[-1].start()
        xcopy(floc_ref, fcols(c + 1), 0, recv_x.at[1], xr).wait_recv()
        xsends.append(xcopy(fcols(c + 1, hcol, hcol), fcols(c + 1, hcol, hcol), 67, recv_x.at[3], xl))
        xsends[-1].start()
    else:
        partner_wait(0)
        multiply(y)
    for i, off in enumerate(offs):
        wait(blk(y + 2, z + off, k), recv_y.at[2 if off in to_right else 3, i])
        send(blk(y + 2, z + off, k), blk(y + 2, z + off, k), recv_c.at[2, i], partner)
    if mode == "first":
        for d in (0, -1, 1, 2):
            partner_wait(d)
        flocal.wait()
        multiply(c)
        multiply(c - 1)
        multiply(c + 1)
        xcopy(fcols(c + 2, 0, hcol), fcols(c + 2, 0, hcol), 0, recv_x.at[2], xr).wait_recv()
        xcopy(fcols(c + 2, hcol, hcol), fcols(c + 2, hcol, hcol), 0, recv_x.at[3], xr).wait_recv()
        multiply(c + 2)
        for cp in xsends:
            cp.wait_send()
        fout = pltpu.make_async_copy(f_ref, fout_ref, local_sem.at[1])
        fout.start()
        fout.wait()
    else:
        for d in (-1, 1, 2):
            partner_wait(d)
            multiply(y + d)

    for cp in sends:
        cp.wait_send()
    if mode == "first":
        out_ref[...] = jnp.where(sel_ref[section:section + 1, :] > 0.5, acc[...], 0.0)
    else:
        for ref, value in zip(out_refs, epilogue(acc[...], *[e[...] for e in extra_refs])):
            ref[...] = value


def _sems():
    return [
        pltpu.SemaphoreType.DMA((2,)),
        pltpu.SemaphoreType.DMA((68,)),
        pltpu.SemaphoreType.DMA((NZ,)),
        pltpu.SemaphoreType.DMA((4, NZ)),
        pltpu.SemaphoreType.DMA((NY, NZ)),
    ]


def _specs(n):
    return [pl.BlockSpec(memory_space=pltpu.VMEM)] * n


def first_product(floc, mask_row, sel, x, cid):
    nb, w = x.shape
    rows = floc.shape[0]
    ncol = floc.shape[1] * 4
    return pl.pallas_call(
        functools.partial(gather_kernel, mode="first", which=0),
        out_shape=(jax.ShapeDtypeStruct((rows, w), jnp.float32), jax.ShapeDtypeStruct((rows, ncol), floc.dtype)),
        in_specs=_specs(4),
        out_specs=(pl.BlockSpec(memory_space=pltpu.VMEM), pl.BlockSpec(memory_space=pl.ANY)),
        scratch_shapes=[pltpu.VMEM((NY * NZ, NC, nb, w), x.dtype), pltpu.VMEM((rows, ncol), floc.dtype),
                        pltpu.VMEM((rows, w), jnp.float32)]
        + _sems() + [pltpu.SemaphoreType.DMA((4,))],
        compiler_params=pltpu.CompilerParams(collective_id=cid, has_side_effects=True),
        cost_estimate=pl.CostEstimate(
            flops=2 * rows * ncol * w, transcendentals=0, bytes_accessed=(2 * rows * ncol + 2 * x.size * 64) * 4,
        ),
    )(x, floc, mask_row, sel)


def gather_product(matrix, mask_row, which, x, cid, extras, epilogue, n_out):
    nb, w = x.shape
    shape = (NY * NZ, NC, nb, w)
    out = jax.ShapeDtypeStruct((matrix.shape[0], w), jnp.float32)
    return pl.pallas_call(
        functools.partial(gather_kernel, mode="fused", which=which, epilogue=epilogue, n_extra=len(extras),
                          n_out=n_out),
        out_shape=tuple([out] * n_out),
        in_specs=_specs(3 + len(extras)),
        out_specs=tuple(pl.BlockSpec(memory_space=pltpu.VMEM) for _ in range(n_out)),
        scratch_shapes=[pltpu.VMEM(shape, x.dtype), pltpu.VMEM((matrix.shape[0], w), jnp.float32)]
        + _sems(),
        compiler_params=pltpu.CompilerParams(collective_id=cid, has_side_effects=True),
        cost_estimate=pl.CostEstimate(
            flops=2 * matrix.shape[0] * matrix.shape[1] * w, transcendentals=0,
            bytes_accessed=(matrix.size + 2 * x.size * 64) * 4,
        ),
    )(x, matrix, mask_row, *extras)


def _link_epilogue(prod, accum, rhs):
    accum = accum + prod
    return accum, rhs - accum


def _first_link_epilogue(prod, rhs):
    accum = jnp.zeros_like(prod) + prod
    return accum, rhs - accum


def _diag_epilogue(prod, sel, result, section):
    solved = jnp.where(sel[section:section + 1, :] > 0.5, prod, 0.0)
    return solved, result + solved


def body(factor, rhs, parent, bounds, slot, structure):
    level_mine, same, link = row_masks(parent, bounds, slot, structure, lax.axis_index("row"))
    masks = jnp.repeat(jnp.stack([same, link]).astype(jnp.float32), B, axis=1)
    sels = jnp.repeat((level_mine == jnp.arange(3, dtype=jnp.int32)).astype(jnp.float32)[:, None], rhs.shape[1],
                      axis=1)

    solved, full_rows = first_product(factor, masks, sels, rhs, 0)
    result = solved
    accum, vector = gather_product(full_rows, masks, 1, solved, 1, (rhs,), _first_link_epilogue, 2)
    for section in (1, 2):
        epi = functools.partial(_diag_epilogue, section=section)
        solved, result = gather_product(full_rows, masks, 0, vector, 2 * section, (sels, result), epi, 2)
        if section < 2:
            accum, vector = gather_product(full_rows, masks, 1, solved, 2 * section + 1, (accum, rhs),
                                           _link_epilogue, 2)
    return result


def solution(mesh):
    in_specs = (P("row", "col"), P("row", "col"), P(), P(), P(), P())
    out_specs = P("row", "col")
    return jax.shard_map(body, mesh=mesh, in_specs=in_specs, out_specs=out_specs, check_vma=False)
```

```python
import functools

import jax
import jax.numpy as jnp
from jax import lax
from jax.experimental import pallas as pl
from jax.experimental.pallas import tpu as pltpu
from jax.sharding import PartitionSpec as P

B = 128
RB = 1
MESH = pl.DeviceIdType.MESH
NY, NZ, NC = 4, 8, 2


def row_masks(parent, bounds, slot, structure, r):
    count = slot.shape[0]
    ar = jnp.arange(count, dtype=jnp.int32)
    nodes = jnp.arange(parent.shape[0], dtype=jnp.int32)
    logical = jnp.sum(jnp.where(slot[:, None] == ar[None, :], ar[:, None], 0), axis=0)
    node = jnp.sum((logical[:, None] >= bounds[None, 1:7]).astype(jnp.int32), axis=1)
    mine = ar == r
    node_r = jnp.sum(jnp.where(mine, node, 0))
    logical_r = jnp.sum(jnp.where(mine, logical, 0))
    level_r = (node_r >= 4).astype(jnp.int32) + (node_r >= 6).astype(jnp.int32)
    hot = node[:, None] == nodes[None, :]
    par = jnp.sum(jnp.where(hot, parent[None, :], 0), axis=1)
    grand = jnp.sum(jnp.where(par[:, None] == nodes[None, :], parent[None, :], 0), axis=1)
    ancestor = ((par == node_r) | (grand == node_r)) & (node != node_r)
    column = jnp.sum(jnp.where(ar[None, :] == logical_r, structure, 0), axis=1)
    listed = jnp.sum(jnp.where(hot, column[None, :], 0), axis=1) == 1
    return level_r, node == node_r, ancestor & listed


def gather_kernel(*refs, mode, which, section=0, epilogue=None, n_extra=0, n_out=1):
    fused = True
    if mode == "first":
        x_ref, floc_ref, m_ref, sel_ref, out_ref, fout_ref, G, f_ref, acc, local_sem, send_sem, recv_z, recv_y, recv_c, \
            recv_x = refs
    else:
        x_ref, f_ref, m_ref = refs[:3]
        extra_refs = refs[3:3 + n_extra]
        out_refs = refs[3 + n_extra:3 + n_extra + n_out]
        G, acc, local_sem, send_sem, recv_z, recv_y, recv_c = refs[3 + n_extra + n_out:]
    nb, w = x_ref.shape
    r = lax.axis_index("row")
    c = lax.axis_index("col")
    y = r // (NZ * NC)
    z = (r // NC) % NZ
    k = r % NC

    def dev(yy, zz, kk):
        return (((yy + NY) % NY) * NZ + (zz + NZ) % NZ) * NC + kk

    def blk(yy, zz, kk):
        return G.at[((yy + NY) % NY) * NZ + (zz + NZ) % NZ, kk]

    def chunk(kk, yy, lo=0, n=NZ):
        return G.at[pl.ds(((yy + NY) % NY) * NZ + lo, n), kk]

    zr, zl = dev(y, z + 1, k), dev(y, z - 1, k)
    yr, yl = dev(y + 1, z, k), dev(y - 1, z, k)
    partner = dev(y, z, 1 - k)

    barrier = pltpu.get_barrier_semaphore()
    peers = [(d, c) for d in (zr, zl, dev(y, z + 2, k), dev(y, z - 2, k), yr, yl, partner)]
    nx = 4
    xr, xl = (r, (c + 1) % nx), (r, (c + nx - 1) % nx)
    if mode == "first":
        peers += [xr, xl]
    for d in peers:
        pl.semaphore_signal(barrier, inc=1, device_id=d, device_id_type=MESH)
    pl.semaphore_wait(barrier, len(peers))

    local = pltpu.make_async_copy(x_ref, blk(y, z, k), local_sem.at[0])
    local.start()
    acc[...] = jnp.zeros_like(acc)

    if mode == "first":
        wcol = floc_ref.shape[1]
        hcol = wcol // 2

        def fcols(cc, lo=0, n=wcol):
            return f_ref.at[:, pl.ds(pl.multiple_of(((cc + nx) % nx) * wcol + lo, 128), n)]

        def xcopy(src, dst, si, rsem, d):
            return pltpu.make_async_remote_copy(
                src_ref=src, dst_ref=dst, send_sem=send_sem.at[si], recv_sem=rsem,
                device_id=d, device_id_type=MESH,
            )

        flocal = pltpu.make_async_copy(floc_ref, fcols(c), local_sem.at[1])
        flocal.start()
        xsends = [xcopy(floc_ref, fcols(c), 64, recv_x.at[0], xr), xcopy(floc_ref, fcols(c), 65, recv_x.at[1], xl)]
        for cp in xsends:
            cp.start()

    sends = []

    def remote(src, dst, rsem, d, si=0):
        return pltpu.make_async_remote_copy(
            src_ref=src, dst_ref=dst, send_sem=send_sem.at[si], recv_sem=rsem,
            device_id=(d, c), device_id_type=MESH,
        )

    def send(src, dst, rsem, d):
        cp = remote(src, dst, rsem, d, len(sends))
        cp.start()
        sends.append(cp)

    def wait(ref, rsem):
        remote(ref, ref, rsem, partner).wait_recv()

    def multiply(yy):
        if fused:
            plane = (yy + NY) % NY
            cols = pl.ds(pl.multiple_of(plane * (NZ * NC * nb), nb), NZ * NC * nb)
            vec = G[pl.ds(plane * NZ, NZ)].reshape(NZ * NC * nb, w)
            acc[...] += jnp.dot(
                f_ref[:, cols] * m_ref[which:which + 1, cols], vec,
                precision=lax.Precision.HIGHEST, preferred_element_type=jnp.float32,
            )

    offs = [0, -1, 1, -2, 2, -3, 3, -4]
    to_right = {0, -1, -2, -3}

    def spread(off):
        i = offs.index(off)
        ref = x_ref if off == 0 else blk(y, z + off, k)
        send(ref, blk(y, z + off, k), recv_y.at[0, i], yr)
        send(ref, blk(y, z + off, k), recv_y.at[1, i], yl)
        send(ref, blk(y, z + off, k), recv_c.at[0, i], partner)

    def recv_of(zsrc):
        return recv_z.at[(zsrc + NZ) % NZ]

    for d in (1, 2, -1, -2):
        send(x_ref, blk(y, z, k), recv_of(z), dev(y, z + d, k))
    spread(0)
    wait(blk(y, z - 2, k), recv_of(z - 2))
    send(blk(y, z - 2, k), blk(y, z - 2, k), recv_of(z - 2), dev(y, z + 1, k))
    send(blk(y, z - 2, k), blk(y, z - 2, k), recv_of(z - 2), dev(y, z + 2, k))
    wait(blk(y, z + 2, k), recv_of(z + 2))
    send(blk(y, z + 2, k), blk(y, z + 2, k), recv_of(z + 2), dev(y, z - 1, k))
    for off in (-1, 1):
        wait(blk(y, z + off, k), recv_of(z + off))
        spread(off)
    spread(-2)
    spread(2)
    for off in (-3, 3, -4):
        wait(blk(y, z + off, k), recv_of(z + off))
        spread(off)
    local.wait()

    for i, off in enumerate(offs):
        wait(blk(y - 1, z + off, k), recv_y.at[0, i])
        if off in to_right:
            send(blk(y - 1, z + off, k), blk(y - 1, z + off, k), recv_y.at[2, i], yr)
        send(blk(y - 1, z + off, k), blk(y - 1, z + off, k), recv_c.at[3, i], partner)
        wait(blk(y + 1, z + off, k), recv_y.at[1, i])
        if off not in to_right:
            send(blk(y + 1, z + off, k), blk(y + 1, z + off, k), recv_y.at[3, i], yl)
        send(blk(y + 1, z + off, k), blk(y + 1, z + off, k), recv_c.at[1, i], partner)

    def partner_plane(d):
        for i, off in enumerate(offs):
            wait(blk(y + d, z + off, 1 - k), recv_c.at[d % NY, i])
        multiply(y + d)

    def partner_wait(d):
        for i, off in enumerate(offs):
            wait(blk(y + d, z + off, 1 - k), recv_c.at[d % NY, i])

    if mode == "first":
        xcopy(floc_ref, fcols(c - 1), 0, recv_x.at[0], xr).wait_recv()
        xsends.append(xcopy(fcols(c - 1, 0, hcol), fcols(c - 1, 0, hcol), 66, recv_x.at[2], xr))
        xsends[-1].start()
        xcopy(floc_ref, fcols(c + 1), 0, recv_x.at[1], xr).wait_recv()
        xsends.append(xcopy(fcols(c + 1, hcol, hcol), fcols(c + 1, hcol, hcol), 67, recv_x.at[3], xl))
        xsends[-1].start()
    else:
        partner_wait(0)
        multiply(y)
    for i, off in enumerate(offs):
        wait(blk(y + 2, z + off, k), recv_y.at[2 if off in to_right else 3, i])
        send(blk(y + 2, z + off, k), blk(y + 2, z + off, k), recv_c.at[2, i], partner)
    if mode == "first":
        for d in (0, -1, 1, 2):
            partner_wait(d)
        flocal.wait()
        multiply(c)
        multiply(c - 1)
        multiply(c + 1)
        xcopy(fcols(c + 2, 0, hcol), fcols(c + 2, 0, hcol), 0, recv_x.at[2], xr).wait_recv()
        xcopy(fcols(c + 2, hcol, hcol), fcols(c + 2, hcol, hcol), 0, recv_x.at[3], xr).wait_recv()
        multiply(c + 2)
        for cp in xsends:
            cp.wait_send()
        fout = pltpu.make_async_copy(f_ref, fout_ref, local_sem.at[1])
        fout.start()
        fout.wait()
    else:
        for d in (-1, 1, 2):
            partner_wait(d)
            multiply(y + d)

    for cp in sends:
        cp.wait_send()
    if mode == "first":
        out_ref[...] = jnp.where(sel_ref[section:section + 1, :] > 0.5, acc[...], 0.0)
    else:
        for ref, value in zip(out_refs, epilogue(acc[...], *[e[...] for e in extra_refs])):
            ref[...] = value


def _sems():
    return [
        pltpu.SemaphoreType.DMA((2,)),
        pltpu.SemaphoreType.DMA((68,)),
        pltpu.SemaphoreType.DMA((NZ,)),
        pltpu.SemaphoreType.DMA((4, NZ)),
        pltpu.SemaphoreType.DMA((NY, NZ)),
    ]


def _specs(n):
    return [pl.BlockSpec(memory_space=pltpu.VMEM)] * n


def first_product(floc, mask_row, sel, x, cid):
    nb, w = x.shape
    rows = floc.shape[0]
    ncol = floc.shape[1] * 4
    return pl.pallas_call(
        functools.partial(gather_kernel, mode="first", which=0),
        out_shape=(jax.ShapeDtypeStruct((rows, w), jnp.float32), jax.ShapeDtypeStruct((rows, ncol), floc.dtype)),
        in_specs=_specs(4),
        out_specs=(pl.BlockSpec(memory_space=pltpu.VMEM), pl.BlockSpec(memory_space=pl.ANY)),
        scratch_shapes=[pltpu.VMEM((NY * NZ, NC, nb, w), x.dtype), pltpu.VMEM((rows, ncol), floc.dtype),
                        pltpu.VMEM((rows, w), jnp.float32)]
        + _sems() + [pltpu.SemaphoreType.DMA((4,))],
        compiler_params=pltpu.CompilerParams(collective_id=cid, has_side_effects=True),
        cost_estimate=pl.CostEstimate(
            flops=2 * rows * ncol * w, transcendentals=0, bytes_accessed=(2 * rows * ncol + 2 * x.size * 64) * 4,
        ),
    )(x, floc, mask_row, sel)


def gather_product(matrix, mask_row, which, x, cid, extras, epilogue, n_out):
    nb, w = x.shape
    shape = (NY * NZ, NC, nb, w)
    out = jax.ShapeDtypeStruct((matrix.shape[0], w), jnp.float32)
    return pl.pallas_call(
        functools.partial(gather_kernel, mode="fused", which=which, epilogue=epilogue, n_extra=len(extras),
                          n_out=n_out),
        out_shape=tuple([out] * n_out),
        in_specs=_specs(3 + len(extras)),
        out_specs=tuple(pl.BlockSpec(memory_space=pltpu.VMEM) for _ in range(n_out)),
        scratch_shapes=[pltpu.VMEM(shape, x.dtype), pltpu.VMEM((matrix.shape[0], w), jnp.float32)]
        + _sems(),
        compiler_params=pltpu.CompilerParams(collective_id=cid, has_side_effects=True),
        cost_estimate=pl.CostEstimate(
            flops=2 * matrix.shape[0] * matrix.shape[1] * w, transcendentals=0,
            bytes_accessed=(matrix.size + 2 * x.size * 64) * 4,
        ),
    )(x, matrix, mask_row, *extras)


def _link_epilogue(prod, accum, rhs):
    accum = accum + prod
    return accum, rhs - accum


def _first_link_epilogue(prod, rhs):
    accum = jnp.zeros_like(prod) + prod
    return accum, rhs - accum


def _last_epilogue(prod, sel):
    return (jnp.where(sel[2:3, :] > 0.5, prod, 0.0),)


def _diag_epilogue(prod, sel, result, section):
    solved = jnp.where(sel[section:section + 1, :] > 0.5, prod, 0.0)
    return solved, result + solved


def body(factor, rhs, parent, bounds, slot, structure):
    level_mine, same, link = row_masks(parent, bounds, slot, structure, lax.axis_index("row"))
    masks = jnp.repeat(jnp.stack([same, link]).astype(jnp.float32), B, axis=1)
    sels = jnp.repeat((level_mine == jnp.arange(3, dtype=jnp.int32)).astype(jnp.float32)[:, None], rhs.shape[1],
                      axis=1)

    solved, full_rows = first_product(factor, masks, sels, rhs, 0)
    result = solved
    accum, vector = gather_product(full_rows, masks, 1, solved, 1, (rhs,), _first_link_epilogue, 2)
    epi = functools.partial(_diag_epilogue, section=1)
    solved, result = gather_product(full_rows, masks, 0, vector, 2, (sels, result), epi, 2)
    accum, vector = gather_product(full_rows, masks, 1, solved, 3, (accum, rhs), _link_epilogue, 2)
    (solved,) = gather_product(full_rows, masks, 0, vector, 4, (sels,), _last_epilogue, 1)
    return result + solved


def solution(mesh):
    in_specs = (P("row", "col"), P("row", "col"), P(), P(), P(), P())
    out_specs = P("row", "col")
    return jax.shard_map(body, mesh=mesh, in_specs=in_specs, out_specs=out_specs, check_vma=False)
```

```python
import functools

import jax
import jax.numpy as jnp
from jax import lax
from jax.experimental import pallas as pl
from jax.experimental.pallas import tpu as pltpu
from jax.sharding import PartitionSpec as P

B = 128
RB = 1
MESH = pl.DeviceIdType.MESH
NY, NZ, NC = 4, 8, 2


def row_masks(parent, bounds, slot, structure, r):
    count = slot.shape[0]
    ar = jnp.arange(count, dtype=jnp.int32)
    nodes = jnp.arange(parent.shape[0], dtype=jnp.int32)
    logical = jnp.sum(jnp.where(slot[:, None] == ar[None, :], ar[:, None], 0), axis=0)
    node = jnp.sum((logical[:, None] >= bounds[None, 1:7]).astype(jnp.int32), axis=1)
    mine = ar == r
    node_r = jnp.sum(jnp.where(mine, node, 0))
    logical_r = jnp.sum(jnp.where(mine, logical, 0))
    level_r = (node_r >= 4).astype(jnp.int32) + (node_r >= 6).astype(jnp.int32)
    hot = node[:, None] == nodes[None, :]
    par = jnp.sum(jnp.where(hot, parent[None, :], 0), axis=1)
    grand = jnp.sum(jnp.where(par[:, None] == nodes[None, :], parent[None, :], 0), axis=1)
    ancestor = ((par == node_r) | (grand == node_r)) & (node != node_r)
    column = jnp.sum(jnp.where(ar[None, :] == logical_r, structure, 0), axis=1)
    listed = jnp.sum(jnp.where(hot, column[None, :], 0), axis=1) == 1
    return level_r, node == node_r, ancestor & listed


def gather_kernel(*refs, mode, which, section=0, epilogue=None, n_extra=0, n_out=1):
    fused = True
    if mode == "first":
        x_ref, floc_ref, m_ref, sel_ref, out_ref, fout_ref, G, f_ref, acc, local_sem, send_sem, recv_z, recv_y, recv_c, \
            recv_x = refs
    else:
        x_ref, f_ref, m_ref = refs[:3]
        extra_refs = refs[3:3 + n_extra]
        out_refs = refs[3 + n_extra:3 + n_extra + n_out]
        G, acc, local_sem, send_sem, recv_z, recv_y, recv_c = refs[3 + n_extra + n_out:]
    nb, w = x_ref.shape
    r = lax.axis_index("row")
    c = lax.axis_index("col")
    y = r // (NZ * NC)
    z = (r // NC) % NZ
    k = r % NC

    def dev(yy, zz, kk):
        return (((yy + NY) % NY) * NZ + (zz + NZ) % NZ) * NC + kk

    def blk(yy, zz, kk):
        return G.at[((yy + NY) % NY) * NZ + (zz + NZ) % NZ, kk]

    def chunk(kk, yy, lo=0, n=NZ):
        return G.at[pl.ds(((yy + NY) % NY) * NZ + lo, n), kk]

    zr, zl = dev(y, z + 1, k), dev(y, z - 1, k)
    yr, yl = dev(y + 1, z, k), dev(y - 1, z, k)
    partner = dev(y, z, 1 - k)

    barrier = pltpu.get_barrier_semaphore()
    peers = [(d, c) for d in (zr, zl, dev(y, z + 2, k), dev(y, z - 2, k), yr, yl, partner)]
    nx = 4
    xr, xl = (r, (c + 1) % nx), (r, (c + nx - 1) % nx)
    if mode == "first":
        peers += [xr, xl]
    for d in peers:
        pl.semaphore_signal(barrier, inc=1, device_id=d, device_id_type=MESH)
    pl.semaphore_wait(barrier, len(peers))

    local = pltpu.make_async_copy(x_ref, blk(y, z, k), local_sem.at[0])
    local.start()
    acc[...] = jnp.zeros_like(acc)

    if mode == "first":
        wcol = floc_ref.shape[1]
        hcol = wcol // 2

        def fcols(cc, lo=0, n=wcol):
            return f_ref.at[:, pl.ds(pl.multiple_of(((cc + nx) % nx) * wcol + lo, 128), n)]

        def xcopy(src, dst, si, rsem, d):
            return pltpu.make_async_remote_copy(
                src_ref=src, dst_ref=dst, send_sem=send_sem.at[si], recv_sem=rsem,
                device_id=d, device_id_type=MESH,
            )

        flocal = pltpu.make_async_copy(floc_ref, fcols(c), local_sem.at[1])
        flocal.start()
        lo_half, hi_half = floc_ref.at[:, pl.ds(0, hcol)], floc_ref.at[:, pl.ds(hcol, hcol)]
        xsends = [
            xcopy(lo_half, fcols(c, 0, hcol), 64, recv_x.at[0], xr),
            xcopy(hi_half, fcols(c, hcol, hcol), 65, recv_x.at[1], xl),
            xcopy(hi_half, fcols(c, hcol, hcol), 68, recv_x.at[4], xr),
            xcopy(lo_half, fcols(c, 0, hcol), 69, recv_x.at[5], xl),
        ]
        for cp in xsends:
            cp.start()

    sends = []

    def remote(src, dst, rsem, d, si=0):
        return pltpu.make_async_remote_copy(
            src_ref=src, dst_ref=dst, send_sem=send_sem.at[si], recv_sem=rsem,
            device_id=(d, c), device_id_type=MESH,
        )

    def send(src, dst, rsem, d):
        cp = remote(src, dst, rsem, d, len(sends))
        cp.start()
        sends.append(cp)

    def wait(ref, rsem):
        remote(ref, ref, rsem, partner).wait_recv()

    def multiply(yy):
        if fused:
            plane = (yy + NY) % NY
            cols = pl.ds(pl.multiple_of(plane * (NZ * NC * nb), nb), NZ * NC * nb)
            vec = G[pl.ds(plane * NZ, NZ)].reshape(NZ * NC * nb, w)
            acc[...] += jnp.dot(
                f_ref[:, cols] * m_ref[which:which + 1, cols], vec,
                precision=lax.Precision.HIGHEST, preferred_element_type=jnp.float32,
            )

    offs = [0, -1, 1, -2, 2, -3, 3, -4]
    to_right = {0, -1, -2, -3}

    def spread(off):
        i = offs.index(off)
        ref = x_ref if off == 0 else blk(y, z + off, k)
        send(ref, blk(y, z + off, k), recv_y.at[0, i], yr)
        send(ref, blk(y, z + off, k), recv_y.at[1, i], yl)
        send(ref, blk(y, z + off, k), recv_c.at[0, i], partner)

    def recv_of(zsrc):
        return recv_z.at[(zsrc + NZ) % NZ]

    for d in (1, 2, -1, -2):
        send(x_ref, blk(y, z, k), recv_of(z), dev(y, z + d, k))
    spread(0)
    wait(blk(y, z - 2, k), recv_of(z - 2))
    send(blk(y, z - 2, k), blk(y, z - 2, k), recv_of(z - 2), dev(y, z + 1, k))
    send(blk(y, z - 2, k), blk(y, z - 2, k), recv_of(z - 2), dev(y, z + 2, k))
    wait(blk(y, z + 2, k), recv_of(z + 2))
    send(blk(y, z + 2, k), blk(y, z + 2, k), recv_of(z + 2), dev(y, z - 1, k))
    for off in (-1, 1):
        wait(blk(y, z + off, k), recv_of(z + off))
        spread(off)
    spread(-2)
    spread(2)
    for off in (-3, 3, -4):
        wait(blk(y, z + off, k), recv_of(z + off))
        spread(off)
    local.wait()

    for i, off in enumerate(offs):
        wait(blk(y - 1, z + off, k), recv_y.at[0, i])
        if off in to_right:
            send(blk(y - 1, z + off, k), blk(y - 1, z + off, k), recv_y.at[2, i], yr)
        send(blk(y - 1, z + off, k), blk(y - 1, z + off, k), recv_c.at[3, i], partner)
        wait(blk(y + 1, z + off, k), recv_y.at[1, i])
        if off not in to_right:
            send(blk(y + 1, z + off, k), blk(y + 1, z + off, k), recv_y.at[3, i], yl)
        send(blk(y + 1, z + off, k), blk(y + 1, z + off, k), recv_c.at[1, i], partner)

    def partner_plane(d):
        for i, off in enumerate(offs):
            wait(blk(y + d, z + off, 1 - k), recv_c.at[d % NY, i])
        multiply(y + d)

    def partner_wait(d):
        for i, off in enumerate(offs):
            wait(blk(y + d, z + off, 1 - k), recv_c.at[d % NY, i])

    if mode == "first":
        xcopy(lo_half, fcols(c - 1, 0, hcol), 0, recv_x.at[0], xr).wait_recv()
        xsends.append(xcopy(fcols(c - 1, 0, hcol), fcols(c - 1, 0, hcol), 66, recv_x.at[2], xr))
        xsends[-1].start()
        xcopy(hi_half, fcols(c + 1, hcol, hcol), 0, recv_x.at[1], xr).wait_recv()
        xsends.append(xcopy(fcols(c + 1, hcol, hcol), fcols(c + 1, hcol, hcol), 67, recv_x.at[3], xl))
        xsends[-1].start()
    else:
        partner_wait(0)
        multiply(y)
    for i, off in enumerate(offs):
        wait(blk(y + 2, z + off, k), recv_y.at[2 if off in to_right else 3, i])
        send(blk(y + 2, z + off, k), blk(y + 2, z + off, k), recv_c.at[2, i], partner)
    if mode == "first":
        for d in (0, -1, 1, 2):
            partner_wait(d)
        flocal.wait()
        multiply(c)
        xcopy(hi_half, fcols(c - 1, hcol, hcol), 0, recv_x.at[4], xr).wait_recv()
        multiply(c - 1)
        xcopy(lo_half, fcols(c + 1, 0, hcol), 0, recv_x.at[5], xr).wait_recv()
        multiply(c + 1)
        xcopy(fcols(c + 2, 0, hcol), fcols(c + 2, 0, hcol), 0, recv_x.at[2], xr).wait_recv()
        xcopy(fcols(c + 2, hcol, hcol), fcols(c + 2, hcol, hcol), 0, recv_x.at[3], xr).wait_recv()
        multiply(c + 2)
        for cp in xsends:
            cp.wait_send()
        fout = pltpu.make_async_copy(f_ref, fout_ref, local_sem.at[1])
        fout.start()
        fout.wait()
    else:
        for d in (-1, 1, 2):
            partner_wait(d)
            multiply(y + d)

    for cp in sends:
        cp.wait_send()
    if mode == "first":
        out_ref[...] = jnp.where(sel_ref[section:section + 1, :] > 0.5, acc[...], 0.0)
    else:
        for ref, value in zip(out_refs, epilogue(acc[...], *[e[...] for e in extra_refs])):
            ref[...] = value


def _sems():
    return [
        pltpu.SemaphoreType.DMA((2,)),
        pltpu.SemaphoreType.DMA((70,)),
        pltpu.SemaphoreType.DMA((NZ,)),
        pltpu.SemaphoreType.DMA((4, NZ)),
        pltpu.SemaphoreType.DMA((NY, NZ)),
    ]


def _specs(n):
    return [pl.BlockSpec(memory_space=pltpu.VMEM)] * n


def first_product(floc, mask_row, sel, x, cid):
    nb, w = x.shape
    rows = floc.shape[0]
    ncol = floc.shape[1] * 4
    return pl.pallas_call(
        functools.partial(gather_kernel, mode="first", which=0),
        out_shape=(jax.ShapeDtypeStruct((rows, w), jnp.float32), jax.ShapeDtypeStruct((rows, ncol), floc.dtype)),
        in_specs=_specs(4),
        out_specs=(pl.BlockSpec(memory_space=pltpu.VMEM), pl.BlockSpec(memory_space=pl.ANY)),
        scratch_shapes=[pltpu.VMEM((NY * NZ, NC, nb, w), x.dtype), pltpu.VMEM((rows, ncol), floc.dtype),
                        pltpu.VMEM((rows, w), jnp.float32)]
        + _sems() + [pltpu.SemaphoreType.DMA((6,))],
        compiler_params=pltpu.CompilerParams(collective_id=cid, has_side_effects=True),
        cost_estimate=pl.CostEstimate(
            flops=2 * rows * ncol * w, transcendentals=0, bytes_accessed=(2 * rows * ncol + 2 * x.size * 64) * 4,
        ),
    )(x, floc, mask_row, sel)


def gather_product(matrix, mask_row, which, x, cid, extras, epilogue, n_out):
    nb, w = x.shape
    shape = (NY * NZ, NC, nb, w)
    out = jax.ShapeDtypeStruct((matrix.shape[0], w), jnp.float32)
    return pl.pallas_call(
        functools.partial(gather_kernel, mode="fused", which=which, epilogue=epilogue, n_extra=len(extras),
                          n_out=n_out),
        out_shape=tuple([out] * n_out),
        in_specs=_specs(3 + len(extras)),
        out_specs=tuple(pl.BlockSpec(memory_space=pltpu.VMEM) for _ in range(n_out)),
        scratch_shapes=[pltpu.VMEM(shape, x.dtype), pltpu.VMEM((matrix.shape[0], w), jnp.float32)]
        + _sems(),
        compiler_params=pltpu.CompilerParams(collective_id=cid, has_side_effects=True),
        cost_estimate=pl.CostEstimate(
            flops=2 * matrix.shape[0] * matrix.shape[1] * w, transcendentals=0,
            bytes_accessed=(matrix.size + 2 * x.size * 64) * 4,
        ),
    )(x, matrix, mask_row, *extras)


def _link_epilogue(prod, accum, rhs):
    accum = accum + prod
    return accum, rhs - accum


def _first_link_epilogue(prod, rhs):
    accum = jnp.zeros_like(prod) + prod
    return accum, rhs - accum


def _last_epilogue(prod, sel):
    return (jnp.where(sel[2:3, :] > 0.5, prod, 0.0),)


def _diag_epilogue(prod, sel, result, section):
    solved = jnp.where(sel[section:section + 1, :] > 0.5, prod, 0.0)
    return solved, result + solved


def body(factor, rhs, parent, bounds, slot, structure):
    level_mine, same, link = row_masks(parent, bounds, slot, structure, lax.axis_index("row"))
    masks = jnp.repeat(jnp.stack([same, link]).astype(jnp.float32), B, axis=1)
    sels = jnp.repeat((level_mine == jnp.arange(3, dtype=jnp.int32)).astype(jnp.float32)[:, None], rhs.shape[1],
                      axis=1)

    solved, full_rows = first_product(factor, masks, sels, rhs, 0)
    result = solved
    accum, vector = gather_product(full_rows, masks, 1, solved, 1, (rhs,), _first_link_epilogue, 2)
    epi = functools.partial(_diag_epilogue, section=1)
    solved, result = gather_product(full_rows, masks, 0, vector, 2, (sels, result), epi, 2)
    accum, vector = gather_product(full_rows, masks, 1, solved, 3, (accum, rhs), _link_epilogue, 2)
    (solved,) = gather_product(full_rows, masks, 0, vector, 4, (sels,), _last_epilogue, 1)
    return result + solved


def solution(mesh):
    in_specs = (P("row", "col"), P("row", "col"), P(), P(), P(), P())
    out_specs = P("row", "col")
    return jax.shard_map(body, mesh=mesh, in_specs=in_specs, out_specs=out_specs, check_vma=False)
```

```python
import functools

import jax
import jax.numpy as jnp
from jax import lax
from jax.experimental import pallas as pl
from jax.experimental.pallas import tpu as pltpu
from jax.sharding import PartitionSpec as P

B = 128
RB = 1
MESH = pl.DeviceIdType.MESH
NY, NZ, NC = 4, 8, 2


def row_masks(parent, bounds, slot, structure, r):
    count = slot.shape[0]
    ar = jnp.arange(count, dtype=jnp.int32)
    nodes = jnp.arange(parent.shape[0], dtype=jnp.int32)
    logical = jnp.sum(jnp.where(slot[:, None] == ar[None, :], ar[:, None], 0), axis=0)
    node = jnp.sum((logical[:, None] >= bounds[None, 1:7]).astype(jnp.int32), axis=1)
    mine = ar == r
    node_r = jnp.sum(jnp.where(mine, node, 0))
    logical_r = jnp.sum(jnp.where(mine, logical, 0))
    level_r = (node_r >= 4).astype(jnp.int32) + (node_r >= 6).astype(jnp.int32)
    hot = node[:, None] == nodes[None, :]
    par = jnp.sum(jnp.where(hot, parent[None, :], 0), axis=1)
    grand = jnp.sum(jnp.where(par[:, None] == nodes[None, :], parent[None, :], 0), axis=1)
    ancestor = ((par == node_r) | (grand == node_r)) & (node != node_r)
    column = jnp.sum(jnp.where(ar[None, :] == logical_r, structure, 0), axis=1)
    listed = jnp.sum(jnp.where(hot, column[None, :], 0), axis=1) == 1
    return level_r, node == node_r, ancestor & listed


def gather_kernel(*refs, mode, which, section=0, epilogue=None, n_extra=0, n_out=1):
    fused = True
    if mode == "first":
        x_ref, floc_ref, m_ref, sel_ref, out_ref, fout_ref, G, f_ref, acc, local_sem, send_sem, recv_z, recv_y, recv_c, \
            recv_x = refs
    else:
        x_ref, f_ref, m_ref = refs[:3]
        extra_refs = refs[3:3 + n_extra]
        out_refs = refs[3 + n_extra:3 + n_extra + n_out]
        G, acc, local_sem, send_sem, recv_z, recv_y, recv_c = refs[3 + n_extra + n_out:]
    nb, w = x_ref.shape
    r = lax.axis_index("row")
    c = lax.axis_index("col")
    y = r // (NZ * NC)
    z = (r // NC) % NZ
    k = r % NC

    def dev(yy, zz, kk):
        return (((yy + NY) % NY) * NZ + (zz + NZ) % NZ) * NC + kk

    def blk(yy, zz, kk):
        return G.at[((yy + NY) % NY) * NZ + (zz + NZ) % NZ, kk]

    def chunk(kk, yy, lo=0, n=NZ):
        return G.at[pl.ds(((yy + NY) % NY) * NZ + lo, n), kk]

    zr, zl = dev(y, z + 1, k), dev(y, z - 1, k)
    yr, yl = dev(y + 1, z, k), dev(y - 1, z, k)
    partner = dev(y, z, 1 - k)

    barrier = pltpu.get_barrier_semaphore()
    peers = [(d, c) for d in (zr, zl, dev(y, z + 2, k), dev(y, z - 2, k), yr, yl, partner)]
    nx = 4
    xr, xl = (r, (c + 1) % nx), (r, (c + nx - 1) % nx)
    if mode == "first":
        peers += [xr, xl]
    for d in peers:
        pl.semaphore_signal(barrier, inc=1, device_id=d, device_id_type=MESH)
    pl.semaphore_wait(barrier, len(peers))

    local = pltpu.make_async_copy(x_ref, blk(y, z, k), local_sem.at[0])
    local.start()
    acc[...] = jnp.zeros_like(acc)

    if mode == "first":
        wcol = floc_ref.shape[1]
        hcol = wcol // 2

        def fcols(cc, lo=0, n=wcol):
            return f_ref.at[:, pl.ds(pl.multiple_of(((cc + nx) % nx) * wcol + lo, 128), n)]

        def xcopy(src, dst, si, rsem, d):
            return pltpu.make_async_remote_copy(
                src_ref=src, dst_ref=dst, send_sem=send_sem.at[si], recv_sem=rsem,
                device_id=d, device_id_type=MESH,
            )

        flocal = pltpu.make_async_copy(floc_ref, fcols(c), local_sem.at[1])
        flocal.start()
        xsends = [xcopy(floc_ref, fcols(c), 64, recv_x.at[0], xr), xcopy(floc_ref, fcols(c), 65, recv_x.at[1], xl)]
        for cp in xsends:
            cp.start()

    sends = []

    def remote(src, dst, rsem, d, si=0):
        return pltpu.make_async_remote_copy(
            src_ref=src, dst_ref=dst, send_sem=send_sem.at[si], recv_sem=rsem,
            device_id=(d, c), device_id_type=MESH,
        )

    def send(src, dst, rsem, d):
        cp = remote(src, dst, rsem, d, len(sends))
        cp.start()
        sends.append(cp)

    def wait(ref, rsem):
        remote(ref, ref, rsem, partner).wait_recv()

    def multiply(yy):
        if fused:
            plane = (yy + NY) % NY
            cols = pl.ds(pl.multiple_of(plane * (NZ * NC * nb), nb), NZ * NC * nb)
            vec = G[pl.ds(plane * NZ, NZ)].reshape(NZ * NC * nb, w)
            acc[...] += jnp.dot(
                f_ref[:, cols] * m_ref[which:which + 1, cols], vec,
                precision=lax.Precision.HIGHEST, preferred_element_type=jnp.float32,
            )

    offs = [0, -1, 1, -2, 2, -3, 3, -4]
    to_right = {0, -1, -2, -3}

    def spread(off):
        i = offs.index(off)
        ref = x_ref if off == 0 else blk(y, z + off, k)
        send(ref, blk(y, z + off, k), recv_y.at[0, i], yr)
        send(ref, blk(y, z + off, k), recv_y.at[1, i], yl)
        send(ref, blk(y, z + off, k), recv_c.at[0, i], partner)

    def recv_of(zsrc):
        return recv_z.at[(zsrc + NZ) % NZ]

    for d in (1, 2, -1, -2):
        send(x_ref, blk(y, z, k), recv_of(z), dev(y, z + d, k))
    spread(0)
    wait(blk(y, z - 2, k), recv_of(z - 2))
    send(blk(y, z - 2, k), blk(y, z - 2, k), recv_of(z - 2), dev(y, z + 1, k))
    send(blk(y, z - 2, k), blk(y, z - 2, k), recv_of(z - 2), dev(y, z + 2, k))
    wait(blk(y, z + 2, k), recv_of(z + 2))
    send(blk(y, z + 2, k), blk(y, z + 2, k), recv_of(z + 2), dev(y, z - 1, k))
    for off in (-1, 1):
        wait(blk(y, z + off, k), recv_of(z + off))
        spread(off)
    spread(-2)
    spread(2)
    for off in (-3, 3, -4):
        wait(blk(y, z + off, k), recv_of(z + off))
        spread(off)
    local.wait()

    for i, off in enumerate(offs):
        wait(blk(y - 1, z + off, k), recv_y.at[0, i])
        if off in to_right:
            send(blk(y - 1, z + off, k), blk(y - 1, z + off, k), recv_y.at[2, i], yr)
        send(blk(y - 1, z + off, k), blk(y - 1, z + off, k), recv_c.at[3, i], partner)
        wait(blk(y + 1, z + off, k), recv_y.at[1, i])
        if off not in to_right:
            send(blk(y + 1, z + off, k), blk(y + 1, z + off, k), recv_y.at[3, i], yl)
        send(blk(y + 1, z + off, k), blk(y + 1, z + off, k), recv_c.at[1, i], partner)

    def partner_plane(d):
        for i, off in enumerate(offs):
            wait(blk(y + d, z + off, 1 - k), recv_c.at[d % NY, i])
        multiply(y + d)

    def partner_wait(d):
        for i, off in enumerate(offs):
            wait(blk(y + d, z + off, 1 - k), recv_c.at[d % NY, i])

    if mode == "first":
        xcopy(floc_ref, fcols(c - 1), 0, recv_x.at[0], xr).wait_recv()
        xsends.append(xcopy(fcols(c - 1, 0, hcol), fcols(c - 1, 0, hcol), 66, recv_x.at[2], xr))
        xsends[-1].start()
        xcopy(floc_ref, fcols(c + 1), 0, recv_x.at[1], xr).wait_recv()
        xsends.append(xcopy(fcols(c + 1, hcol, hcol), fcols(c + 1, hcol, hcol), 67, recv_x.at[3], xl))
        xsends[-1].start()
    for i, off in enumerate(offs):
        wait(blk(y + 2, z + off, k), recv_y.at[2 if off in to_right else 3, i])
        send(blk(y + 2, z + off, k), blk(y + 2, z + off, k), recv_c.at[2, i], partner)
    if mode == "first":
        for d in (0, -1, 1, 2):
            partner_wait(d)
        flocal.wait()
        multiply(c)
        multiply(c - 1)
        multiply(c + 1)
        xcopy(fcols(c + 2, 0, hcol), fcols(c + 2, 0, hcol), 0, recv_x.at[2], xr).wait_recv()
        xcopy(fcols(c + 2, hcol, hcol), fcols(c + 2, hcol, hcol), 0, recv_x.at[3], xr).wait_recv()
        multiply(c + 2)
        for cp in xsends:
            cp.wait_send()
        fout = pltpu.make_async_copy(f_ref, fout_ref, local_sem.at[1])
        fout.start()
        fout.wait()
    else:
        for d in (0, -1, 1, 2):
            partner_wait(d)
            multiply(y + d)

    for cp in sends:
        cp.wait_send()
    if mode == "first":
        out_ref[...] = jnp.where(sel_ref[section:section + 1, :] > 0.5, acc[...], 0.0)
    else:
        for ref, value in zip(out_refs, epilogue(acc[...], *[e[...] for e in extra_refs])):
            ref[...] = value


def _sems():
    return [
        pltpu.SemaphoreType.DMA((2,)),
        pltpu.SemaphoreType.DMA((68,)),
        pltpu.SemaphoreType.DMA((NZ,)),
        pltpu.SemaphoreType.DMA((4, NZ)),
        pltpu.SemaphoreType.DMA((NY, NZ)),
    ]


def _specs(n):
    return [pl.BlockSpec(memory_space=pltpu.VMEM)] * n


def first_product(floc, mask_row, sel, x, cid):
    nb, w = x.shape
    rows = floc.shape[0]
    ncol = floc.shape[1] * 4
    return pl.pallas_call(
        functools.partial(gather_kernel, mode="first", which=0),
        out_shape=(jax.ShapeDtypeStruct((rows, w), jnp.float32), jax.ShapeDtypeStruct((rows, ncol), floc.dtype)),
        in_specs=_specs(4),
        out_specs=(pl.BlockSpec(memory_space=pltpu.VMEM), pl.BlockSpec(memory_space=pl.ANY)),
        scratch_shapes=[pltpu.VMEM((NY * NZ, NC, nb, w), x.dtype), pltpu.VMEM((rows, ncol), floc.dtype),
                        pltpu.VMEM((rows, w), jnp.float32)]
        + _sems() + [pltpu.SemaphoreType.DMA((4,))],
        compiler_params=pltpu.CompilerParams(collective_id=cid, has_side_effects=True),
        cost_estimate=pl.CostEstimate(
            flops=2 * rows * ncol * w, transcendentals=0, bytes_accessed=(2 * rows * ncol + 2 * x.size * 64) * 4,
        ),
    )(x, floc, mask_row, sel)


def gather_product(matrix, mask_row, which, x, cid, extras, epilogue, n_out):
    nb, w = x.shape
    shape = (NY * NZ, NC, nb, w)
    out = jax.ShapeDtypeStruct((matrix.shape[0], w), jnp.float32)
    return pl.pallas_call(
        functools.partial(gather_kernel, mode="fused", which=which, epilogue=epilogue, n_extra=len(extras),
                          n_out=n_out),
        out_shape=tuple([out] * n_out),
        in_specs=_specs(3 + len(extras)),
        out_specs=tuple(pl.BlockSpec(memory_space=pltpu.VMEM) for _ in range(n_out)),
        scratch_shapes=[pltpu.VMEM(shape, x.dtype), pltpu.VMEM((matrix.shape[0], w), jnp.float32)]
        + _sems(),
        compiler_params=pltpu.CompilerParams(collective_id=cid, has_side_effects=True),
        cost_estimate=pl.CostEstimate(
            flops=2 * matrix.shape[0] * matrix.shape[1] * w, transcendentals=0,
            bytes_accessed=(matrix.size + 2 * x.size * 64) * 4,
        ),
    )(x, matrix, mask_row, *extras)


def _link_epilogue(prod, accum, rhs):
    accum = accum + prod
    return accum, rhs - accum


def _first_link_epilogue(prod, rhs):
    accum = jnp.zeros_like(prod) + prod
    return accum, rhs - accum


def _last_epilogue(prod, sel):
    return (jnp.where(sel[2:3, :] > 0.5, prod, 0.0),)


def _diag_epilogue(prod, sel, result, section):
    solved = jnp.where(sel[section:section + 1, :] > 0.5, prod, 0.0)
    return solved, result + solved


def body(factor, rhs, parent, bounds, slot, structure):
    level_mine, same, link = row_masks(parent, bounds, slot, structure, lax.axis_index("row"))
    masks = jnp.repeat(jnp.stack([same, link]).astype(jnp.float32), B, axis=1)
    sels = jnp.repeat((level_mine == jnp.arange(3, dtype=jnp.int32)).astype(jnp.float32)[:, None], rhs.shape[1],
                      axis=1)

    solved, full_rows = first_product(factor, masks, sels, rhs, 0)
    result = solved
    accum, vector = gather_product(full_rows, masks, 1, solved, 1, (rhs,), _first_link_epilogue, 2)
    epi = functools.partial(_diag_epilogue, section=1)
    solved, result = gather_product(full_rows, masks, 0, vector, 2, (sels, result), epi, 2)
    accum, vector = gather_product(full_rows, masks, 1, solved, 3, (accum, rhs), _link_epilogue, 2)
    (solved,) = gather_product(full_rows, masks, 0, vector, 4, (sels,), _last_epilogue, 1)
    return result + solved


def solution(mesh):
    in_specs = (P("row", "col"), P("row", "col"), P(), P(), P(), P())
    out_specs = P("row", "col")
    return jax.shard_map(body, mesh=mesh, in_specs=in_specs, out_specs=out_specs, check_vma=False)
```

```python
import functools

import jax
import jax.numpy as jnp
from jax import lax
from jax.experimental import pallas as pl
from jax.experimental.pallas import tpu as pltpu
from jax.sharding import PartitionSpec as P

B = 128
RB = 1
MESH = pl.DeviceIdType.MESH
NY, NZ, NC = 4, 8, 2


def row_masks(parent, bounds, slot, structure, r):
    count = slot.shape[0]
    ar = jnp.arange(count, dtype=jnp.int32)
    nodes = jnp.arange(parent.shape[0], dtype=jnp.int32)
    logical = jnp.sum(jnp.where(slot[:, None] == ar[None, :], ar[:, None], 0), axis=0)
    node = jnp.sum((logical[:, None] >= bounds[None, 1:7]).astype(jnp.int32), axis=1)
    mine = ar == r
    node_r = jnp.sum(jnp.where(mine, node, 0))
    logical_r = jnp.sum(jnp.where(mine, logical, 0))
    level_r = (node_r >= 4).astype(jnp.int32) + (node_r >= 6).astype(jnp.int32)
    hot = node[:, None] == nodes[None, :]
    par = jnp.sum(jnp.where(hot, parent[None, :], 0), axis=1)
    grand = jnp.sum(jnp.where(par[:, None] == nodes[None, :], parent[None, :], 0), axis=1)
    ancestor = ((par == node_r) | (grand == node_r)) & (node != node_r)
    column = jnp.sum(jnp.where(ar[None, :] == logical_r, structure, 0), axis=1)
    listed = jnp.sum(jnp.where(hot, column[None, :], 0), axis=1) == 1
    return level_r, node == node_r, ancestor & listed


def gather_kernel(*refs, mode, which, section=0, epilogue=None, n_extra=0, n_out=1):
    fused = True
    if mode == "first":
        x_ref, floc_ref, m_ref, sel_ref, out_ref, fout_ref, G, f_ref, acc, local_sem, send_sem, recv_z, recv_y, recv_c, \
            recv_x = refs
    else:
        x_ref, f_ref, m_ref = refs[:3]
        extra_refs = refs[3:3 + n_extra]
        out_refs = refs[3 + n_extra:3 + n_extra + n_out]
        G, acc, local_sem, send_sem, recv_z, recv_y, recv_c = refs[3 + n_extra + n_out:]
    nb, w = x_ref.shape
    r = lax.axis_index("row")
    c = lax.axis_index("col")
    y = r // (NZ * NC)
    z = (r // NC) % NZ
    k = r % NC

    def dev(yy, zz, kk):
        return (((yy + NY) % NY) * NZ + (zz + NZ) % NZ) * NC + kk

    def blk(yy, zz, kk):
        return G.at[((yy + NY) % NY) * NZ + (zz + NZ) % NZ, kk]

    def chunk(kk, yy, lo=0, n=NZ):
        return G.at[pl.ds(((yy + NY) % NY) * NZ + lo, n), kk]

    zr, zl = dev(y, z + 1, k), dev(y, z - 1, k)
    yr, yl = dev(y + 1, z, k), dev(y - 1, z, k)
    partner = dev(y, z, 1 - k)

    barrier = pltpu.get_barrier_semaphore()
    peers = [(d, c) for d in (zr, zl, dev(y, z + 2, k), dev(y, z - 2, k), yr, yl, partner)]
    nx = 4
    xr, xl = (r, (c + 1) % nx), (r, (c + nx - 1) % nx)
    if mode == "first":
        peers += [xr, xl]
    for d in peers:
        pl.semaphore_signal(barrier, inc=1, device_id=d, device_id_type=MESH)
    pl.semaphore_wait(barrier, len(peers))

    local = pltpu.make_async_copy(x_ref, blk(y, z, k), local_sem.at[0])
    local.start()
    acc[...] = jnp.zeros_like(acc)

    if mode == "first":
        wcol = floc_ref.shape[1]
        hcol = wcol // 2

        def fcols(cc, lo=0, n=wcol):
            return f_ref.at[:, pl.ds(pl.multiple_of(((cc + nx) % nx) * wcol + lo, 128), n)]

        def xcopy(src, dst, si, rsem, d):
            return pltpu.make_async_remote_copy(
                src_ref=src, dst_ref=dst, send_sem=send_sem.at[si], recv_sem=rsem,
                device_id=d, device_id_type=MESH,
            )

        flocal = pltpu.make_async_copy(floc_ref, fcols(c), local_sem.at[1])
        flocal.start()
        xsends = [xcopy(floc_ref, fcols(c), 64, recv_x.at[0], xr), xcopy(floc_ref, fcols(c), 65, recv_x.at[1], xl)]
        for cp in xsends:
            cp.start()

    sends = []

    def remote(src, dst, rsem, d, si=0):
        return pltpu.make_async_remote_copy(
            src_ref=src, dst_ref=dst, send_sem=send_sem.at[si], recv_sem=rsem,
            device_id=(d, c), device_id_type=MESH,
        )

    def send(src, dst, rsem, d):
        cp = remote(src, dst, rsem, d, len(sends))
        cp.start()
        sends.append(cp)

    def wait(ref, rsem):
        remote(ref, ref, rsem, partner).wait_recv()

    def multiply(yy):
        if fused:
            plane = (yy + NY) % NY
            cols = pl.ds(pl.multiple_of(plane * (NZ * NC * nb), nb), NZ * NC * nb)
            vec = G[pl.ds(plane * NZ, NZ)].reshape(NZ * NC * nb, w)
            acc[...] += jnp.dot(
                f_ref[:, cols] * m_ref[which:which + 1, cols], vec,
                precision=lax.Precision.HIGHEST, preferred_element_type=jnp.float32,
            )

    offs = [0, -1, 1, -2, 2, -3, 3, -4]
    to_right = {0, -1, -2, -3}

    def spread(off):
        i = offs.index(off)
        ref = x_ref if off == 0 else blk(y, z + off, k)
        send(ref, blk(y, z + off, k), recv_y.at[0, i], yr)
        send(ref, blk(y, z + off, k), recv_y.at[1, i], yl)
        send(ref, blk(y, z + off, k), recv_c.at[0, i], partner)

    def recv_of(zsrc):
        return recv_z.at[(zsrc + NZ) % NZ]

    for d in (1, 2, -1, -2):
        send(x_ref, blk(y, z, k), recv_of(z), dev(y, z + d, k))
    spread(0)
    wait(blk(y, z - 2, k), recv_of(z - 2))
    send(blk(y, z - 2, k), blk(y, z - 2, k), recv_of(z - 2), dev(y, z + 1, k))
    send(blk(y, z - 2, k), blk(y, z - 2, k), recv_of(z - 2), dev(y, z + 2, k))
    wait(blk(y, z + 2, k), recv_of(z + 2))
    send(blk(y, z + 2, k), blk(y, z + 2, k), recv_of(z + 2), dev(y, z - 1, k))
    for off in (-1, 1):
        wait(blk(y, z + off, k), recv_of(z + off))
        spread(off)
    spread(-2)
    spread(2)
    for off in (-3, 3, -4):
        wait(blk(y, z + off, k), recv_of(z + off))
        spread(off)
    local.wait()
    if mode != "first":
        for i, off in enumerate(offs):
            wait(blk(y, z + off, 1 - k), recv_c.at[0, i])
        multiply(y)

    for i, off in enumerate(offs):
        wait(blk(y - 1, z + off, k), recv_y.at[0, i])
        if off in to_right:
            send(blk(y - 1, z + off, k), blk(y - 1, z + off, k), recv_y.at[2, i], yr)
        send(blk(y - 1, z + off, k), blk(y - 1, z + off, k), recv_c.at[3, i], partner)
        wait(blk(y + 1, z + off, k), recv_y.at[1, i])
        if off not in to_right:
            send(blk(y + 1, z + off, k), blk(y + 1, z + off, k), recv_y.at[3, i], yl)
        send(blk(y + 1, z + off, k), blk(y + 1, z + off, k), recv_c.at[1, i], partner)

    def partner_plane(d):
        for i, off in enumerate(offs):
            wait(blk(y + d, z + off, 1 - k), recv_c.at[d % NY, i])
        multiply(y + d)

    def partner_wait(d):
        for i, off in enumerate(offs):
            wait(blk(y + d, z + off, 1 - k), recv_c.at[d % NY, i])

    if mode == "first":
        xcopy(floc_ref, fcols(c - 1), 0, recv_x.at[0], xr).wait_recv()
        xsends.append(xcopy(fcols(c - 1, 0, hcol), fcols(c - 1, 0, hcol), 66, recv_x.at[2], xr))
        xsends[-1].start()
        xcopy(floc_ref, fcols(c + 1), 0, recv_x.at[1], xr).wait_recv()
        xsends.append(xcopy(fcols(c + 1, hcol, hcol), fcols(c + 1, hcol, hcol), 67, recv_x.at[3], xl))
        xsends[-1].start()
    for i, off in enumerate(offs):
        wait(blk(y + 2, z + off, k), recv_y.at[2 if off in to_right else 3, i])
        send(blk(y + 2, z + off, k), blk(y + 2, z + off, k), recv_c.at[2, i], partner)
    if mode == "first":
        for d in (0, -1, 1, 2):
            partner_wait(d)
        flocal.wait()
        multiply(c)
        multiply(c - 1)
        multiply(c + 1)
        xcopy(fcols(c + 2, 0, hcol), fcols(c + 2, 0, hcol), 0, recv_x.at[2], xr).wait_recv()
        xcopy(fcols(c + 2, hcol, hcol), fcols(c + 2, hcol, hcol), 0, recv_x.at[3], xr).wait_recv()
        multiply(c + 2)
        for cp in xsends:
            cp.wait_send()
        fout = pltpu.make_async_copy(f_ref, fout_ref, local_sem.at[1])
        fout.start()
        fout.wait()
    else:
        for d in (-1, 1, 2):
            partner_wait(d)
            multiply(y + d)

    for cp in sends:
        cp.wait_send()
    if mode == "first":
        out_ref[...] = jnp.where(sel_ref[section:section + 1, :] > 0.5, acc[...], 0.0)
    else:
        for ref, value in zip(out_refs, epilogue(acc[...], *[e[...] for e in extra_refs])):
            ref[...] = value


def _sems():
    return [
        pltpu.SemaphoreType.DMA((2,)),
        pltpu.SemaphoreType.DMA((68,)),
        pltpu.SemaphoreType.DMA((NZ,)),
        pltpu.SemaphoreType.DMA((4, NZ)),
        pltpu.SemaphoreType.DMA((NY, NZ)),
    ]


def _specs(n):
    return [pl.BlockSpec(memory_space=pltpu.VMEM)] * n


def first_product(floc, mask_row, sel, x, cid):
    nb, w = x.shape
    rows = floc.shape[0]
    ncol = floc.shape[1] * 4
    return pl.pallas_call(
        functools.partial(gather_kernel, mode="first", which=0),
        out_shape=(jax.ShapeDtypeStruct((rows, w), jnp.float32), jax.ShapeDtypeStruct((rows, ncol), floc.dtype)),
        in_specs=_specs(4),
        out_specs=(pl.BlockSpec(memory_space=pltpu.VMEM), pl.BlockSpec(memory_space=pl.ANY)),
        scratch_shapes=[pltpu.VMEM((NY * NZ, NC, nb, w), x.dtype), pltpu.VMEM((rows, ncol), floc.dtype),
                        pltpu.VMEM((rows, w), jnp.float32)]
        + _sems() + [pltpu.SemaphoreType.DMA((4,))],
        compiler_params=pltpu.CompilerParams(collective_id=cid, has_side_effects=True),
        cost_estimate=pl.CostEstimate(
            flops=2 * rows * ncol * w, transcendentals=0, bytes_accessed=(2 * rows * ncol + 2 * x.size * 64) * 4,
        ),
    )(x, floc, mask_row, sel)


def gather_product(matrix, mask_row, which, x, cid, extras, epilogue, n_out):
    nb, w = x.shape
    shape = (NY * NZ, NC, nb, w)
    out = jax.ShapeDtypeStruct((matrix.shape[0], w), jnp.float32)
    return pl.pallas_call(
        functools.partial(gather_kernel, mode="fused", which=which, epilogue=epilogue, n_extra=len(extras),
                          n_out=n_out),
        out_shape=tuple([out] * n_out),
        in_specs=_specs(3 + len(extras)),
        out_specs=tuple(pl.BlockSpec(memory_space=pltpu.VMEM) for _ in range(n_out)),
        scratch_shapes=[pltpu.VMEM(shape, x.dtype), pltpu.VMEM((matrix.shape[0], w), jnp.float32)]
        + _sems(),
        compiler_params=pltpu.CompilerParams(collective_id=cid, has_side_effects=True),
        cost_estimate=pl.CostEstimate(
            flops=2 * matrix.shape[0] * matrix.shape[1] * w, transcendentals=0,
            bytes_accessed=(matrix.size + 2 * x.size * 64) * 4,
        ),
    )(x, matrix, mask_row, *extras)


def _link_epilogue(prod, accum, rhs):
    accum = accum + prod
    return accum, rhs - accum


def _first_link_epilogue(prod, rhs):
    accum = jnp.zeros_like(prod) + prod
    return accum, rhs - accum


def _last_epilogue(prod, sel):
    return (jnp.where(sel[2:3, :] > 0.5, prod, 0.0),)


def _diag_epilogue(prod, sel, result, section):
    solved = jnp.where(sel[section:section + 1, :] > 0.5, prod, 0.0)
    return solved, result + solved


def body(factor, rhs, parent, bounds, slot, structure):
    level_mine, same, link = row_masks(parent, bounds, slot, structure, lax.axis_index("row"))
    masks = jnp.repeat(jnp.stack([same, link]).astype(jnp.float32), B, axis=1)
    sels = jnp.repeat((level_mine == jnp.arange(3, dtype=jnp.int32)).astype(jnp.float32)[:, None], rhs.shape[1],
                      axis=1)

    solved, full_rows = first_product(factor, masks, sels, rhs, 0)
    result = solved
    accum, vector = gather_product(full_rows, masks, 1, solved, 1, (rhs,), _first_link_epilogue, 2)
    epi = functools.partial(_diag_epilogue, section=1)
    solved, result = gather_product(full_rows, masks, 0, vector, 2, (sels, result), epi, 2)
    accum, vector = gather_product(full_rows, masks, 1, solved, 3, (accum, rhs), _link_epilogue, 2)
    (solved,) = gather_product(full_rows, masks, 0, vector, 4, (sels,), _last_epilogue, 1)
    return result + solved


def solution(mesh):
    in_specs = (P("row", "col"), P("row", "col"), P(), P(), P(), P())
    out_specs = P("row", "col")
    return jax.shard_map(body, mesh=mesh, in_specs=in_specs, out_specs=out_specs, check_vma=False)
```

```python
import functools

import jax
import jax.numpy as jnp
from jax import lax
from jax.experimental import pallas as pl
from jax.experimental.pallas import tpu as pltpu
from jax.sharding import PartitionSpec as P

B = 128
RB = 1
MESH = pl.DeviceIdType.MESH
NY, NZ, NC = 4, 8, 2


def row_masks(parent, bounds, slot, structure, r):
    count = slot.shape[0]
    ar = jnp.arange(count, dtype=jnp.int32)
    nodes = jnp.arange(parent.shape[0], dtype=jnp.int32)
    logical = jnp.sum(jnp.where(slot[:, None] == ar[None, :], ar[:, None], 0), axis=0)
    node = jnp.sum((logical[:, None] >= bounds[None, 1:7]).astype(jnp.int32), axis=1)
    mine = ar == r
    node_r = jnp.sum(jnp.where(mine, node, 0))
    logical_r = jnp.sum(jnp.where(mine, logical, 0))
    level_r = (node_r >= 4).astype(jnp.int32) + (node_r >= 6).astype(jnp.int32)
    hot = node[:, None] == nodes[None, :]
    par = jnp.sum(jnp.where(hot, parent[None, :], 0), axis=1)
    grand = jnp.sum(jnp.where(par[:, None] == nodes[None, :], parent[None, :], 0), axis=1)
    ancestor = ((par == node_r) | (grand == node_r)) & (node != node_r)
    column = jnp.sum(jnp.where(ar[None, :] == logical_r, structure, 0), axis=1)
    listed = jnp.sum(jnp.where(hot, column[None, :], 0), axis=1) == 1
    return level_r, node == node_r, ancestor & listed


def gather_kernel(*refs, mode, which, section=0, epilogue=None, n_extra=0, n_out=1):
    fused = True
    if mode == "first":
        x_ref, floc_ref, m_ref, sel_ref, out_ref, fout_ref, G, f_ref, acc, local_sem, send_sem, recv_z, recv_y, recv_c, \
            recv_x = refs
    else:
        x_ref, f_ref, m_ref = refs[:3]
        extra_refs = refs[3:3 + n_extra]
        out_refs = refs[3 + n_extra:3 + n_extra + n_out]
        G, acc, local_sem, send_sem, recv_z, recv_y, recv_c = refs[3 + n_extra + n_out:]
    nb, w = x_ref.shape
    r = lax.axis_index("row")
    c = lax.axis_index("col")
    y = r // (NZ * NC)
    z = (r // NC) % NZ
    k = r % NC

    def dev(yy, zz, kk):
        return (((yy + NY) % NY) * NZ + (zz + NZ) % NZ) * NC + kk

    def blk(yy, zz, kk):
        return G.at[((yy + NY) % NY) * NZ + (zz + NZ) % NZ, kk]

    def chunk(kk, yy, lo=0, n=NZ):
        return G.at[pl.ds(((yy + NY) % NY) * NZ + lo, n), kk]

    zr, zl = dev(y, z + 1, k), dev(y, z - 1, k)
    yr, yl = dev(y + 1, z, k), dev(y - 1, z, k)
    partner = dev(y, z, 1 - k)

    barrier = pltpu.get_barrier_semaphore()
    peers = [(d, c) for d in (zr, zl, dev(y, z + 2, k), dev(y, z - 2, k), yr, yl, partner)]
    nx = 4
    xr, xl = (r, (c + 1) % nx), (r, (c + nx - 1) % nx)
    if mode == "first":
        peers += [xr, xl]
    for d in peers:
        pl.semaphore_signal(barrier, inc=1, device_id=d, device_id_type=MESH)
    pl.semaphore_wait(barrier, len(peers))

    local = pltpu.make_async_copy(x_ref, blk(y, z, k), local_sem.at[0])
    local.start()
    acc[...] = jnp.zeros_like(acc)

    if mode == "first":
        wcol = floc_ref.shape[1]
        hcol = wcol // 2

        def fcols(cc, lo=0, n=wcol):
            return f_ref.at[:, pl.ds(pl.multiple_of(((cc + nx) % nx) * wcol + lo, 128), n)]

        def xcopy(src, dst, si, rsem, d):
            return pltpu.make_async_remote_copy(
                src_ref=src, dst_ref=dst, send_sem=send_sem.at[si], recv_sem=rsem,
                device_id=d, device_id_type=MESH,
            )

        flocal = pltpu.make_async_copy(floc_ref, fcols(c), local_sem.at[1])
        flocal.start()
        xsends = [xcopy(floc_ref, fcols(c), 64, recv_x.at[0], xr), xcopy(floc_ref, fcols(c), 65, recv_x.at[1], xl)]
        for cp in xsends:
            cp.start()

    sends = []

    def remote(src, dst, rsem, d, si=0):
        return pltpu.make_async_remote_copy(
            src_ref=src, dst_ref=dst, send_sem=send_sem.at[si], recv_sem=rsem,
            device_id=(d, c), device_id_type=MESH,
        )

    def send(src, dst, rsem, d):
        cp = remote(src, dst, rsem, d, len(sends))
        cp.start()
        sends.append(cp)

    def wait(ref, rsem):
        remote(ref, ref, rsem, partner).wait_recv()

    def multiply(yy):
        if fused:
            plane = (yy + NY) % NY
            cols = pl.ds(pl.multiple_of(plane * (NZ * NC * nb), nb), NZ * NC * nb)
            vec = G[pl.ds(plane * NZ, NZ)].reshape(NZ * NC * nb, w)
            acc[...] += jnp.dot(
                f_ref[:, cols] * m_ref[which:which + 1, cols], vec,
                precision=lax.Precision.HIGHEST, preferred_element_type=jnp.float32,
            )

    offs = [0, -1, 1, -2, 2, -3, 3, -4]
    to_right = {0, -1, -2, -3}

    def spread(off):
        i = offs.index(off)
        ref = x_ref if off == 0 else blk(y, z + off, k)
        send(ref, blk(y, z + off, k), recv_y.at[0, i], yr)
        send(ref, blk(y, z + off, k), recv_y.at[1, i], yl)
        send(ref, blk(y, z + off, k), recv_c.at[0, i], partner)

    def recv_of(zsrc):
        return recv_z.at[(zsrc + NZ) % NZ]

    for d in (1, 2, -1, -2):
        send(x_ref, blk(y, z, k), recv_of(z), dev(y, z + d, k))
    spread(0)
    wait(blk(y, z - 2, k), recv_of(z - 2))
    send(blk(y, z - 2, k), blk(y, z - 2, k), recv_of(z - 2), dev(y, z + 1, k))
    send(blk(y, z - 2, k), blk(y, z - 2, k), recv_of(z - 2), dev(y, z + 2, k))
    wait(blk(y, z + 2, k), recv_of(z + 2))
    send(blk(y, z + 2, k), blk(y, z + 2, k), recv_of(z + 2), dev(y, z - 1, k))
    for off in (-1, 1):
        wait(blk(y, z + off, k), recv_of(z + off))
        spread(off)
    spread(-2)
    spread(2)
    for off in (-3, 3, -4):
        wait(blk(y, z + off, k), recv_of(z + off))
        spread(off)
    local.wait()
    if mode != "first":
        for i, off in enumerate(offs):
            wait(blk(y, z + off, 1 - k), recv_c.at[0, i])
        multiply(y)

    for i, off in enumerate(offs):
        wait(blk(y - 1, z + off, k), recv_y.at[0, i])
        if off in to_right:
            send(blk(y - 1, z + off, k), blk(y - 1, z + off, k), recv_y.at[2, i], yr)
        send(blk(y - 1, z + off, k), blk(y - 1, z + off, k), recv_c.at[3, i], partner)
        wait(blk(y + 1, z + off, k), recv_y.at[1, i])
        if off not in to_right:
            send(blk(y + 1, z + off, k), blk(y + 1, z + off, k), recv_y.at[3, i], yl)
        send(blk(y + 1, z + off, k), blk(y + 1, z + off, k), recv_c.at[1, i], partner)

    def partner_plane(d):
        for i, off in enumerate(offs):
            wait(blk(y + d, z + off, 1 - k), recv_c.at[d % NY, i])
        multiply(y + d)

    def partner_wait(d):
        for i, off in enumerate(offs):
            wait(blk(y + d, z + off, 1 - k), recv_c.at[d % NY, i])

    if mode == "first":
        xcopy(floc_ref, fcols(c - 1), 0, recv_x.at[0], xr).wait_recv()
        xsends.append(xcopy(fcols(c - 1, 0, hcol), fcols(c - 1, 0, hcol), 66, recv_x.at[2], xr))
        xsends[-1].start()
        xcopy(floc_ref, fcols(c + 1), 0, recv_x.at[1], xr).wait_recv()
        xsends.append(xcopy(fcols(c + 1, hcol, hcol), fcols(c + 1, hcol, hcol), 67, recv_x.at[3], xl))
        xsends[-1].start()
    if mode != "first":
        for d in (-1, 1):
            partner_wait(d)
            multiply(y + d)
    for i, off in enumerate(offs):
        wait(blk(y + 2, z + off, k), recv_y.at[2 if off in to_right else 3, i])
        send(blk(y + 2, z + off, k), blk(y + 2, z + off, k), recv_c.at[2, i], partner)
    if mode == "first":
        for d in (0, -1, 1, 2):
            partner_wait(d)
        flocal.wait()
        multiply(c)
        multiply(c - 1)
        multiply(c + 1)
        xcopy(fcols(c + 2, 0, hcol), fcols(c + 2, 0, hcol), 0, recv_x.at[2], xr).wait_recv()
        xcopy(fcols(c + 2, hcol, hcol), fcols(c + 2, hcol, hcol), 0, recv_x.at[3], xr).wait_recv()
        multiply(c + 2)
        for cp in xsends:
            cp.wait_send()
        fout = pltpu.make_async_copy(f_ref, fout_ref, local_sem.at[1])
        fout.start()
        fout.wait()
    else:
        partner_wait(2)
        multiply(y + 2)

    for cp in sends:
        cp.wait_send()
    if mode == "first":
        out_ref[...] = jnp.where(sel_ref[section:section + 1, :] > 0.5, acc[...], 0.0)
    else:
        for ref, value in zip(out_refs, epilogue(acc[...], *[e[...] for e in extra_refs])):
            ref[...] = value


def _sems():
    return [
        pltpu.SemaphoreType.DMA((2,)),
        pltpu.SemaphoreType.DMA((68,)),
        pltpu.SemaphoreType.DMA((NZ,)),
        pltpu.SemaphoreType.DMA((4, NZ)),
        pltpu.SemaphoreType.DMA((NY, NZ)),
    ]


def _specs(n):
    return [pl.BlockSpec(memory_space=pltpu.VMEM)] * n


def first_product(floc, mask_row, sel, x, cid):
    nb, w = x.shape
    rows = floc.shape[0]
    ncol = floc.shape[1] * 4
    return pl.pallas_call(
        functools.partial(gather_kernel, mode="first", which=0),
        out_shape=(jax.ShapeDtypeStruct((rows, w), jnp.float32), jax.ShapeDtypeStruct((rows, ncol), floc.dtype)),
        in_specs=_specs(4),
        out_specs=(pl.BlockSpec(memory_space=pltpu.VMEM), pl.BlockSpec(memory_space=pl.ANY)),
        scratch_shapes=[pltpu.VMEM((NY * NZ, NC, nb, w), x.dtype), pltpu.VMEM((rows, ncol), floc.dtype),
                        pltpu.VMEM((rows, w), jnp.float32)]
        + _sems() + [pltpu.SemaphoreType.DMA((4,))],
        compiler_params=pltpu.CompilerParams(collective_id=cid, has_side_effects=True),
        cost_estimate=pl.CostEstimate(
            flops=2 * rows * ncol * w, transcendentals=0, bytes_accessed=(2 * rows * ncol + 2 * x.size * 64) * 4,
        ),
    )(x, floc, mask_row, sel)


def gather_product(matrix, mask_row, which, x, cid, extras, epilogue, n_out):
    nb, w = x.shape
    shape = (NY * NZ, NC, nb, w)
    out = jax.ShapeDtypeStruct((matrix.shape[0], w), jnp.float32)
    return pl.pallas_call(
        functools.partial(gather_kernel, mode="fused", which=which, epilogue=epilogue, n_extra=len(extras),
                          n_out=n_out),
        out_shape=tuple([out] * n_out),
        in_specs=_specs(3 + len(extras)),
        out_specs=tuple(pl.BlockSpec(memory_space=pltpu.VMEM) for _ in range(n_out)),
        scratch_shapes=[pltpu.VMEM(shape, x.dtype), pltpu.VMEM((matrix.shape[0], w), jnp.float32)]
        + _sems(),
        compiler_params=pltpu.CompilerParams(collective_id=cid, has_side_effects=True),
        cost_estimate=pl.CostEstimate(
            flops=2 * matrix.shape[0] * matrix.shape[1] * w, transcendentals=0,
            bytes_accessed=(matrix.size + 2 * x.size * 64) * 4,
        ),
    )(x, matrix, mask_row, *extras)


def _link_epilogue(prod, accum, rhs):
    accum = accum + prod
    return accum, rhs - accum


def _first_link_epilogue(prod, rhs):
    accum = jnp.zeros_like(prod) + prod
    return accum, rhs - accum


def _last_epilogue(prod, sel):
    return (jnp.where(sel[2:3, :] > 0.5, prod, 0.0),)


def _diag_epilogue(prod, sel, result, section):
    solved = jnp.where(sel[section:section + 1, :] > 0.5, prod, 0.0)
    return solved, result + solved


def body(factor, rhs, parent, bounds, slot, structure):
    level_mine, same, link = row_masks(parent, bounds, slot, structure, lax.axis_index("row"))
    masks = jnp.repeat(jnp.stack([same, link]).astype(jnp.float32), B, axis=1)
    sels = jnp.repeat((level_mine == jnp.arange(3, dtype=jnp.int32)).astype(jnp.float32)[:, None], rhs.shape[1],
                      axis=1)

    solved, full_rows = first_product(factor, masks, sels, rhs, 0)
    result = solved
    accum, vector = gather_product(full_rows, masks, 1, solved, 1, (rhs,), _first_link_epilogue, 2)
    epi = functools.partial(_diag_epilogue, section=1)
    solved, result = gather_product(full_rows, masks, 0, vector, 2, (sels, result), epi, 2)
    accum, vector = gather_product(full_rows, masks, 1, solved, 3, (accum, rhs), _link_epilogue, 2)
    (solved,) = gather_product(full_rows, masks, 0, vector, 4, (sels,), _last_epilogue, 1)
    return result + solved


def solution(mesh):
    in_specs = (P("row", "col"), P("row", "col"), P(), P(), P(), P())
    out_specs = P("row", "col")
    return jax.shard_map(body, mesh=mesh, in_specs=in_specs, out_specs=out_specs, check_vma=False)
```

```python
import functools

import jax
import jax.numpy as jnp
from jax import lax
from jax.experimental import pallas as pl
from jax.experimental.pallas import tpu as pltpu
from jax.sharding import PartitionSpec as P

B = 128
RB = 1
MESH = pl.DeviceIdType.MESH
NY, NZ, NC = 4, 8, 2


def row_masks(parent, bounds, slot, structure, r):
    count = slot.shape[0]
    ar = jnp.arange(count, dtype=jnp.int32)
    nodes = jnp.arange(parent.shape[0], dtype=jnp.int32)
    logical = jnp.sum(jnp.where(slot[:, None] == ar[None, :], ar[:, None], 0), axis=0)
    node = jnp.sum((logical[:, None] >= bounds[None, 1:7]).astype(jnp.int32), axis=1)
    mine = ar == r
    node_r = jnp.sum(jnp.where(mine, node, 0))
    logical_r = jnp.sum(jnp.where(mine, logical, 0))
    level_r = (node_r >= 4).astype(jnp.int32) + (node_r >= 6).astype(jnp.int32)
    hot = node[:, None] == nodes[None, :]
    par = jnp.sum(jnp.where(hot, parent[None, :], 0), axis=1)
    grand = jnp.sum(jnp.where(par[:, None] == nodes[None, :], parent[None, :], 0), axis=1)
    ancestor = ((par == node_r) | (grand == node_r)) & (node != node_r)
    column = jnp.sum(jnp.where(ar[None, :] == logical_r, structure, 0), axis=1)
    listed = jnp.sum(jnp.where(hot, column[None, :], 0), axis=1) == 1
    return level_r, node == node_r, ancestor & listed


def gather_kernel(*refs, mode, which, section=0, epilogue=None, n_extra=0, n_out=1):
    fused = True
    if mode == "first":
        x_ref, floc_ref, m_ref, sel_ref, out_ref, fout_ref, G, f_ref, acc, local_sem, send_sem, recv_z, recv_y, recv_c, \
            recv_x = refs
    else:
        x_ref, f_ref, m_ref = refs[:3]
        extra_refs = refs[3:3 + n_extra]
        out_refs = refs[3 + n_extra:3 + n_extra + n_out]
        G, acc, local_sem, send_sem, recv_z, recv_y, recv_c = refs[3 + n_extra + n_out:]
    nb, w = x_ref.shape
    r = lax.axis_index("row")
    c = lax.axis_index("col")
    y = r // (NZ * NC)
    z = (r // NC) % NZ
    k = r % NC

    def dev(yy, zz, kk):
        return (((yy + NY) % NY) * NZ + (zz + NZ) % NZ) * NC + kk

    def blk(yy, zz, kk):
        return G.at[((yy + NY) % NY) * NZ + (zz + NZ) % NZ, kk]

    def chunk(kk, yy, lo=0, n=NZ):
        return G.at[pl.ds(((yy + NY) % NY) * NZ + lo, n), kk]

    zr, zl = dev(y, z + 1, k), dev(y, z - 1, k)
    yr, yl = dev(y + 1, z, k), dev(y - 1, z, k)
    partner = dev(y, z, 1 - k)

    barrier = pltpu.get_barrier_semaphore()
    peers = [(d, c) for d in (zr, zl, yr, yl, partner)]
    nx = 4
    xr, xl = (r, (c + 1) % nx), (r, (c + nx - 1) % nx)
    if mode == "first":
        peers += [xr, xl]
    for d in peers:
        pl.semaphore_signal(barrier, inc=1, device_id=d, device_id_type=MESH)
    pl.semaphore_wait(barrier, len(peers))

    local = pltpu.make_async_copy(x_ref, blk(y, z, k), local_sem.at[0])
    local.start()
    acc[...] = jnp.zeros_like(acc)

    if mode == "first":
        wcol = floc_ref.shape[1]
        hcol = wcol // 2

        def fcols(cc, lo=0, n=wcol):
            return f_ref.at[:, pl.ds(pl.multiple_of(((cc + nx) % nx) * wcol + lo, 128), n)]

        def xcopy(src, dst, si, rsem, d):
            return pltpu.make_async_remote_copy(
                src_ref=src, dst_ref=dst, send_sem=send_sem.at[si], recv_sem=rsem,
                device_id=d, device_id_type=MESH,
            )

        flocal = pltpu.make_async_copy(floc_ref, fcols(c), local_sem.at[1])
        flocal.start()
        xsends = [xcopy(floc_ref, fcols(c), 64, recv_x.at[0], xr), xcopy(floc_ref, fcols(c), 65, recv_x.at[1], xl)]
        for cp in xsends:
            cp.start()

    sends = []

    def remote(src, dst, rsem, d, si=0):
        return pltpu.make_async_remote_copy(
            src_ref=src, dst_ref=dst, send_sem=send_sem.at[si], recv_sem=rsem,
            device_id=(d, c), device_id_type=MESH,
        )

    def send(src, dst, rsem, d):
        cp = remote(src, dst, rsem, d, len(sends))
        cp.start()
        sends.append(cp)

    def wait(ref, rsem):
        remote(ref, ref, rsem, partner).wait_recv()

    def multiply(yy):
        if fused:
            plane = (yy + NY) % NY
            cols = pl.ds(pl.multiple_of(plane * (NZ * NC * nb), nb), NZ * NC * nb)
            vec = G[pl.ds(plane * NZ, NZ)].reshape(NZ * NC * nb, w)
            acc[...] += jnp.dot(
                f_ref[:, cols] * m_ref[which:which + 1, cols], vec,
                precision=lax.Precision.HIGHEST, preferred_element_type=jnp.float32,
            )

    offs = [0, -1, 1, -2, 2, -3, 3, -4]
    to_right = {0, -1, -2, -3}

    def spread(off):
        i = offs.index(off)
        ref = x_ref if off == 0 else blk(y, z + off, k)
        send(ref, blk(y, z + off, k), recv_y.at[0, i], yr)
        send(ref, blk(y, z + off, k), recv_y.at[1, i], yl)
        send(ref, blk(y, z + off, k), recv_c.at[0, i], partner)

    def recv_of(zsrc):
        return recv_z.at[(zsrc + NZ) % NZ]

    for s in range(4):
        if s >= 1:
            wait(blk(y, z - s, k), recv_of(z - s))
        send(x_ref if s == 0 else blk(y, z - s, k), blk(y, z - s, k), recv_of(z - s), zr)
        if s < 3:
            if s >= 1:
                wait(blk(y, z + s, k), recv_of(z + s))
            send(x_ref if s == 0 else blk(y, z + s, k), blk(y, z + s, k), recv_of(z + s), zl)
        if s == 0:
            spread(0)
        else:
            spread(-s)
            if s < 3:
                spread(s)
    wait(blk(y, z - 4, k), recv_of(z - 4))
    spread(-4)
    wait(blk(y, z + 3, k), recv_of(z + 3))
    spread(3)
    local.wait()
    if mode != "first":
        for i, off in enumerate(offs):
            wait(blk(y, z + off, 1 - k), recv_c.at[0, i])
        multiply(y)

    for i, off in enumerate(offs):
        wait(blk(y - 1, z + off, k), recv_y.at[0, i])
        if off in to_right:
            send(blk(y - 1, z + off, k), blk(y - 1, z + off, k), recv_y.at[2, i], yr)
        send(blk(y - 1, z + off, k), blk(y - 1, z + off, k), recv_c.at[3, i], partner)
        wait(blk(y + 1, z + off, k), recv_y.at[1, i])
        if off not in to_right:
            send(blk(y + 1, z + off, k), blk(y + 1, z + off, k), recv_y.at[3, i], yl)
        send(blk(y + 1, z + off, k), blk(y + 1, z + off, k), recv_c.at[1, i], partner)

    def partner_plane(d):
        for i, off in enumerate(offs):
            wait(blk(y + d, z + off, 1 - k), recv_c.at[d % NY, i])
        multiply(y + d)

    def partner_wait(d):
        for i, off in enumerate(offs):
            wait(blk(y + d, z + off, 1 - k), recv_c.at[d % NY, i])

    if mode == "first":
        xcopy(floc_ref, fcols(c - 1), 0, recv_x.at[0], xr).wait_recv()
        xsends.append(xcopy(fcols(c - 1, 0, hcol), fcols(c - 1, 0, hcol), 66, recv_x.at[2], xr))
        xsends[-1].start()
        xcopy(floc_ref, fcols(c + 1), 0, recv_x.at[1], xr).wait_recv()
        xsends.append(xcopy(fcols(c + 1, hcol, hcol), fcols(c + 1, hcol, hcol), 67, recv_x.at[3], xl))
        xsends[-1].start()
    for i, off in enumerate(offs):
        wait(blk(y + 2, z + off, k), recv_y.at[2 if off in to_right else 3, i])
        send(blk(y + 2, z + off, k), blk(y + 2, z + off, k), recv_c.at[2, i], partner)
    if mode == "first":
        for d in (0, -1, 1, 2):
            partner_wait(d)
        flocal.wait()
        multiply(c)
        multiply(c - 1)
        multiply(c + 1)
        xcopy(fcols(c + 2, 0, hcol), fcols(c + 2, 0, hcol), 0, recv_x.at[2], xr).wait_recv()
        xcopy(fcols(c + 2, hcol, hcol), fcols(c + 2, hcol, hcol), 0, recv_x.at[3], xr).wait_recv()
        multiply(c + 2)
        for cp in xsends:
            cp.wait_send()
        fout = pltpu.make_async_copy(f_ref, fout_ref, local_sem.at[1])
        fout.start()
        fout.wait()
    else:
        for d in (-1, 1, 2):
            partner_wait(d)
            multiply(y + d)

    for cp in sends:
        cp.wait_send()
    if mode == "first":
        out_ref[...] = jnp.where(sel_ref[section:section + 1, :] > 0.5, acc[...], 0.0)
    else:
        for ref, value in zip(out_refs, epilogue(acc[...], *[e[...] for e in extra_refs])):
            ref[...] = value


def _sems():
    return [
        pltpu.SemaphoreType.DMA((2,)),
        pltpu.SemaphoreType.DMA((68,)),
        pltpu.SemaphoreType.DMA((NZ,)),
        pltpu.SemaphoreType.DMA((4, NZ)),
        pltpu.SemaphoreType.DMA((NY, NZ)),
    ]


def _specs(n):
    return [pl.BlockSpec(memory_space=pltpu.VMEM)] * n


def first_product(floc, mask_row, sel, x, cid):
    nb, w = x.shape
    rows = floc.shape[0]
    ncol = floc.shape[1] * 4
    return pl.pallas_call(
        functools.partial(gather_kernel, mode="first", which=0),
        out_shape=(jax.ShapeDtypeStruct((rows, w), jnp.float32), jax.ShapeDtypeStruct((rows, ncol), floc.dtype)),
        in_specs=_specs(4),
        out_specs=(pl.BlockSpec(memory_space=pltpu.VMEM), pl.BlockSpec(memory_space=pl.ANY)),
        scratch_shapes=[pltpu.VMEM((NY * NZ, NC, nb, w), x.dtype), pltpu.VMEM((rows, ncol), floc.dtype),
                        pltpu.VMEM((rows, w), jnp.float32)]
        + _sems() + [pltpu.SemaphoreType.DMA((4,))],
        compiler_params=pltpu.CompilerParams(collective_id=cid, has_side_effects=True),
        cost_estimate=pl.CostEstimate(
            flops=2 * rows * ncol * w, transcendentals=0, bytes_accessed=(2 * rows * ncol + 2 * x.size * 64) * 4,
        ),
    )(x, floc, mask_row, sel)


def gather_product(matrix, mask_row, which, x, cid, extras, epilogue, n_out):
    nb, w = x.shape
    shape = (NY * NZ, NC, nb, w)
    out = jax.ShapeDtypeStruct((matrix.shape[0], w), jnp.float32)
    return pl.pallas_call(
        functools.partial(gather_kernel, mode="fused", which=which, epilogue=epilogue, n_extra=len(extras),
                          n_out=n_out),
        out_shape=tuple([out] * n_out),
        in_specs=_specs(3 + len(extras)),
        out_specs=tuple(pl.BlockSpec(memory_space=pltpu.VMEM) for _ in range(n_out)),
        scratch_shapes=[pltpu.VMEM(shape, x.dtype), pltpu.VMEM((matrix.shape[0], w), jnp.float32)]
        + _sems(),
        compiler_params=pltpu.CompilerParams(collective_id=cid, has_side_effects=True),
        cost_estimate=pl.CostEstimate(
            flops=2 * matrix.shape[0] * matrix.shape[1] * w, transcendentals=0,
            bytes_accessed=(matrix.size + 2 * x.size * 64) * 4,
        ),
    )(x, matrix, mask_row, *extras)


def _link_epilogue(prod, accum, rhs):
    accum = accum + prod
    return accum, rhs - accum


def _first_link_epilogue(prod, rhs):
    accum = jnp.zeros_like(prod) + prod
    return accum, rhs - accum


def _last_epilogue(prod, sel):
    return (jnp.where(sel[2:3, :] > 0.5, prod, 0.0),)


def _diag_epilogue(prod, sel, result, section):
    solved = jnp.where(sel[section:section + 1, :] > 0.5, prod, 0.0)
    return solved, result + solved


def body(factor, rhs, parent, bounds, slot, structure):
    level_mine, same, link = row_masks(parent, bounds, slot, structure, lax.axis_index("row"))
    masks = jnp.repeat(jnp.stack([same, link]).astype(jnp.float32), B, axis=1)
    sels = jnp.repeat((level_mine == jnp.arange(3, dtype=jnp.int32)).astype(jnp.float32)[:, None], rhs.shape[1],
                      axis=1)

    solved, full_rows = first_product(factor, masks, sels, rhs, 0)
    result = solved
    accum, vector = gather_product(full_rows, masks, 1, solved, 1, (rhs,), _first_link_epilogue, 2)
    epi = functools.partial(_diag_epilogue, section=1)
    solved, result = gather_product(full_rows, masks, 0, vector, 2, (sels, result), epi, 2)
    accum, vector = gather_product(full_rows, masks, 1, solved, 3, (accum, rhs), _link_epilogue, 2)
    (solved,) = gather_product(full_rows, masks, 0, vector, 4, (sels,), _last_epilogue, 1)
    return result + solved


def solution(mesh):
    in_specs = (P("row", "col"), P("row", "col"), P(), P(), P(), P())
    out_specs = P("row", "col")
    return jax.shard_map(body, mesh=mesh, in_specs=in_specs, out_specs=out_specs, check_vma=False)
```
